32 devices in a mesh: replica: 2 (over x), shard: 4 (over z), seq: 4 (over y, core).
Axes of the slice: x: 2, y: 2, z: 4, core: 2. Of those that a mesh axis runs over, the one named last changes fastest.
Arguments:
- tokens: bfloat16 [16, 1024, 768], P(('replica', 'shard'), 'seq'), may hold values from -6 to 6
- teacher: bfloat16 [16, 1024, 768], P(('replica', 'shard'), 'seq'), may hold values from -6 to 6
- seg_ids: int32 [16, 1024], P(('replica', 'shard'), 'seq'), may hold values from 0 to 7, never falling along the last dimension, each value on 1 to 512 neighbouring positions
- parent_seg: int32 [16, 8], P(('replica', 'shard')), may hold values from 0 to 6, as said below
- valid: int32 [16, 1024], P(('replica', 'shard'), 'seq'), may hold values from 0 to 1, as said below
- query_weight: bfloat16 [768, 768], P('shard'), may hold values from -0.21875 to 0.21875
- query_bias: bfloat16 [768], P('shard'), may hold values from -1.5 to 1.5
- key_weight: bfloat16 [768, 768], P('shard'), may hold values from -0.21875 to 0.21875
- value_weight: bfloat16 [768, 768], P('shard'), may hold values from -0.21875 to 0.21875
- value_bias: bfloat16 [768], P('shard'), may hold values from -1.5 to 1.5
- mix_weight: bfloat16 [768, 768], P('shard'), may hold values from -3.5 to 3.5
- mix_bias: bfloat16 [768], P('shard'), may hold values from -1.5 to 1.5
- first_gain: bfloat16 [768], P('shard'), may hold values from 0.5 to 1.5
- first_shift: bfloat16 [768], P('shard'), may hold values from -1.5 to 1.5
- inner_weight: bfloat16 [768, 3072], P('shard'), may hold values from -0.21875 to 0.21875
- inner_bias: bfloat16 [3072], P('shard'), may hold values from -1.5 to 1.5
- outer_weight: bfloat16 [3072, 768], P('shard'), may hold values from -0.109375 to 0.109375
- outer_bias: bfloat16 [768], P('shard'), may hold values from -1.5 to 1.5
- second_gain: bfloat16 [768], P('shard'), may hold values from 0.5 to 1.5
- second_shift: bfloat16 [768], P('shard'), may hold values from -1.5 to 1.5
Outputs:
- layer_out: bfloat16 [16, 1024, 768], P(('replica', 'shard'), 'seq')
- loss_value: float32 [], replicated
- input_grad: float32 [16, 1024, 768], P(('replica', 'shard'), 'seq')
- dquery_weight: float32 [768, 768], P('shard')
- dquery_bias: float32 [768], P('shard')
- dkey_weight: float32 [768, 768], P('shard')
- dvalue_weight: float32 [768, 768], P('shard')
- dvalue_bias: float32 [768], P('shard')
- dmix_weight: float32 [768, 768], P('shard')
- dmix_bias: float32 [768], P('shard')
- dfirst_gain: float32 [768], P('shard')
- dfirst_shift: float32 [768], P('shard')
- dinner_weight: float32 [768, 3072], P('shard')
- dinner_bias: float32 [3072], P('shard')
- douter_weight: float32 [3072, 768], P('shard')
- douter_bias: float32 [768], P('shard')
- dsecond_gain: float32 [768], P('shard')
- dsecond_shift: float32 [768], P('shard')
The draws below stay inside these ranges and needn't reach their ends.
Inputs may be any that keep to these rules, and one draw needn't show every extreme that they name: `seg_ids`: in each tree the segment numbers never fall along the tokens, every one of the 8 segments has 1 to 512 tokens and one has exactly 512. parent_seg[t, 0] = 0 and parent_seg[t, s] < s for s >= 1, so segment 0 is an ancestor of every segment. valid[t, 0] = 1 in every tree.
All inputs are finite; a program needn't handle non-finite values.
Results may differ from the reference program's by a relative error of at most 0.014.
Values may be sent and summed in bfloat16 or wider, within the bound.
A program may use at most 192 MiB of HBM per device.

```python
import math
import jax
import jax.numpy as jnp
import numpy as np
from jax import lax

D = 768
HEADS = 12
HD = 64
FF = 3072
LEN = 1024
NSEG = 8
MOST = 512
TREES = 16
TOKENS = 16384


def draw_parent_seg(key, part):
    upper = jnp.maximum(jnp.arange(NSEG, dtype=jnp.int32), 1)
    return jax.random.randint(key, (TREES, NSEG), 0, upper[None, :], dtype=jnp.int32)


def draw_valid(key, part):
    level = jax.random.randint(key, (TREES, LEN), 0, 100, dtype=jnp.int32)
    place = jnp.arange(TREES, dtype=jnp.int32)[:, None]
    limit = 30 + 65 * place // max(TREES - 1, 1)
    keep = (level < limit).astype(jnp.int32)
    first = (jnp.arange(LEN, dtype=jnp.int32) == 0).astype(jnp.int32)[None, :]
    return jnp.maximum(keep, first)


def steps_of(key, dims, shards, low, high):
    def one(dim, blocks):
        heights = jax.random.uniform(jax.random.fold_in(jax.random.fold_in(key, 6), dim), (blocks,), jnp.float32, low / len(shards), high / len(shards))
        return jnp.repeat(jnp.exp(heights), dims[dim] // blocks).reshape((-1,) + (1,) * (len(dims) - dim - 1))

    loudness = one(*shards[0])
    for cut in shards[1:]:
        loudness = loudness * one(*cut)
    return loudness


def profile(number_of, total, reach, lean):
    portions = [(1 << 20) // math.isqrt(standing ** lean) + 1 for standing in range(2, number_of + 1)]
    surplus, holding = total - reach - (number_of - 1), [1] * (number_of - 1)
    while surplus > 0:
        free = [i for i in range(number_of - 1) if holding[i] < reach]
        mass, left = sum([portions[i] for i in free]), surplus
        for i in free:
            more = min(reach - holding[i], max(1, left * portions[i] // mass), surplus)
            holding[i] = holding[i] + more
            surplus = surplus - more
    return np.array([reach] + holding)


def ragged_sizes(rng, number_of, total, most, skew):
    if number_of == 2:
        one = jax.random.randint(rng, (), max(1, total - most), min(most, total - 1) + 1)
        return jnp.stack([one, total - one])
    tallies = jnp.asarray(profile(number_of, total, most, skew), jnp.int32)
    twos = (number_of - 1) // 2
    source_of, taker = tallies[1:1 + 2 * twos:2], tallies[2:2 + 2 * twos:2]
    margin = jnp.minimum(source_of - 1, most - taker)
    shifted = jax.random.randint(jax.random.fold_in(rng, 1), (twos,), 0, 1 << 20) % (margin + 1)
    tallies = tallies.at[1:1 + 2 * twos:2].set(source_of - shifted).at[2:2 + 2 * twos:2].set(taker + shifted)
    return tallies[jax.random.permutation(jax.random.fold_in(rng, 2), number_of)]


def centred(stream_key, extent, width, reach, shards=(), kind=jnp.bfloat16):
    level = steps_of(stream_key, extent, shards, -0.22, 0.18) if shards else 1.0
    values = jax.random.normal(stream_key, extent, jnp.float32) * width * level
    return jnp.minimum(jnp.maximum(values, -reach), reach).astype(kind)


def setup_inputs(seed: int = 0) -> dict:
    keys = jax.random.split(jax.random.key(seed), 21)
    return {
        "tokens": centred(keys[0], (TREES, LEN, D), 1.0, 6.0, ((0, 8), (1, 4))),
        "teacher": centred(keys[1], (TREES, LEN, D), 1.0, 6.0, ((0, 8), (1, 4))),
        "seg_ids": jax.vmap(lambda own: jnp.searchsorted(jnp.cumsum(ragged_sizes(own, NSEG, LEN, MOST, 0)), jnp.arange(LEN), side="right"))(jax.random.split(keys[2], TREES)).reshape((TREES, LEN)).astype(jnp.int32),
        "parent_seg": draw_parent_seg(jax.random.fold_in(keys[20], 71), 0),
        "valid": draw_valid(jax.random.fold_in(keys[20], 71), 0),
        "query_weight": centred(keys[5], (D, D), D ** -0.5, 0.21875, ((0, 4),)),
        "query_bias": centred(keys[6], (D,), 0.3, 1.5, ((0, 4),)),
        "key_weight": centred(keys[7], (D, D), D ** -0.5, 0.21875, ((0, 4),)),
        "value_weight": centred(keys[8], (D, D), D ** -0.5, 0.21875, ((0, 4),)),
        "value_bias": centred(keys[9], (D,), 0.3, 1.5, ((0, 4),)),
        "mix_weight": centred(keys[10], (D, D), (max(D // 256, 1)) ** -0.5, 3.5, ((0, 4),)),
        "mix_bias": centred(keys[11], (D,), 0.3, 1.5, ((0, 4),)),
        "first_gain": jnp.clip(1.0 + 0.1 * jax.random.normal(keys[12], (D,), jnp.float32), 0.5, 1.5).astype(jnp.bfloat16),
        "first_shift": centred(keys[13], (D,), 0.3, 1.5, ((0, 4),)),
        "inner_weight": centred(keys[14], (D, FF), D ** -0.5, 0.21875, ((0, 4),)),
        "inner_bias": centred(keys[15], (FF,), 0.3, 1.5, ((0, 4),)),
        "outer_weight": centred(keys[16], (FF, D), FF ** -0.5, 0.109375, ((0, 4),)),
        "outer_bias": centred(keys[17], (D,), 0.3, 1.5, ((0, 4),)),
        "second_gain": jnp.clip(1.0 + 0.1 * jax.random.normal(keys[18], (D,), jnp.float32), 0.5, 1.5).astype(jnp.bfloat16),
        "second_shift": centred(keys[19], (D,), 0.3, 1.5, ((0, 4),)),
    }


norm_eps = 1e-12
highest = lax.Precision.HIGHEST

@jax.custom_vjp
def low(v):
    return lax.optimization_barrier(v.astype(jnp.bfloat16)).astype(jnp.float32)

@jax.custom_vjp
def low_back(v):
    return v

def low_keep(v):
    return (low(v), None)

def low_pass(kept, grad):
    return (grad,)

def back_keep(v):
    return (v, None)

def back_low(kept, grad):
    return (low(grad),)
low.defvjp(low_keep, low_pass)
low_back.defvjp(back_keep, back_low)

def layer_norm(resid, gain, shift):
    center = resid - lax.optimization_barrier(jnp.mean(resid, axis=-1, keepdims=True))
    spread = lax.optimization_barrier(jnp.mean(center * center, axis=-1, keepdims=True))
    return center * lax.rsqrt(spread + norm_eps) * gain + shift

def one_hot_segs(segments):
    return (segments[..., None] == jnp.arange(NSEG, dtype=jnp.int32)).astype(jnp.float32)

def ancestors(parent_seg):
    choose = one_hot_segs(parent_seg)
    current = jnp.broadcast_to(jnp.eye(NSEG, dtype=jnp.float32), choose.shape)
    table = current
    for level in range(NSEG - 1):
        current = jnp.einsum('gsa,gab->gsb', current, choose, precision=highest)
        table = jnp.maximum(table, current)
    return table

def group_forward(params, inputs, segments, valid, parent_seg, teacher):
    query_weight, query_bias, key_weight, value_weight, value_bias, mix_weight, mix_bias, first_gain, first_shift, inner_weight, inner_bias, outer_weight, outer_bias, second_gain, second_shift = params
    group = inputs.shape[0]
    table = ancestors(parent_seg)
    query_side = jnp.einsum('gqs,gsk->gqk', one_hot_segs(segments), table, precision=highest)
    key_side = one_hot_segs(segments) * valid[..., None].astype(jnp.float32)
    allowed = jnp.einsum('gqs,gks->gqk', query_side, key_side, precision=highest) > 0.5
    flat = inputs.reshape(group * LEN, D)
    query = low_back(low(jnp.dot(flat, query_weight, precision=highest) + query_bias))
    key = low_back(low(jnp.dot(flat, key_weight, precision=highest)))
    value = low_back(low(jnp.dot(flat, value_weight, precision=highest) + value_bias))
    query = query.reshape(group, LEN, HEADS, HD)
    key = key.reshape(group, LEN, HEADS, HD)
    value = value.reshape(group, LEN, HEADS, HD)
    scores = jnp.einsum('gqhd,gkhd->ghqk', query, key, precision=highest) * 0.125
    scores = low_back(scores)
    masked = jnp.where(allowed[:, None], scores, -1e+30)
    probs = low(jax.nn.softmax(masked, axis=-1))
    attended = jnp.einsum('ghqk,gkhd->gqhd', probs, value, precision=highest)
    attended = low_back(low(attended.reshape(group * LEN, D)))
    branch = low_back(jnp.dot(attended, mix_weight, precision=highest) + mix_bias)
    first = layer_norm(flat + branch, first_gain, first_shift)
    hidden_pre = low_back(jnp.dot(low(first), inner_weight, precision=highest) + inner_bias)
    hidden = low(jax.nn.gelu(hidden_pre, approximate=False))
    ffn = low_back(jnp.dot(hidden, outer_weight, precision=highest) + outer_bias)
    output = layer_norm(first + ffn, second_gain, second_shift)
    error = output - teacher.reshape(group * LEN, D)
    weight_rows = valid.reshape(group * LEN, 1).astype(jnp.float32)
    part = jnp.sum(weight_rows * error * error)
    return (output.reshape(group, LEN, D), part)

def reference(tokens, teacher, seg_ids, parent_seg, valid, query_weight, query_bias, key_weight, value_weight, value_bias, mix_weight, mix_bias, first_gain, first_shift, inner_weight, inner_bias, outer_weight, outer_bias, second_gain, second_shift):
    params = tuple((item.astype(jnp.float32) for item in (query_weight, query_bias, key_weight, value_weight, value_bias, mix_weight, mix_bias, first_gain, first_shift, inner_weight, inner_bias, outer_weight, outer_bias, second_gain, second_shift)))
    inputs = tokens.astype(jnp.float32)
    count = jnp.sum(valid.astype(jnp.float32))
    scale = TOKENS / count
    groups = TREES // 4
    checked = jax.checkpoint(group_forward)
    items = (seg_ids.reshape(groups, 4, LEN), valid.reshape(groups, 4, LEN), parent_seg.reshape(groups, 4, NSEG), teacher.astype(jnp.float32).reshape(groups, 4, LEN, D))

    def objective(params, inputs):

        def step(carry, group_items):
            block, segments, valid_rows, parents, targets = group_items
            output, part = checked(params, block, segments, valid_rows, parents, targets)
            return (carry + part, output)
        loss_sum, outputs = lax.scan(step, jnp.zeros((), jnp.float32), (inputs.reshape(groups, 4, LEN, D),) + items)
        return ((outputs, loss_sum * scale), loss_sum)
    (outputs, scaled), pullback, loss_sum = jax.vjp(objective, params, inputs, has_aux=True)
    param_grads, input_grad = pullback((jnp.zeros_like(outputs), jnp.ones_like(scaled)))
    layer_out = outputs.reshape(TREES, LEN, D).astype(jnp.bfloat16)
    return (layer_out, loss_sum / count, input_grad.reshape(TREES, LEN, D), param_grads[0], param_grads[1], param_grads[2], param_grads[3], param_grads[4], param_grads[5], param_grads[6], param_grads[7], param_grads[8], param_grads[9], param_grads[10], param_grads[11], param_grads[12], param_grads[13], param_grads[14])
```

```python
import functools

import jax
import jax.numpy as jnp
from jax import lax
from jax.experimental import pallas as pl
from jax.experimental.pallas import tpu as pltpu
from jax.sharding import PartitionSpec as P

HEADS = 12
HD = 64
NSEG = 8
MESH = pl.DeviceIdType.MESH
BIG = 1e30
norm_eps = 1e-12
f32 = jnp.float32
bf16 = jnp.bfloat16
VMEM_LIMIT = 60 * 1024 * 1024


class Place:
    def __init__(self, nz):
        self.nz = nz
        self.x = lax.axis_index("replica")
        self.z = lax.axis_index("shard")
        self.q = lax.axis_index("seq")
        self.y = self.q // 2
        self.c = self.q % 2
        x, z, y, c = self.x, self.z, self.y, self.c
        self.core = (x, z, 2 * y + 1 - c)
        self.ynb = (x, z, 2 * (1 - y) + c)
        self.xnb = (1 - x, z, self.q)
        self.right = (x, z + 1, self.q)
        self.left = (x, z - 1, self.q)

    def greet(self):
        bar = pltpu.get_barrier_semaphore()
        for peer in (self.core, self.ynb, self.xnb):
            pl.semaphore_signal(bar, inc=1, device_id=peer, device_id_type=MESH)

        @pl.when(self.z > 0)
        def _():
            pl.semaphore_signal(bar, inc=1, device_id=self.left, device_id_type=MESH)

        @pl.when(self.z < self.nz - 1)
        def _():
            pl.semaphore_signal(bar, inc=1, device_id=self.right, device_id_type=MESH)

        peers = 3 + (self.z > 0).astype(jnp.int32) + (self.z < self.nz - 1).astype(jnp.int32)
        pl.semaphore_wait(bar, peers)


def rcopy(src, dst, ssem, rsem, dev):
    return pltpu.make_async_remote_copy(
        src_ref=src, dst_ref=dst, send_sem=ssem, recv_sem=rsem, device_id=dev, device_id_type=MESH
    )


def both(a, b):
    return jnp.logical_and(a, b)


def gather_body(
    nz, x_ref, tag_ref, pay_ref, mix_ref, inn_ref, out_ref,
    xa, taga, paya, mixa, inna, outa,
    loc, xs, xr, zs, zr, ns, nr, cs, cr,
):
    p = Place(nz)
    z, c, y, q = p.z, p.c, p.y, p.q
    rz = mix_ref.shape[0]
    length = x_ref.shape[1]
    half = mix_ref.shape[1] // 2
    quarter = inn_ref.shape[1] // 4
    p.greet()

    def token_block(j):
        return xa.at[:, pl.ds(pl.multiple_of(j * length, length), length)]

    x_core = rcopy(x_ref, token_block(q), xs.at[0], xr.at[0], p.core)
    x_y = rcopy(x_ref, token_block(q), xs.at[1], xr.at[1], p.ynb)
    qy = 2 * (1 - y) + c
    x_on = rcopy(token_block(qy), token_block(qy), xs.at[2], xr.at[2], p.core)
    t_core = rcopy(tag_ref, taga.at[q], xs.at[3], xr.at[3], p.core)
    t_y = rcopy(tag_ref, taga.at[q], xs.at[4], xr.at[4], p.ynb)
    t_on = rcopy(taga.at[qy], taga.at[qy], xs.at[5], xr.at[5], p.core)
    for cp in (t_y, t_core, x_y, x_core):
        cp.start()

    def mix_piece(ref):
        return ref.at[:, pl.ds(pl.multiple_of(c * half, half), half)]

    def inn_piece(ref, yy):
        return ref.at[:, pl.ds(pl.multiple_of((c * 2 + yy) * quarter, quarter), quarter)]

    def out_piece(ref, xx):
        return ref.at[pl.ds(pl.multiple_of((c * 2 + xx) * rz, 8), rz)]

    own = (
        lambda: pay_ref,
        lambda: mix_piece(mix_ref),
        lambda: inn_piece(inn_ref, y),
        lambda: out_piece(out_ref, p.x),
    )
    there = (
        lambda b: paya.at[b],
        lambda b: mix_piece(mixa.at[b]),
        lambda b: inn_piece(inna.at[b], y),
        lambda b: out_piece(outa.at[b], p.x),
    )
    other = {
        2: lambda b: inn_piece(inna.at[b], 1 - y),
        3: lambda b: out_piece(outa.at[b], 1 - p.x),
    }
    side = {2: p.ynb, 3: p.xnb}

    def zcopy(k, way, s, b, first):
        src = own[k]() if first else there[k](b)
        dev = p.right if way == 0 else p.left
        return rcopy(src, there[k](b), zs.at[k, way, s], zr.at[k, way, s], dev)

    def send_when(way, s):
        if way == 0:
            return both(z >= s - 1, z < nz - 1), z - s + 1
        return both(z <= nz - s, z > 0), z + s - 1

    def recv_when(way, s):
        if way == 0:
            return z >= s, z - s
        return z <= nz - 1 - s, z + s

    def live(s):
        return both(s >= 1, s <= nz - 1)

    def start_wave(k, s):
        for way in (0, 1):
            cond, b = send_when(way, s)
            cond = both(cond, live(s))

            @pl.when(both(cond, s == 1))
            def _():
                zcopy(k, way, s, b, True).start()

            @pl.when(both(cond, s > 1))
            def _():
                zcopy(k, way, s, b, False).start()

    def side_copy(k, b):
        return rcopy(there[k](b), there[k](b), ns.at[k - 2, b], nr.at[k - 2, b], side[k])

    def core_copy(k, b, part):
        piece = there[k](b) if part == 0 else other[k](b)
        return rcopy(piece, piece, cs.at[k - 1, part, b], cr.at[k - 1, part, b], p.core)

    def each(k, s, fn):
        for way in (0, 1):
            cond, b = recv_when(way, s)

            @pl.when(both(cond, live(s)))
            def _():
                fn(k, way, b)

    def take(k, s):
        def got(k, way, b):
            zcopy(k, way, s, b, False).wait_recv()
            if k >= 2:
                side_copy(k, b).start()
            if k >= 1:
                core_copy(k, b, 0).start()

        each(k, s, got)

    def pass_on(k, s):
        def got(k, way, b):
            side_copy(k, b).wait_recv()
            core_copy(k, b, 1).start()

        each(k, s, got)

    start_wave(0, jnp.int32(1))
    locals_ = [
        pltpu.make_async_copy(x_ref, token_block(q), loc.at[0]),
        pltpu.make_async_copy(tag_ref, taga.at[q], loc.at[1]),
        pltpu.make_async_copy(pay_ref, paya.at[z], loc.at[2]),
        pltpu.make_async_copy(mix_ref, mixa.at[z], loc.at[3]),
        pltpu.make_async_copy(inn_ref, inna.at[z], loc.at[4]),
        pltpu.make_async_copy(out_ref, outa.at[z], loc.at[5]),
    ]
    for cp in locals_:
        cp.start()

    def wave(w, carry):
        for k in range(4):
            s = w - k

            @pl.when(w > 1)
            def _():
                start_wave(k, s)

        for k in range(4):
            take(k, w - k)
        for k in (2, 3):
            pass_on(k, w - k - 1)

        @pl.when(w == 2)
        def _():
            x_y.wait_recv()
            x_on.start()
            t_y.wait_recv()
            t_on.start()

        return carry

    lax.fori_loop(1, nz + 4, wave, 0)

    for cp in locals_:
        cp.wait()
    for cp in (x_core, x_on, t_core, t_on):
        cp.wait()
    x_y.wait_send()
    t_y.wait_send()

    def drain(s, carry):
        for k in range(4):
            for way in (0, 1):
                cond, b = send_when(way, s)

                @pl.when(cond)
                def _():
                    zcopy(k, way, s, b, False).wait_send()

            def done(k, way, b):
                if k >= 2:
                    side_copy(k, b).wait_send()
                    core_copy(k, b, 1).wait()
                if k >= 1:
                    core_copy(k, b, 0).wait()

            each(k, s, done)
        return carry

    lax.fori_loop(1, nz, drain, 0)


def gather(nz, x, tags, pay, mix, inn, out):
    trees, length, width = x.shape
    dma = pltpu.SemaphoreType.DMA
    anyspace = pl.BlockSpec(memory_space=pl.ANY)
    return pl.pallas_call(
        functools.partial(gather_body, nz),
        out_shape=(
            jax.ShapeDtypeStruct((trees, 4 * length, width), x.dtype),
            jax.ShapeDtypeStruct((4,) + tags.shape, tags.dtype),
            jax.ShapeDtypeStruct((nz,) + pay.shape, pay.dtype),
            jax.ShapeDtypeStruct((nz,) + mix.shape, mix.dtype),
            jax.ShapeDtypeStruct((nz,) + inn.shape, inn.dtype),
            jax.ShapeDtypeStruct((nz,) + out.shape, out.dtype),
        ),
        in_specs=[anyspace] * 6,
        out_specs=[anyspace] * 6,
        scratch_shapes=[
            dma((6,)), dma((6,)), dma((6,)),
            dma((4, 2, nz)), dma((4, 2, nz)),
            dma((2, nz)), dma((2, nz)),
            dma((3, 2, nz)), dma((3, 2, nz)),
        ],
        compiler_params=pltpu.CompilerParams(collective_id=1, has_side_effects=True),
        name="gather_all",
    )(x, tags, pay, mix, inn, out)


def swap_body(nz, to_heads, in_ref, out_ref, loc, ss, rs):
    p = Place(nz)
    q = p.q
    bar = pltpu.get_barrier_semaphore()
    for d in (1, 2, 3):
        pl.semaphore_signal(bar, inc=1, device_id=(p.x, p.z, (q + d) % 4), device_id_type=MESH)
    pl.semaphore_wait(bar, 3)

    def src(j):
        return in_ref.at[j] if to_heads else in_ref.at[:, j]

    def dst(j):
        return out_ref.at[:, j] if to_heads else out_ref.at[j]

    copies = []
    for d in (1, 2, 3):
        t = (q + d) % 4
        cp = rcopy(src(t), dst(q), ss.at[d - 1], rs.at[d - 1], (p.x, p.z, t))
        cp.start()
        copies.append(cp)
    own = pltpu.make_async_copy(src(q), dst(q), loc)
    own.start()
    for cp in copies:
        cp.wait()
    own.wait()


def swap(nz, block, to_heads, cid):
    a, b = (0, 1) if to_heads else (1, 0)
    shape = (block.shape[1], block.shape[0]) + block.shape[2:]
    dma = pltpu.SemaphoreType.DMA
    anyspace = pl.BlockSpec(memory_space=pl.ANY)
    return pl.pallas_call(
        functools.partial(swap_body, nz, to_heads),
        out_shape=jax.ShapeDtypeStruct(shape, block.dtype),
        in_specs=[anyspace],
        out_specs=anyspace,
        scratch_shapes=[dma, dma((3,)), dma((3,))],
        compiler_params=pltpu.CompilerParams(collective_id=cid, has_side_effects=True),
        name="swap_heads" if to_heads else "swap_tokens",
    )(block)


def dot_nt(a, b):
    return lax.dot_general(a, b, (((1,), (1,)), ((), ())), preferred_element_type=f32)


def dot_tn(a, b):
    return lax.dot_general(a, b, (((0,), (0,)), ((), ())), preferred_element_type=f32)


def dot_nn(a, b):
    return jnp.dot(a, b, preferred_element_type=f32)


QB = 256


def attend_body(x_ref, w_ref, b_ref, qm_ref, km_ref, qkv_ref, att_ref, lse_ref):
    n = w_ref.shape[1] // 3
    heads = n // HD
    length = x_ref.shape[1]
    qkv_ref[0] = (dot_nn(x_ref[0], w_ref[...]) + b_ref[...]).astype(bf16)
    for h in range(heads):
        keys = jnp.concatenate([qkv_ref[0, :, n + h * HD : n + (h + 1) * HD], km_ref[0]], axis=1)
        values = qkv_ref[0, :, 2 * n + h * HD : 2 * n + (h + 1) * HD]

        def block(i, carry):
            rows = pl.ds(pl.multiple_of(i * QB, QB), QB)
            queries = jnp.concatenate(
                [qkv_ref[0, rows, h * HD : (h + 1) * HD] * 0.125, qm_ref[0, rows]], axis=1
            )
            s = dot_nt(queries, keys)
            peak = jnp.max(s, axis=1, keepdims=True)
            e = jnp.exp(s - peak)
            total = jnp.sum(e, axis=1, keepdims=True)
            o = dot_nn(e.astype(bf16), values) / total
            att_ref[0, rows, h * HD : (h + 1) * HD] = o.astype(bf16)
            lse_ref[0, rows, h : h + 1] = peak + jnp.log(total)
            return carry

        lax.fori_loop(0, length // QB, block, 0)


def attend(x_all, w, b, qm, km):
    trees, length, width = x_all.shape
    n3 = w.shape[1]
    tree = lambda d: pl.BlockSpec((1, length, d), lambda t: (t, 0, 0))
    return pl.pallas_call(
        attend_body,
        grid=(trees,),
        out_shape=(
            jax.ShapeDtypeStruct((trees, length, n3), bf16),
            jax.ShapeDtypeStruct((trees, length, n3 // 3), bf16),
            jax.ShapeDtypeStruct((trees, length, 8), f32),
        ),
        in_specs=[
            tree(width),
            pl.BlockSpec((width, n3), lambda t: (0, 0)),
            pl.BlockSpec((1, n3), lambda t: (0, 0)),
            tree(HD),
            tree(HD),
        ],
        out_specs=[tree(n3), tree(n3 // 3), tree(8)],
        compiler_params=pltpu.CompilerParams(vmem_limit_bytes=VMEM_LIMIT),
        name="attend",
    )(x_all, w, b, qm, km)


def attend_back_body(qkv_ref, do_ref, lse_ref, qm_ref, km_ref, d_ref, dk_ref, dv_ref):
    n = qkv_ref.shape[2] // 3
    heads = n // HD
    length = qkv_ref.shape[1]
    for h in range(heads):
        cols = slice(h * HD, (h + 1) * HD)
        key = qkv_ref[0, :, n + h * HD : n + (h + 1) * HD]
        keys = jnp.concatenate([key, km_ref[0]], axis=1)
        values = qkv_ref[0, :, 2 * n + h * HD : 2 * n + (h + 1) * HD]
        dk_ref[...] = jnp.zeros_like(dk_ref)
        dv_ref[...] = jnp.zeros_like(dv_ref)

        def block(i, carry):
            rows = pl.ds(pl.multiple_of(i * QB, QB), QB)
            query = qkv_ref[0, rows, cols]
            queries = jnp.concatenate([query * 0.125, qm_ref[0, rows]], axis=1)
            s = dot_nt(queries, keys)
            probs = jnp.exp(s - lse_ref[0, rows, h : h + 1])
            grad = do_ref[0, rows, cols]
            dp = dot_nt(grad, values)
            inner = jnp.sum(probs * dp, axis=1, keepdims=True)
            ds = (probs * (dp - inner)).astype(bf16)
            dv_ref[...] += dot_tn(probs.astype(bf16), grad)
            dk_ref[...] += dot_tn(ds, query)
            d_ref[0, rows, cols] = (dot_nn(ds, key) * 0.125).astype(bf16)
            return carry

        lax.fori_loop(0, length // QB, block, 0)
        d_ref[0, :, n + h * HD : n + (h + 1) * HD] = (dk_ref[...] * 0.125).astype(bf16)
        d_ref[0, :, 2 * n + h * HD : 2 * n + (h + 1) * HD] = dv_ref[...].astype(bf16)


def attend_back(qkv, do, lse, qm, km):
    trees, length, n3 = qkv.shape
    tree = lambda d: pl.BlockSpec((1, length, d), lambda t: (t, 0, 0))
    return pl.pallas_call(
        attend_back_body,
        grid=(trees,),
        out_shape=jax.ShapeDtypeStruct((trees, length, n3), bf16),
        in_specs=[tree(n3), tree(n3 // 3), tree(8), tree(HD), tree(HD)],
        out_specs=tree(n3),
        scratch_shapes=[pltpu.VMEM((length, HD), f32), pltpu.VMEM((length, HD), f32)],
        compiler_params=pltpu.CompilerParams(vmem_limit_bytes=VMEM_LIMIT),
        name="attend_back",
    )(qkv, do, lse, qm, km)


def add_to(dst, src):
    dst[...] = (dst[...].astype(f32) + src[...].astype(f32)).astype(dst.dtype)


def reduce_body(
    nz, inn, out, mix, qkv, ig, vec,
    o_inn, o_out, o_mix, o_qkv, o_ig, o_vec,
    ci, co, cm, cg, xi, yo, yi, xo, yg, zi, zo, zm, zq, aq, xm, ym, xq, v_in, v_z, v_acc,
    loc, cs, cr, s1, r1, s2, r2, zs, zr, gs, gr, vs, vr,
):
    p = Place(nz)
    z, c, y, x, q = p.z, p.c, p.y, p.x, p.q
    rz = mix.shape[1]
    wide = inn.shape[2]
    width = mix.shape[2]
    h = width // 2
    p.greet()

    def lanes(start, size):
        return pl.ds(pl.multiple_of(start, 128), size)

    def rows(start, size):
        return pl.ds(pl.multiple_of(start, 8), size)

    w2, w4, w8 = wide // 2, wide // 4, wide // 8
    first = [
        rcopy(ig.at[:, 1 - c], cg.at[0], cs.at[0], cr.at[0], p.core),
        rcopy(ig.at[:, 3 - c], cg.at[1], cs.at[1], cr.at[1], p.core),
        rcopy(vec, v_in.at[0], cs.at[2], cr.at[2], p.core),
        rcopy(mix.at[:, :, lanes((1 - c) * h, h)], cm, cs.at[3], cr.at[3], p.core),
        rcopy(out.at[:, :, lanes((1 - c) * h, h)], co, cs.at[4], cr.at[4], p.core),
        rcopy(inn.at[:, :, lanes((1 - c) * w2, w2)], ci, cs.at[5], cr.at[5], p.core),
    ]
    for cp in first:
        cp.start()

    def ig_sum(b):
        @pl.when(c == 0)
        def _():
            add_to(cg.at[b], ig.at[:, 2 * b])

        @pl.when(c == 1)
        def _():
            add_to(cg.at[b], ig.at[:, 2 * b + 1])

    first[0].wait()
    first[1].wait()
    ig_sum(0)
    ig_sum(1)
    ig_y = rcopy(cg.at[1 - y], yg, s1.at[2], r1.at[2], p.ynb)
    ig_y.start()

    first[2].wait()
    v_acc[...] = vec[...] + v_in[0]
    v_x = rcopy(v_acc, v_in.at[1], vs.at[0], vr.at[0], p.xnb)
    v_x.start()

    first[3].wait()

    def mix_sum(i, carry):
        add_to(cm.at[i], mix.at[i, :, lanes(c * h, h)])
        return carry

    lax.fori_loop(0, nz, mix_sum, 0)

    first[4].wait()

    def out_sum(i, carry):
        for j in range(4):
            add_to(co.at[i, j * rz : (j + 1) * rz], out.at[i, j * rz : (j + 1) * rz, lanes(c * h, h)])
        return carry

    lax.fori_loop(0, nz, out_sum, 0)
    out_y = rcopy(co.at[:, rows((1 - y) * 2 * rz, 2 * rz)], yo, s1.at[1], r1.at[1], p.ynb)
    out_y.start()
    first[5].wait()

    def inn_sum(i, carry):
        for j in range(4):
            add_to(ci.at[i, :, j * w8 : (j + 1) * w8], inn.at[i, :, lanes(c * w2 + j * w8, w8)])
        return carry

    lax.fori_loop(0, nz, inn_sum, 0)
    inn_x = rcopy(ci.at[:, :, lanes((1 - x) * w4, w4)], xi, s1.at[0], r1.at[0], p.xnb)
    inn_x.start()

    def chain(k, acc, buf):
        def copy(way, s, d):
            dev = p.right if way == 0 else p.left
            return rcopy(acc(d), buf(way, d), zs.at[k, way, s], zr.at[k, way, s], dev)

        def sending(way, s):
            if way == 0:
                d = z + nz - s
                return both(d <= nz - 1, z < nz - 1), d
            d = z - nz + s
            return both(d >= 0, z > 0), d

        def getting(way, s):
            if way == 0:
                d = z - 1 + nz - s
                return both(d <= nz - 1, z > 0), d
            d = z + 1 - nz + s
            return both(d >= 0, z < nz - 1), d

        def send(s):
            for way in (0, 1):
                ok, d = sending(way, s)

                @pl.when(ok)
                def _():
                    copy(way, s, d).start()

        def get(s):
            for way in (0, 1):
                ok, d = getting(way, s)

                @pl.when(ok)
                def _():
                    copy(way, s, d).wait_recv()
                    add_to(acc(d), buf(way, d))

        def drain(s, carry):
            for way in (0, 1):
                ok, d = sending(way, s)

                @pl.when(ok)
                def _():
                    copy(way, s, d).wait_send()

            return carry

        return send, get, lambda: lax.fori_loop(1, nz, drain, 0)

    def own_qkv(i, carry):
        aq[i] = qkv[i]
        return carry

    lax.fori_loop(0, nz, own_qkv, 0)
    qkv_chain = chain(0, lambda d: aq.at[d], lambda way, d: zq.at[way, d])
    mix_chain = chain(1, lambda d: cm.at[d], lambda way, d: zm.at[way, d])

    def late(s, carry):
        qkv_chain[0](s)
        mix_chain[0](s)
        qkv_chain[1](s)
        mix_chain[1](s)
        return carry

    lax.fori_loop(1, nz, late, 0)

    v_x.wait()
    v_acc[...] = v_acc[...] + v_in[1]
    v_y = rcopy(v_acc, v_in.at[2], vs.at[1], vr.at[1], p.ynb)
    v_y.start()

    x_q = rcopy(aq.at[z], xq, gs.at[0], gr.at[0], p.xnb)
    x_m = rcopy(cm.at[z], xm, gs.at[1], gr.at[1], p.xnb)
    x_q.start()
    x_m.start()

    inn_x.wait()

    def inn_sum2(i, carry):
        add_to(xi.at[i], ci.at[i, :, lanes(x * w4, w4)])
        return carry

    lax.fori_loop(0, nz, inn_sum2, 0)
    inn_y = rcopy(xi.at[:, :, lanes((1 - y) * w8, w8)], yi, s2.at[0], r2.at[0], p.ynb)
    inn_y.start()
    out_y.wait()

    def out_sum2(i, carry):
        add_to(yo.at[i], co.at[i, rows(y * 2 * rz, 2 * rz)])
        return carry

    lax.fori_loop(0, nz, out_sum2, 0)
    out_x = rcopy(yo.at[:, rows((1 - x) * rz, rz)], xo, s2.at[1], r2.at[1], p.xnb)
    out_x.start()

    v_y.wait()
    v_acc[...] = v_acc[...] + v_in[2]
    v_z[z] = v_acc[...]

    ig_y.wait()
    o_ig[...] = (cg[y].astype(f32) + yg[...].astype(f32)).astype(o_ig.dtype)

    x_q.wait()
    o_qkv[q] = (aq[z].astype(f32) + xq[...].astype(f32)).astype(bf16)
    q_core = rcopy(o_qkv.at[q], o_qkv.at[q], gs.at[2], gr.at[2], p.core)
    q_y = rcopy(o_qkv.at[q], o_qkv.at[q], gs.at[3], gr.at[3], p.ynb)
    q_y.start()
    q_core.start()
    x_m.wait()
    add_to(xm, cm.at[z])
    y_m = rcopy(xm, ym, gs.at[4], gr.at[4], p.ynb)
    y_m.start()

    inn_y.wait()

    def inn_sum3(i, carry):
        add_to(yi.at[i], xi.at[i, :, lanes(y * w8, w8)])
        return carry

    lax.fori_loop(0, nz, inn_sum3, 0)
    out_x.wait()

    def out_sum3(i, carry):
        add_to(xo.at[i], yo.at[i, rows(x * rz, rz)])
        return carry

    lax.fori_loop(0, nz, out_sum3, 0)

    inn_chain = chain(2, lambda d: yi.at[d], lambda way, d: zi.at[way, d])
    out_chain = chain(3, lambda d: xo.at[d], lambda way, d: zo.at[way, d])

    def vcopy(way, s, b):
        dev = p.right if way == 0 else p.left
        return rcopy(v_z.at[b], v_z.at[b], zs.at[4, way, s], zr.at[4, way, s], dev)

    def vsend(way, s):
        if way == 0:
            return both(z >= s - 1, z < nz - 1), z - s + 1
        return both(z <= nz - s, z > 0), z + s - 1

    def vget(way, s):
        if way == 0:
            return z >= s, z - s
        return z <= nz - 1 - s, z + s

    def last(s, carry):
        inn_chain[0](s)
        out_chain[0](s)
        for way in (0, 1):
            ok, b = vsend(way, s)

            @pl.when(ok)
            def _():
                vcopy(way, s, b).start()

        inn_chain[1](s)
        out_chain[1](s)
        for way in (0, 1):
            ok, b = vget(way, s)

            @pl.when(ok)
            def _():
                vcopy(way, s, b).wait_recv()

        return carry

    lax.fori_loop(1, nz, last, 0)

    def i_at(xx, yy):
        return o_inn.at[:, lanes(c * w2 + xx * w4 + yy * w8, w8)]

    def i_half(xx):
        return o_inn.at[:, lanes(c * w2 + xx * w4, w4)]

    def o_at(xx, yy):
        return o_out.at[rows((2 * yy + xx) * rz, rz), lanes(c * h, h)]

    def o_half(yy):
        return o_out.at[rows(2 * yy * rz, 2 * rz), lanes(c * h, h)]

    o_inn[:, lanes(c * w2 + x * w4 + y * w8, w8)] = yi[z]
    o_out[rows((2 * y + x) * rz, rz), lanes(c * h, h)] = xo[z]
    i_y = rcopy(i_at(x, y), i_at(x, y), gs.at[5], gr.at[5], p.ynb)
    o_x = rcopy(o_at(x, y), o_at(x, y), gs.at[6], gr.at[6], p.xnb)
    i_y.start()
    o_x.start()
    y_m.wait()
    o_mix[:, lanes(c * h, h)] = (xm[...].astype(f32) + ym[...].astype(f32)).astype(bf16)
    m_core = rcopy(
        o_mix.at[:, lanes(c * h, h)], o_mix.at[:, lanes(c * h, h)], gs.at[7], gr.at[7], p.core
    )
    m_core.start()
    q_y.wait()
    qy = 2 * (1 - y) + c
    q_on = rcopy(o_qkv.at[qy], o_qkv.at[qy], gs.at[8], gr.at[8], p.core)
    q_on.start()

    def v_sum(i, carry):
        return carry + v_z[i]

    o_vec[...] = lax.fori_loop(0, nz, v_sum, jnp.zeros(o_vec.shape, f32))

    i_y.wait()
    i_x = rcopy(i_half(x), i_half(x), gs.at[9], gr.at[9], p.xnb)
    i_x.start()
    o_x.wait()
    o_y = rcopy(o_half(y), o_half(y), gs.at[10], gr.at[10], p.ynb)
    o_y.start()
    i_x.wait()
    i_all = o_inn.at[:, lanes(c * w2, w2)]
    i_core = rcopy(i_all, i_all, gs.at[11], gr.at[11], p.core)
    i_core.start()
    o_y.wait()
    o_all = o_out.at[:, lanes(c * h, h)]
    o_core = rcopy(o_all, o_all, gs.at[12], gr.at[12], p.core)
    o_core.start()
    for cp in (m_core, q_core, q_on, i_core, o_core):
        cp.wait()
    for ch in (qkv_chain, mix_chain, inn_chain, out_chain):
        ch[2]()

    def vdrain(s, carry):
        for way in (0, 1):
            ok, b = vsend(way, s)

            @pl.when(ok)
            def _():
                vcopy(way, s, b).wait_send()

        return carry

    lax.fori_loop(1, nz, vdrain, 0)


def reduce_all(nz, inn, out, mix, qkv, ig, vec):
    rz, width = mix.shape[1], mix.shape[2]
    wide = inn.shape[2]
    h, w2, w4, w8 = width // 2, wide // 2, wide // 4, wide // 8
    n3 = qkv.shape[2]
    trees, _, length, _ = ig.shape
    dma = pltpu.SemaphoreType.DMA
    V = pltpu.VMEM
    vm = pl.BlockSpec(memory_space=pltpu.VMEM)
    return pl.pallas_call(
        functools.partial(reduce_body, nz),
        out_shape=(
            jax.ShapeDtypeStruct((rz, wide), bf16),
            jax.ShapeDtypeStruct((4 * rz, width), bf16),
            jax.ShapeDtypeStruct((rz, width), bf16),
            jax.ShapeDtypeStruct((4, rz, n3), bf16),
            jax.ShapeDtypeStruct((trees, length, width), bf16),
            jax.ShapeDtypeStruct(vec.shape, f32),
        ),
        in_specs=[vm] * 6,
        out_specs=[vm] * 6,
        scratch_shapes=[
            V((nz, rz, w2), bf16),
            V((nz, 4 * rz, h), bf16),
            V((nz, rz, h), bf16),
            V((2, trees, length, width), bf16),
            V((nz, rz, w4), bf16),
            V((nz, 2 * rz, h), bf16),
            V((nz, rz, w8), bf16),
            V((nz, rz, h), bf16),
            V((trees, length, width), bf16),
            V((2, nz, rz, w8), bf16),
            V((2, nz, rz, h), bf16),
            V((2, nz, rz, h), bf16),
            V((2, nz, rz, n3), bf16),
            V((nz, rz, n3), bf16),
            V((rz, h), bf16),
            V((rz, h), bf16),
            V((rz, n3), bf16),
            V((3,) + vec.shape, f32),
            V((nz,) + vec.shape, f32),
            V(vec.shape, f32),
            dma,
            dma((6,)), dma((6,)),
            dma((3,)), dma((3,)),
            dma((2,)), dma((2,)),
            dma((5, 2, nz)), dma((5, 2, nz)),
            dma((13,)), dma((13,)),
            dma((2,)), dma((2,)),
        ],
        compiler_params=pltpu.CompilerParams(
            collective_id=4, has_side_effects=True, vmem_limit_bytes=VMEM_LIMIT
        ),
        name="reduce_all",
    )(inn, out, mix, qkv, ig, vec)


def normed(resid):
    center = resid - jnp.mean(resid, axis=-1, keepdims=True)
    spread = jnp.mean(center * center, axis=-1, keepdims=True)
    inv = lax.rsqrt(spread + norm_eps)
    return center * inv, inv


def norm_back(grad_hat, hat, inv):
    mean = jnp.mean(grad_hat, axis=-1, keepdims=True)
    along = jnp.mean(grad_hat * hat, axis=-1, keepdims=True)
    return inv * (grad_hat - mean - hat * along)


def per_device(
    nz,
    tokens, teacher, seg_ids, parent_seg, valid,
    query_weight, query_bias, key_weight, value_weight, value_bias,
    mix_weight, mix_bias, first_gain, first_shift,
    inner_weight, inner_bias, outer_weight, outer_bias, second_gain, second_shift,
):
    trees, local_len, width = tokens.shape
    n_seq = lax.axis_size("seq")
    full_len = local_len * n_seq
    row_count = trees * local_len
    total_slots = row_count * lax.axis_size("replica") * nz * n_seq
    seq = lax.axis_index("seq")
    rz = mix_weight.shape[0]
    cols = width // n_seq

    def mine(w):
        return lax.dynamic_slice_in_dim(w, seq * cols, cols, axis=1)

    heads_weight = jnp.concatenate([mine(query_weight), mine(key_weight), mine(value_weight)], axis=1)
    small = (query_bias, value_bias, mix_bias, first_gain, first_shift, outer_bias, second_gain, second_shift, inner_bias)
    flat = jnp.concatenate(small)
    flat = jnp.pad(flat, (0, 8 * 3 * cols - flat.shape[0])).reshape(8, 3 * cols)
    pay = jnp.concatenate([heads_weight, flat], axis=0)
    tags = jnp.where(valid == 1, seg_ids, seg_ids + NSEG).reshape(1, row_count)
    tags = jnp.broadcast_to(tags, (8, row_count))

    x_all, tags_all, pay_all, mix_all, inn_all, out_all = gather(
        nz, tokens, tags, pay, mix_weight, inner_weight, outer_weight
    )

    vecs = pay_all[:, rz:].reshape(nz, -1)
    whole = [vecs[:, i * rz : (i + 1) * rz].reshape(width).astype(f32) for i in range(8)]
    b_query, b_value, b_mix, g_first, s_first, b_outer, g_second, s_second = whole
    b_inner = vecs[:, 8 * rz : 8 * rz + inner_bias.shape[0]].reshape(-1).astype(f32)
    w_heads = pay_all[:, :rz].reshape(width, 3 * cols)
    w_mix = mix_all.reshape(width, width)
    w_inner = inn_all.reshape(width, -1)
    w_outer = out_all.reshape(-1, width)

    def own_part(v):
        return lax.dynamic_slice_in_dim(v, seq * cols, cols, axis=0)

    b_heads = jnp.concatenate([own_part(b_query), jnp.zeros((cols,), f32), own_part(b_value)])[None]

    segment_range = jnp.arange(NSEG, dtype=jnp.int32)
    choose = (parent_seg[..., None] == segment_range).astype(f32)
    current = jnp.broadcast_to(jnp.eye(NSEG, dtype=f32), choose.shape)
    table = current
    for level in range(NSEG - 1):
        current = jnp.sum(current[..., None] * choose[:, None], axis=2)
        table = jnp.maximum(table, current)
    tag = tags_all[:, 0].reshape(n_seq, trees, local_len).transpose(1, 0, 2).reshape(trees, full_len)
    segs = tag % NSEG
    hidden_key = (tag >= NSEG).astype(f32)
    onehot = (segs[..., None] == segment_range).astype(f32)
    seen = jnp.sum(onehot[..., None] * table[:, None], axis=2)
    q_feat = jnp.concatenate(
        [(seen - 1.0) * BIG, jnp.full((trees, full_len, 1), -BIG, f32)], axis=-1
    )
    k_feat = jnp.concatenate([onehot, hidden_key[..., None]], axis=-1)
    pad = ((0, 0), (0, 0), (0, HD - NSEG - 1))
    q_feat = jnp.pad(q_feat, pad).astype(bf16)
    k_feat = jnp.pad(k_feat, pad).astype(bf16)

    qkv, att_heads, lse = attend(x_all, w_heads, b_heads, q_feat, k_feat)
    att_blocks = swap(nz, att_heads.reshape(trees, n_seq, local_len, cols), False, 2)
    attended = att_blocks.reshape(n_seq, row_count, cols).transpose(1, 0, 2).reshape(row_count, width)

    inputs = tokens.reshape(row_count, width)
    resid_one = inputs.astype(f32) + dot_nn(attended, w_mix) + b_mix
    hat_one, inv_one = normed(resid_one)
    first = hat_one * g_first + s_first
    first_low = first.astype(bf16)
    hidden_pre = dot_nn(first_low, w_inner) + b_inner
    cdf = 0.5 + 0.5 * lax.erf(hidden_pre * (0.5**0.5))
    slope = cdf + hidden_pre * jnp.exp(-0.5 * hidden_pre * hidden_pre) * 0.3989422804014327
    hidden = (hidden_pre * cdf).astype(bf16)
    resid_two = first + dot_nn(hidden, w_outer) + b_outer
    hat_two, inv_two = normed(resid_two)
    output = hat_two * g_second + s_second
    layer_out = output.astype(bf16).reshape(trees, local_len, width)
    error = output - teacher.reshape(row_count, width).astype(f32)
    row_weight = valid.astype(f32).reshape(row_count, 1)
    weighted = row_weight * error
    local_loss = jnp.sum(weighted * error)
    local_count = jnp.sum(row_weight)

    grad_out = 2.0 * weighted
    dsecond_gain = jnp.sum(grad_out * hat_two, axis=0)
    dsecond_shift = jnp.sum(grad_out, axis=0)
    grad_two = norm_back(grad_out * g_second, hat_two, inv_two)
    grad_ffn = grad_two.astype(bf16)
    douter_bias = jnp.sum(grad_ffn, axis=0, dtype=f32)
    douter_weight = dot_tn(hidden, grad_ffn).astype(bf16)
    grad_pre = (dot_nt(grad_ffn, w_outer) * slope).astype(bf16)
    dinner_bias = jnp.sum(grad_pre, axis=0, dtype=f32)
    dinner_weight = dot_tn(first_low, grad_pre).astype(bf16)
    grad_first = grad_two + dot_nt(grad_pre, w_inner)
    dfirst_gain = jnp.sum(grad_first * hat_one, axis=0)
    dfirst_shift = jnp.sum(grad_first, axis=0)
    grad_one = norm_back(grad_first * g_first, hat_one, inv_one)
    grad_branch = grad_one.astype(bf16)
    dmix_bias = jnp.sum(grad_branch, axis=0, dtype=f32)
    dmix_weight = dot_tn(attended, grad_branch).astype(bf16)
    grad_attended = dot_nt(grad_branch, w_mix).astype(bf16)
    grad_blocks = grad_attended.reshape(trees, local_len, n_seq, cols).transpose(2, 0, 1, 3)
    grad_heads = swap(nz, grad_blocks, True, 3).reshape(trees, full_len, cols)

    dqkv = attend_back(qkv, grad_heads, lse, q_feat, k_feat).reshape(trees * full_len, 3 * cols)
    dheads = dot_tn(x_all.reshape(trees * full_len, width), dqkv).astype(bf16)
    dbias = jnp.sum(dqkv, axis=0, dtype=f32)
    partial = dot_nt(dqkv, w_heads).astype(bf16).reshape(trees, n_seq, local_len, width)

    def place(v):
        return lax.dynamic_update_slice_in_dim(jnp.zeros((width,), f32), v, seq * cols, axis=0)

    scalars = jnp.concatenate([jnp.stack([local_loss, local_count]), jnp.zeros((width - 2,), f32)])
    vec = jnp.concatenate(
        [place(dbias[:cols]), place(dbias[2 * cols :]), dmix_bias, dfirst_gain, dfirst_shift,
         douter_bias, dsecond_gain, dsecond_shift, dinner_bias, scalars]
    ).reshape(-1, width)
    vec = jnp.pad(vec, ((0, 16 - vec.shape[0]), (0, 0)))

    r_inn, r_out, r_mix, r_qkv, r_ig, r_vec = reduce_all(
        nz,
        dinner_weight.reshape(nz, rz, -1),
        douter_weight.reshape(nz, 4 * rz, width),
        dmix_weight.reshape(nz, rz, width),
        dheads.reshape(nz, rz, 3 * cols),
        partial,
        vec,
    )
    flat = r_vec.reshape(-1)
    wide = inner_bias.shape[0] * nz
    spot = 8 * width + wide
    count = flat[spot + 1]
    scale = total_slots / count
    loss_value = flat[spot] / count
    shard = lax.axis_index("shard")

    def vec_out(i):
        return lax.dynamic_slice_in_dim(flat, i * width + shard * rz, rz, axis=0) * scale

    dinner_bias = (
        lax.dynamic_slice_in_dim(flat, 8 * width + shard * inner_bias.shape[0], inner_bias.shape[0], axis=0) * scale
    )

    def full(w):
        return w.astype(f32) * scale

    def heads_out(i):
        part = r_qkv[:, :, i * cols : (i + 1) * cols].transpose(1, 0, 2).reshape(rz, width)
        return full(part)

    input_grad = (grad_one.reshape(trees, local_len, width) + r_ig.astype(f32)) * scale
    return (
        layer_out, loss_value, input_grad,
        heads_out(0), vec_out(0), heads_out(1), heads_out(2), vec_out(1),
        full(r_mix), vec_out(2), vec_out(3), vec_out(4),
        full(r_inn), dinner_bias, full(r_out), vec_out(5), vec_out(6), vec_out(7),
    )


def solution(mesh):
    rows = P(("replica", "shard"), "seq", None)
    line = P(("replica", "shard"), "seq")
    mat = P("shard", None)
    row = P("shard")
    placed = (
        rows, rows, line, P(("replica", "shard"), None), line,
        mat, row, mat, mat, row, mat, row, row, row, mat, row, mat, row, row, row,
    )
    return jax.shard_map(
        functools.partial(per_device, mesh.shape["shard"]),
        mesh=mesh,
        in_specs=placed,
        out_specs=(
            rows, P(), rows,
            mat, row, mat, mat, row, mat, row, row, row, mat, row, mat, row, row, row,
        ),
        check_vma=False,
    )
```

```python
import functools

import jax
import jax.numpy as jnp
from jax import lax
from jax.experimental import pallas as pl
from jax.experimental.pallas import tpu as pltpu
from jax.sharding import PartitionSpec as P

HEADS = 12
HD = 64
NSEG = 8
MESH = pl.DeviceIdType.MESH
BIG = 1e30
norm_eps = 1e-12
f32 = jnp.float32
bf16 = jnp.bfloat16
VMEM_LIMIT = 60 * 1024 * 1024


class Place:
    def __init__(self, nz):
        self.nz = nz
        self.x = lax.axis_index("replica")
        self.z = lax.axis_index("shard")
        self.q = lax.axis_index("seq")
        self.y = self.q // 2
        self.c = self.q % 2
        x, z, y, c = self.x, self.z, self.y, self.c
        self.core = (x, z, 2 * y + 1 - c)
        self.ynb = (x, z, 2 * (1 - y) + c)
        self.xnb = (1 - x, z, self.q)
        self.right = (x, z + 1, self.q)
        self.left = (x, z - 1, self.q)

    def greet(self, more):
        bar = pltpu.get_barrier_semaphore()
        for peer in [self.core, self.ynb, self.xnb] + more:
            pl.semaphore_signal(bar, inc=1, device_id=peer, device_id_type=MESH)

        @pl.when(self.z > 0)
        def _():
            pl.semaphore_signal(bar, inc=1, device_id=self.left, device_id_type=MESH)

        @pl.when(self.z < self.nz - 1)
        def _():
            pl.semaphore_signal(bar, inc=1, device_id=self.right, device_id_type=MESH)

        peers = 3 + len(more) + (self.z > 0).astype(jnp.int32) + (self.z < self.nz - 1).astype(jnp.int32)
        pl.semaphore_wait(bar, peers)


def rcopy(src, dst, ssem, rsem, dev):
    return pltpu.make_async_remote_copy(
        src_ref=src, dst_ref=dst, send_sem=ssem, recv_sem=rsem, device_id=dev, device_id_type=MESH
    )


def both(a, b):
    return jnp.logical_and(a, b)


def dot_nt(a, b):
    return lax.dot_general(a, b, (((1,), (1,)), ((), ())), preferred_element_type=f32)


def dot_tn(a, b):
    return lax.dot_general(a, b, (((0,), (0,)), ((), ())), preferred_element_type=f32)


def dot_nn(a, b):
    return jnp.dot(a, b, preferred_element_type=f32)


def add_to(dst, src):
    dst[...] = (dst[...].astype(f32) + src[...].astype(f32)).astype(dst.dtype)


def lanes(start, size):
    return pl.ds(pl.multiple_of(start, 128), size)


def rows_at(start, size):
    return pl.ds(pl.multiple_of(start, 8), size)


QB = 256
DMA = pltpu.SemaphoreType.DMA
V = pltpu.VMEM


def spread_send(way, s, z, nz):
    if way == 0:
        return both(z >= s - 1, z < nz - 1), z - s + 1
    return both(z <= nz - s, z > 0), z + s - 1


def spread_get(way, s, z, nz):
    if way == 0:
        return z >= s, z - s
    return z <= nz - 1 - s, z + s


def queries_of(qkv_ref, feat_ref, t, rows, h):
    q = qkv_ref[t, rows, h * HD : (h + 1) * HD] * 0.125
    return jnp.concatenate([q, feat_ref[t, rows, HD : 2 * HD]], axis=1)


def keys_of(qkv_ref, feat_ref, t, h, n):
    key = qkv_ref[t, :, n + h * HD : n + (h + 1) * HD]
    return jnp.concatenate([key, feat_ref[t, :, 3 * HD : 4 * HD]], axis=1)


def front_body(
    nz, x_ref, seg_ref, valid_ref, par_ref, wq_ref, wk_ref, wv_ref, sm_ref, bi_ref, mix_ref, inn_ref, out_ref,
    xa, pw, qkv_ref, lse_ref, feat_ref, blocks_ref, vec_ref, binner_ref, mixa, inna, outa,
    bits, sma, bia, tga, att_ref,
    loc, xs, xr, zs, zr, ns, nr, cs, cr, hs, hr,
):
    p = Place(nz)
    z, c, y, x, q = p.z, p.c, p.y, p.x, p.q
    rz, width = mix_ref.shape
    wide = inn_ref.shape[1]
    trees, length = x_ref.shape[0], x_ref.shape[1]
    full = xa.shape[1]
    n = width // 4
    heads = n // HD
    half, quarter = width // 2, wide // 4
    cross = (x, z, 2 * (1 - y) + 1 - c)
    p.greet([cross])

    def token_block(j):
        return xa.at[:, pl.ds(pl.multiple_of(j * length, length), length)]

    qy = 2 * (1 - y) + c
    for t in range(trees):
        seg = seg_ref[t : t + 1, :]
        tga[q, 0:1, t * length : (t + 1) * length] = jnp.where(
            valid_ref[t : t + 1, :] == 1, seg, seg + NSEG
        )
    x_core = rcopy(x_ref, token_block(q), xs.at[0], xr.at[0], p.core)
    x_y = rcopy(x_ref, token_block(q), xs.at[1], xr.at[1], p.ynb)
    x_on = rcopy(token_block(qy), token_block(qy), xs.at[2], xr.at[2], p.core)
    t_core = rcopy(tga.at[q], tga.at[q], xs.at[3], xr.at[3], p.core)
    t_y = rcopy(tga.at[q], tga.at[q], xs.at[4], xr.at[4], p.ynb)
    t_on = rcopy(tga.at[qy], tga.at[qy], xs.at[5], xr.at[5], p.core)
    for cp in (t_y, t_core, x_y, x_core):
        cp.start()

    back = lax.rem(width - q * n, width)
    for i, w in enumerate((wq_ref, wk_ref, wv_ref)):
        turned = pltpu.roll(w[...].astype(f32), back, 1)
        pw[z, :, i * n : (i + 1) * n] = turned[:, :n].astype(bf16)
    sma[z] = pltpu.roll(sm_ref[...].astype(f32), z * rz, 1).astype(bf16)
    bia[z] = pltpu.roll(bi_ref[...].astype(f32), z * (wide // nz), 1).astype(bf16)

    def mix_piece(ref):
        return ref.at[:, lanes(c * half, half)]

    def inn_piece(ref, yy):
        return ref.at[:, lanes((c * 2 + yy) * quarter, quarter)]

    def out_piece(ref, xx):
        return ref.at[rows_at((c * 2 + xx) * rz, rz)]

    own = {
        0: lambda: pw.at[z],
        1: lambda: sma.at[z],
        2: lambda: bia.at[z],
        3: lambda: mix_piece(mix_ref),
        4: lambda: inn_piece(inn_ref, y),
        5: lambda: out_piece(out_ref, x),
    }
    there = {
        0: lambda b: pw.at[b],
        1: lambda b: sma.at[b],
        2: lambda b: bia.at[b],
        3: lambda b: mix_piece(mixa.at[b]),
        4: lambda b: inn_piece(inna.at[b], y),
        5: lambda b: out_piece(outa.at[b], x),
    }
    other = {
        4: lambda b: inn_piece(inna.at[b], 1 - y),
        5: lambda b: out_piece(outa.at[b], 1 - x),
    }
    side = {4: p.ynb, 5: p.xnb}

    def zcopy(k, way, s, b, first):
        src = own[k]() if first else there[k](b)
        dev = p.right if way == 0 else p.left
        return rcopy(src, there[k](b), zs.at[k, way, s], zr.at[k, way, s], dev)

    def start_step(k, s):
        for way in (0, 1):
            cond, b = spread_send(way, s, z, nz)
            cond = both(cond, s <= nz - 1)
            if isinstance(s, int):

                @pl.when(cond)
                def _():
                    zcopy(k, way, s, b, s == 1).start()

            else:

                @pl.when(cond)
                def _():
                    zcopy(k, way, s, b, False).start()

    def each(s, fn):
        for way in (0, 1):
            cond, b = spread_get(way, s, z, nz)

            @pl.when(cond)
            def _():
                fn(way, b)

    def side_copy(k, b):
        return rcopy(there[k](b), there[k](b), ns.at[k - 4, b], nr.at[k - 4, b], side[k])

    def core_copy(k, b, part):
        piece = there[k](b) if part == 0 else other[k](b)
        return rcopy(piece, piece, cs.at[k - 3, part, b], cr.at[k - 3, part, b], p.core)

    for k in (0, 1, 2):
        start_step(k, 1)
    locals_ = [
        pltpu.make_async_copy(x_ref, token_block(q), loc.at[0]),
        pltpu.make_async_copy(mix_ref, mixa.at[z], loc.at[1]),
        pltpu.make_async_copy(inn_ref, inna.at[z], loc.at[2]),
        pltpu.make_async_copy(out_ref, outa.at[z], loc.at[3]),
    ]
    for cp in locals_:
        cp.start()

    def small_step(s, carry):
        for k in (0, 1, 2):
            each(s, lambda way, b: zcopy(k, way, s, b, False).wait_recv())
        for k in (0, 1, 2):
            start_step(k, s + 1)
        return carry

    lax.fori_loop(1, nz - 1, small_step, 0)
    for k in (3, 4, 5):
        start_step(k, 1)
    for k in (0, 1, 2):
        each(nz - 1, lambda way, b: zcopy(k, way, nz - 1, b, False).wait_recv())

    def weights_step(s):
        for k in (3, 4, 5):

            def got(way, b):
                zcopy(k, way, s, b, False).wait_recv()
                if k >= 4:
                    side_copy(k, b).start()
                core_copy(k, b, 0).start()

            each(s, got)
            start_step(k, s + 1)

    def pass_on(s):
        for k in (4, 5):

            def got(way, b):
                side_copy(k, b).wait_recv()
                core_copy(k, b, 1).start()

            each(s, got)

    def vsum(i, carry):
        return carry[0] + sma[i].astype(f32), carry[1] + bia[i].astype(f32)

    vecs, binner = lax.fori_loop(
        0, nz, vsum, (jnp.zeros(vec_ref.shape, f32), jnp.zeros(binner_ref.shape, f32))
    )
    vec_ref[...] = vecs
    binner_ref[...] = binner
    turned = pltpu.roll(vecs, back, 1)
    bias = jnp.concatenate([turned[0:1, :n], jnp.zeros((1, n), f32), turned[1:2, :n]], axis=1)

    t_y.wait_recv()
    t_on.start()
    x_y.wait_recv()
    x_on.start()
    locals_[0].wait()
    t_core.wait()
    x_core.wait()
    t_on.wait()
    x_on.wait()

    row = lax.broadcasted_iota(jnp.int32, (16, 4 * HD), 0)
    lane = lax.broadcasted_iota(jnp.int32, (16, 4 * HD), 1)
    trow = lax.broadcasted_iota(jnp.int32, (16, full), 0)
    for t in range(trees):
        bits[t, 0] = jnp.int32(1)
        for s in range(1, NSEG):
            bits[t, s] = bits[t, par_ref[t, s]] + (1 << s)
        seen = jnp.zeros((16, 4 * HD), jnp.int32)
        for a in range(NSEG):
            seen = jnp.where(row == a, bits[t, a], seen)
        at = jnp.clip(lane - HD, 0, NSEG)
        unseen = ((seen >> at) & 1) == 0
        q_side = both(both(row < NSEG, both(lane >= HD, lane <= HD + NSEG)), unseen)
        k_side = both(row <= NSEG, lane == row + 3 * HD)
        table = jnp.where(q_side, -BIG, jnp.where(k_side, 1.0, 0.0)).astype(bf16)
        tag = jnp.concatenate(
            [tga[j, 0:1, t * length : (t + 1) * length] for j in range(full // length)], axis=1
        )
        gone = tag >= NSEG
        seg = jnp.where(gone, tag - NSEG, tag)
        seg = jnp.broadcast_to(seg, (16, full))
        gone = jnp.broadcast_to(jnp.where(gone, 1, 0), (16, full))
        hot = jnp.where(trow == NSEG, gone, jnp.where(trow == seg, 1, 0)).astype(f32).astype(bf16)
        feat_ref[t] = dot_tn(hot, table).astype(bf16)

    w_heads = pw[...].reshape(width, 3 * n)
    for t in range(trees):
        qkv_ref[t] = (dot_nn(xa[t], w_heads) + bias).astype(bf16)

    def send_heads(t, d):
        to = lax.rem(q + d, 4)
        rows = pl.ds(pl.multiple_of(to * length, length), length)
        return rcopy(
            att_ref.at[t, rows], blocks_ref.at[q, t], hs.at[t, d - 1], hr.at[t, d - 1], (x, z, to)
        )

    done = 0
    for t in range(trees):
        for h in range(heads):
            keys = keys_of(qkv_ref, feat_ref, t, h, n)
            values = qkv_ref[t, :, 2 * n + h * HD : 2 * n + (h + 1) * HD]

            def block(i, carry):
                rows = pl.ds(pl.multiple_of(i * QB, QB), QB)
                s = dot_nt(queries_of(qkv_ref, feat_ref, t, rows, h), keys)
                peak = jnp.max(s, axis=1, keepdims=True)
                e = jnp.exp(s - peak)
                total = jnp.sum(e, axis=1, keepdims=True)
                o = dot_nn(e.astype(bf16), values) / total
                att_ref[t, rows, h * HD : (h + 1) * HD] = o.astype(bf16)
                lse_ref[t, rows, h : h + 1] = peak + jnp.log(total)
                return carry

            lax.fori_loop(0, full // QB, block, 0)
            if t == 0 and h == heads - 1 and nz > 2:
                weights_step(1)
                done = 1
        for d in (1, 2, 3):
            send_heads(t, d).start()
    for t in range(trees):
        blocks_ref[q, t] = att_ref[t, pl.ds(pl.multiple_of(q * length, length), length)]

    def rest(s, carry):
        weights_step(s)

        @pl.when(s > 1)
        def _():
            pass_on(s - 1)

        return carry

    lax.fori_loop(done + 1, nz, rest, 0)
    pass_on(nz - 1)

    for t in range(trees):
        for d in (1, 2, 3):
            send_heads(t, d).wait()
    for cp in locals_[1:]:
        cp.wait()
    x_y.wait_send()
    t_y.wait_send()

    def drain(s, carry):
        for k in range(6):
            for way in (0, 1):
                cond, b = spread_send(way, s, z, nz)

                @pl.when(cond)
                def _():
                    zcopy(k, way, s, b, False).wait_send()

            def end(way, b):
                if k >= 4:
                    side_copy(k, b).wait_send()
                    core_copy(k, b, 1).wait()
                if k >= 3:
                    core_copy(k, b, 0).wait()

            each(s, end)
        return carry

    lax.fori_loop(1, nz, drain, 0)


def front(nz, x, seg, valid, par, wq, wk, wv, small, binner, mix, inn, out):
    trees, length, width = x.shape
    rz, wide = mix.shape[0], inn.shape[1]
    full = 4 * length
    n = width // 4
    vm = pl.BlockSpec(memory_space=pltpu.VMEM)
    anyspace = pl.BlockSpec(memory_space=pl.ANY)
    shape = jax.ShapeDtypeStruct
    return pl.pallas_call(
        functools.partial(front_body, nz),
        out_shape=(
            shape((trees, full, width), bf16),
            shape((nz, rz, 3 * n), bf16),
            shape((trees, full, 3 * n), bf16),
            shape((trees, full, 8), f32),
            shape((trees, full, 4 * HD), bf16),
            shape((4, trees, length, n), bf16),
            shape(small.shape, f32),
            shape(binner.shape, f32),
            shape((nz,) + mix.shape, bf16),
            shape((nz,) + inn.shape, bf16),
            shape((nz,) + out.shape, bf16),
        ),
        in_specs=[vm] * 3 + [pl.BlockSpec(memory_space=pltpu.SMEM)] + [vm] * 8,
        out_specs=[vm] * 8 + [anyspace] * 3,
        scratch_shapes=[
            pltpu.SMEM((trees, NSEG), jnp.int32),
            V((nz,) + small.shape, bf16),
            V((nz,) + binner.shape, bf16),
            V((4, 8, trees * length), jnp.int32),
            V((trees, full, n), bf16),
            DMA((4,)),
            DMA((6,)), DMA((6,)),
            DMA((6, 2, nz)), DMA((6, 2, nz)),
            DMA((2, nz)), DMA((2, nz)),
            DMA((3, 2, nz)), DMA((3, 2, nz)),
            DMA((trees, 3)), DMA((trees, 3)),
        ],
        compiler_params=pltpu.CompilerParams(
            collective_id=1, has_side_effects=True, vmem_limit_bytes=VMEM_LIMIT
        ),
        name="front",
    )(x, seg, valid, par, wq, wk, wv, small, binner, mix, inn, out)


def back_body(
    nz, inn, out, gb_ref, wmix_ref, blocks_ref, qkv_ref, lse_ref, feat_ref, xa, pw, vec_ref,
    o_inn, o_out, o_mix, o_qkv, o_ig, o_vec,
    gsend, gat, dq_ref, dk_ref, dv_ref, mix, ig,
    ci, co, cm, cg, xi, yo, yi, xo, yg, zi, zo, zm, zq, aq, xm, ym, xq, v_in, v_z, v_acc,
    hs, hr, cs, cr, s1, r1, s2, r2, zs, zr, gs, gr, vs, vr,
):
    p = Place(nz)
    z, c, y, x, q = p.z, p.c, p.y, p.x, p.q
    rz = inn.shape[1]
    wide = inn.shape[2]
    width = wmix_ref.shape[1]
    h2 = width // 2
    w2, w4, w8 = wide // 2, wide // 4, wide // 8
    trees, full = qkv_ref.shape[0], qkv_ref.shape[1]
    length = full // 4
    n = width // 4
    heads = n // HD
    cross = (x, z, 2 * (1 - y) + 1 - c)
    p.greet([cross])

    c_out = rcopy(out.at[:, :, lanes((1 - c) * h2, h2)], co, cs.at[4], cr.at[4], p.core)
    c_inn = rcopy(inn.at[:, :, lanes((1 - c) * w2, w2)], ci, cs.at[5], cr.at[5], p.core)
    c_out.start()
    c_inn.start()

    gb = gb_ref[...]
    for j in range(4):
        part = dot_nt(gb, wmix_ref[j * n : (j + 1) * n, :]).astype(bf16)
        for t in range(trees):
            gsend[j, t] = part[t * length : (t + 1) * length]

    def send_heads(d):
        to = lax.rem(q + d, 4)
        rows = pl.ds(pl.multiple_of(q * length, length), length)
        return rcopy(gsend.at[to], gat.at[:, rows], hs.at[d - 1], hr.at[d - 1], (x, z, to))

    for d in (1, 2, 3):
        send_heads(d).start()
    for t in range(trees):
        gat[t, pl.ds(pl.multiple_of(q * length, length), length)] = gsend[q, t]

    for j in range(4):
        mix[j * n : (j + 1) * n, :] = dot_tn(blocks_ref[j], gb).astype(bf16)
    c_mix = rcopy(mix.at[:, lanes((1 - c) * h2, h2)], cm, cs.at[3], cr.at[3], p.core)
    c_mix.start()

    c_out.wait()

    def out_sum(i, carry):
        for j in range(4):
            add_to(co.at[i, j * rz : (j + 1) * rz], out.at[i, j * rz : (j + 1) * rz, lanes(c * h2, h2)])
        return carry

    lax.fori_loop(0, nz, out_sum, 0)
    out_y = rcopy(co.at[:, rows_at((1 - y) * 2 * rz, 2 * rz)], yo, s1.at[1], r1.at[1], p.ynb)
    out_y.start()
    c_inn.wait()

    def inn_sum(i, carry):
        for j in range(4):
            add_to(ci.at[i, :, j * w8 : (j + 1) * w8], inn.at[i, :, lanes(c * w2 + j * w8, w8)])
        return carry

    lax.fori_loop(0, nz, inn_sum, 0)
    inn_x = rcopy(ci.at[:, :, lanes((1 - x) * w4, w4)], xi, s1.at[0], r1.at[0], p.xnb)
    inn_x.start()
    c_mix.wait()

    def mix_sum(i, carry):
        part = rows_at(i * rz, rz)
        add_to(cm.at[part], mix.at[part, lanes(c * h2, h2)])
        return carry

    lax.fori_loop(0, nz, mix_sum, 0)

    def chain(k, acc, buf):
        def copy(way, s, d):
            dev = p.right if way == 0 else p.left
            return rcopy(acc(d), buf(way, d), zs.at[k, way, s], zr.at[k, way, s], dev)

        def sending(way, s):
            if way == 0:
                d = z + nz - s
                return both(d <= nz - 1, z < nz - 1), d
            d = z - nz + s
            return both(d >= 0, z > 0), d

        def getting(way, s):
            if way == 0:
                d = z - 1 + nz - s
                return both(d <= nz - 1, z > 0), d
            d = z + 1 - nz + s
            return both(d >= 0, z < nz - 1), d

        def send(s):
            for way in (0, 1):
                ok, d = sending(way, s)

                @pl.when(ok)
                def _():
                    copy(way, s, d).start()

        def get(s):
            for way in (0, 1):
                ok, d = getting(way, s)

                @pl.when(ok)
                def _():
                    copy(way, s, d).wait_recv()
                    add_to(acc(d), buf(way, d))

        def drain(s, carry):
            for way in (0, 1):
                ok, d = sending(way, s)

                @pl.when(ok)
                def _():
                    copy(way, s, d).wait_send()

            return carry

        return send, get, lambda: lax.fori_loop(1, nz, drain, 0)

    mix_chain = chain(1, lambda d: cm.at[rows_at(d * rz, rz)], lambda way, d: zm.at[way, d])
    mix_chain[0](1)

    for d in (1, 2, 3):
        send_heads(d).wait()

    mix_at = 1
    for h in range(heads):
        cols = slice(h * HD, (h + 1) * HD)
        kcols = slice(n + h * HD, n + (h + 1) * HD)
        vcols = slice(2 * n + h * HD, 2 * n + (h + 1) * HD)
        for t in range(trees):
            key = qkv_ref[t, :, kcols]
            keys = keys_of(qkv_ref, feat_ref, t, h, n)
            values = qkv_ref[t, :, vcols]
            dk_ref[...] = jnp.zeros_like(dk_ref)
            dv_ref[...] = jnp.zeros_like(dv_ref)

            def block(i, carry):
                rows = pl.ds(pl.multiple_of(i * QB, QB), QB)
                s = dot_nt(queries_of(qkv_ref, feat_ref, t, rows, h), keys)
                probs = jnp.exp(s - lse_ref[t, rows, h : h + 1])
                grad = gat[t, rows, cols]
                dp = dot_nt(grad, values)
                inner = jnp.sum(probs * dp, axis=1, keepdims=True)
                ds = (probs * (dp - inner)).astype(bf16)
                dv_ref[...] += dot_tn(probs.astype(bf16), grad)
                dk_ref[...] += dot_tn(ds, qkv_ref[t, rows, cols])
                dq_ref[t, rows, cols] = (dot_nn(ds, key) * 0.125).astype(bf16)
                return carry

            lax.fori_loop(0, full // QB, block, 0)
            dq_ref[t, :, kcols] = (dk_ref[...] * 0.125).astype(bf16)
            dq_ref[t, :, vcols] = dv_ref[...].astype(bf16)
            if mix_at < nz - 1:
                mix_chain[1](mix_at)
                mix_at += 1
                mix_chain[0](mix_at)
    if nz > 1:

        def mix_rest(s, carry):
            mix_chain[1](s)
            mix_chain[0](s + 1)
            return carry

        lax.fori_loop(mix_at, nz - 1, mix_rest, 0)
        mix_chain[1](nz - 1)
    x_m = rcopy(cm.at[rows_at(z * rz, rz)], xm, gs.at[1], gr.at[1], p.xnb)
    x_m.start()

    inn_x.wait()

    def inn_sum2(i, carry):
        add_to(xi.at[i], ci.at[i, :, lanes(x * w4, w4)])
        return carry

    lax.fori_loop(0, nz, inn_sum2, 0)
    inn_y = rcopy(xi.at[:, :, lanes((1 - y) * w8, w8)], yi, s2.at[0], r2.at[0], p.ynb)
    inn_y.start()
    out_y.wait()

    def out_sum2(i, carry):
        add_to(yo.at[i], co.at[i, rows_at(y * 2 * rz, 2 * rz)])
        return carry

    lax.fori_loop(0, nz, out_sum2, 0)
    out_x = rcopy(yo.at[:, rows_at((1 - x) * rz, rz)], xo, s2.at[1], r2.at[1], p.xnb)
    out_x.start()

    w_heads = pw[...].reshape(width, 3 * n)
    grad_w = dot_tn(xa[0], dq_ref[0])
    for t in range(1, trees):
        grad_w = grad_w + dot_tn(xa[t], dq_ref[t])
    aq[...] = grad_w.astype(bf16).reshape(aq.shape)
    qkv_chain = chain(0, lambda d: aq.at[d], lambda way, d: zq.at[way, d])
    qkv_chain[0](1)

    for j in range(4):
        part = slice(j * length, (j + 1) * length)
        for t in range(trees):
            ig[j, t] = dot_nt(dq_ref[t, part], w_heads).astype(bf16)
    c_ig0 = rcopy(ig.at[1 - c], cg.at[0], cs.at[0], cr.at[0], p.core)
    c_ig1 = rcopy(ig.at[3 - c], cg.at[1], cs.at[1], cr.at[1], p.core)
    c_ig0.start()
    c_ig1.start()

    dbias = jnp.zeros((1, 3 * n), f32)
    for t in range(trees):
        dbias = dbias + jnp.sum(dq_ref[t].astype(f32), axis=0, keepdims=True)
    pad = jnp.zeros((1, width - n), f32)
    mine = jnp.concatenate(
        [
            jnp.concatenate([dbias[:, :n], pad], axis=1),
            jnp.concatenate([dbias[:, 2 * n :], pad], axis=1),
            jnp.zeros((6, width), f32),
        ],
        axis=0,
    )
    mine = pltpu.roll(mine, q * n, 1)
    v_acc[0:8] = vec_ref[0:8] + mine
    v_acc[8:16] = vec_ref[8:16]
    v_acc[2:3] = jnp.sum(gb.astype(f32), axis=0, keepdims=True)
    v_c = rcopy(v_acc, v_in.at[0], cs.at[2], cr.at[2], p.core)
    v_c.start()

    c_ig0.wait()
    c_ig1.wait()
    for b in range(2):
        add_to(cg.at[b], ig.at[2 * b + c])
    ig_y = rcopy(cg.at[1 - y], yg, s1.at[2], r1.at[2], p.ynb)
    ig_y.start()

    v_c.wait()
    v_acc[...] = v_acc[...] + v_in[0]
    v_x = rcopy(v_acc, v_in.at[1], vs.at[0], vr.at[0], p.xnb)
    v_x.start()

    def qkv_rest(s, carry):
        qkv_chain[1](s)
        qkv_chain[0](s + 1)
        return carry

    inn_y.wait()

    def inn_sum3(i, carry):
        add_to(yi.at[i], xi.at[i, :, lanes(y * w8, w8)])
        return carry

    lax.fori_loop(0, nz, inn_sum3, 0)
    out_x.wait()

    def out_sum3(i, carry):
        add_to(xo.at[i], yo.at[i, rows_at(x * rz, rz)])
        return carry

    lax.fori_loop(0, nz, out_sum3, 0)

    inn_chain = chain(2, lambda d: yi.at[d], lambda way, d: zi.at[way, d])
    out_chain = chain(3, lambda d: xo.at[d], lambda way, d: zo.at[way, d])
    inn_chain[0](1)
    out_chain[0](1)

    lax.fori_loop(1, nz - 1, qkv_rest, 0)
    v_x.wait()
    v_acc[...] = v_acc[...] + v_in[1]
    v_y = rcopy(v_acc, v_in.at[2], vs.at[1], vr.at[1], p.ynb)
    v_y.start()
    x_m.wait()
    add_to(xm, cm.at[rows_at(z * rz, rz)])
    y_m = rcopy(xm, ym, gs.at[4], gr.at[4], p.ynb)
    y_m.start()
    v_y.wait()
    v_acc[...] = v_acc[...] + v_in[2]
    v_z[z] = v_acc[...]

    qkv_chain[1](nz - 1)
    x_q = rcopy(aq.at[z], xq, gs.at[0], gr.at[0], p.xnb)
    x_q.start()

    def vcopy(way, s, b):
        dev = p.right if way == 0 else p.left
        return rcopy(v_z.at[b], v_z.at[b], zs.at[4, way, s], zr.at[4, way, s], dev)

    def last(s, carry):
        for way in (0, 1):
            ok, b = spread_send(way, s, z, nz)

            @pl.when(ok)
            def _():
                vcopy(way, s, b).start()

        inn_chain[1](s)
        out_chain[1](s)

        @pl.when(s < nz - 1)
        def _():
            inn_chain[0](s + 1)
            out_chain[0](s + 1)

        for way in (0, 1):
            ok, b = spread_get(way, s, z, nz)

            @pl.when(ok)
            def _():
                vcopy(way, s, b).wait_recv()

        return carry

    lax.fori_loop(1, nz, last, 0)

    def i_at(xx, yy):
        return o_inn.at[:, lanes(c * w2 + xx * w4 + yy * w8, w8)]

    def i_half(xx):
        return o_inn.at[:, lanes(c * w2 + xx * w4, w4)]

    def o_at(xx, yy):
        return o_out.at[rows_at((2 * yy + xx) * rz, rz), lanes(c * h2, h2)]

    def o_half(yy):
        return o_out.at[rows_at(2 * yy * rz, 2 * rz), lanes(c * h2, h2)]

    o_inn[:, lanes(c * w2 + x * w4 + y * w8, w8)] = yi[z]
    o_out[rows_at((2 * y + x) * rz, rz), lanes(c * h2, h2)] = xo[z]
    i_y = rcopy(i_at(x, y), i_at(x, y), gs.at[5], gr.at[5], p.ynb)
    o_x = rcopy(o_at(x, y), o_at(x, y), gs.at[6], gr.at[6], p.xnb)
    i_y.start()
    o_x.start()

    x_q.wait()
    o_qkv[q] = (aq[z].astype(f32) + xq[...].astype(f32)).astype(bf16)
    q_core = rcopy(o_qkv.at[q], o_qkv.at[q], gs.at[2], gr.at[2], p.core)
    q_y = rcopy(o_qkv.at[q], o_qkv.at[q], gs.at[3], gr.at[3], p.ynb)
    q_y.start()
    q_core.start()
    y_m.wait()
    o_mix[:, lanes(c * h2, h2)] = (xm[...].astype(f32) + ym[...].astype(f32)).astype(bf16)
    m_core = rcopy(
        o_mix.at[:, lanes(c * h2, h2)], o_mix.at[:, lanes(c * h2, h2)], gs.at[7], gr.at[7], p.core
    )
    m_core.start()

    ig_y.wait()
    o_ig[...] = (cg[y].astype(f32) + yg[...].astype(f32)).astype(o_ig.dtype)

    def v_sum(i, carry):
        return carry + v_z[i]

    o_vec[...] = lax.fori_loop(0, nz, v_sum, jnp.zeros(o_vec.shape, f32))

    i_y.wait()
    i_x = rcopy(i_half(x), i_half(x), gs.at[9], gr.at[9], p.xnb)
    i_x.start()
    o_x.wait()
    o_y = rcopy(o_half(y), o_half(y), gs.at[10], gr.at[10], p.ynb)
    o_y.start()
    q_y.wait()
    qy = 2 * (1 - y) + c
    q_on = rcopy(o_qkv.at[qy], o_qkv.at[qy], gs.at[8], gr.at[8], p.core)
    q_on.start()
    i_x.wait()
    i_all = o_inn.at[:, lanes(c * w2, w2)]
    i_core = rcopy(i_all, i_all, gs.at[11], gr.at[11], p.core)
    i_core.start()
    o_y.wait()
    o_all = o_out.at[:, lanes(c * h2, h2)]
    o_core = rcopy(o_all, o_all, gs.at[12], gr.at[12], p.core)
    o_core.start()
    for cp in (m_core, q_core, q_on, i_core, o_core):
        cp.wait()
    for ch in (qkv_chain, mix_chain, inn_chain, out_chain):
        ch[2]()

    def vdrain(s, carry):
        for way in (0, 1):
            ok, b = spread_send(way, s, z, nz)

            @pl.when(ok)
            def _():
                vcopy(way, s, b).wait_send()

        return carry

    lax.fori_loop(1, nz, vdrain, 0)


def back(nz, inn, out, gb, wmix, blocks, qkv, lse, feat, xa, pw, vec):
    rz, wide = inn.shape[1], inn.shape[2]
    width = wmix.shape[1]
    h, w2, w4, w8 = width // 2, wide // 2, wide // 4, wide // 8
    trees, full, n3 = qkv.shape
    length = full // 4
    n = n3 // 3
    vm = pl.BlockSpec(memory_space=pltpu.VMEM)
    shape = jax.ShapeDtypeStruct
    return pl.pallas_call(
        functools.partial(back_body, nz),
        out_shape=(
            shape((rz, wide), bf16),
            shape((4 * rz, width), bf16),
            shape((rz, width), bf16),
            shape((4, rz, n3), bf16),
            shape((trees, length, width), bf16),
            shape(vec.shape, f32),
        ),
        in_specs=[vm] * 11,
        out_specs=[vm] * 6,
        scratch_shapes=[
            V((4, trees, length, n), bf16),
            V((trees, full, n), bf16),
            V((trees, full, n3), bf16),
            V((full, HD), f32),
            V((full, HD), f32),
            V((width, width), bf16),
            V((4, trees, length, width), bf16),
            V((nz, rz, w2), bf16),
            V((nz, 4 * rz, h), bf16),
            V((width, h), bf16),
            V((2, trees, length, width), bf16),
            V((nz, rz, w4), bf16),
            V((nz, 2 * rz, h), bf16),
            V((nz, rz, w8), bf16),
            V((nz, rz, h), bf16),
            V((trees, length, width), bf16),
            V((2, nz, rz, w8), bf16),
            V((2, nz, rz, h), bf16),
            V((2, nz, rz, h), bf16),
            V((2, nz, rz, n3), bf16),
            V((nz, rz, n3), bf16),
            V((rz, h), bf16),
            V((rz, h), bf16),
            V((rz, n3), bf16),
            V((3,) + vec.shape, f32),
            V((nz,) + vec.shape, f32),
            V(vec.shape, f32),
            DMA((3,)), DMA((3,)),
            DMA((6,)), DMA((6,)),
            DMA((3,)), DMA((3,)),
            DMA((2,)), DMA((2,)),
            DMA((5, 2, nz)), DMA((5, 2, nz)),
            DMA((13,)), DMA((13,)),
            DMA((2,)), DMA((2,)),
        ],
        compiler_params=pltpu.CompilerParams(
            collective_id=2, has_side_effects=True, vmem_limit_bytes=VMEM_LIMIT
        ),
        name="back",
    )(inn, out, gb, wmix, blocks, qkv, lse, feat, xa, pw, vec)


def normed(resid):
    center = resid - jnp.mean(resid, axis=-1, keepdims=True)
    spread = jnp.mean(center * center, axis=-1, keepdims=True)
    inv = lax.rsqrt(spread + norm_eps)
    return center * inv, inv


def norm_back(grad_hat, hat, inv):
    mean = jnp.mean(grad_hat, axis=-1, keepdims=True)
    along = jnp.mean(grad_hat * hat, axis=-1, keepdims=True)
    return inv * (grad_hat - mean - hat * along)


def per_device(
    nz,
    tokens, teacher, seg_ids, parent_seg, valid,
    query_weight, query_bias, key_weight, value_weight, value_bias,
    mix_weight, mix_bias, first_gain, first_shift,
    inner_weight, inner_bias, outer_weight, outer_bias, second_gain, second_shift,
):
    trees, local_len, width = tokens.shape
    n_seq = lax.axis_size("seq")
    row_count = trees * local_len
    total_slots = row_count * lax.axis_size("replica") * nz * n_seq
    rz = mix_weight.shape[0]
    wide = inner_weight.shape[1]
    cols = width // n_seq

    small = jnp.stack(
        [query_bias, value_bias, mix_bias, first_gain, first_shift, outer_bias, second_gain, second_shift]
    )
    small = jnp.pad(small, ((0, 8), (0, width - rz)))
    binner = jnp.pad(inner_bias[None], ((0, 7), (0, wide - inner_bias.shape[0])))

    xa, pw, qkv, lse, feat, blocks, vecs, binner, mix_all, inn_all, out_all = front(
        nz, tokens, seg_ids, valid, parent_seg, query_weight, key_weight, value_weight,
        small, binner, mix_weight, inner_weight, outer_weight,
    )
    b_mix, g_first, s_first, b_outer, g_second, s_second = [vecs[i] for i in range(2, 8)]
    b_inner = binner[0]
    w_mix = mix_all.reshape(width, width)
    w_inner = inn_all.reshape(width, wide)
    w_outer = out_all.reshape(wide, width)

    attended = blocks.reshape(n_seq, row_count, cols).transpose(1, 0, 2).reshape(row_count, width)
    inputs = tokens.reshape(row_count, width)
    resid_one = inputs.astype(f32) + dot_nn(attended, w_mix) + b_mix
    hat_one, inv_one = normed(resid_one)
    first = hat_one * g_first + s_first
    first_low = first.astype(bf16)
    hidden_pre = dot_nn(first_low, w_inner) + b_inner
    cdf = 0.5 + 0.5 * lax.erf(hidden_pre * (0.5**0.5))
    slope = cdf + hidden_pre * jnp.exp(-0.5 * hidden_pre * hidden_pre) * 0.3989422804014327
    hidden = (hidden_pre * cdf).astype(bf16)
    resid_two = first + dot_nn(hidden, w_outer) + b_outer
    hat_two, inv_two = normed(resid_two)
    output = hat_two * g_second + s_second
    layer_out = output.astype(bf16).reshape(trees, local_len, width)
    error = output - teacher.reshape(row_count, width).astype(f32)
    row_weight = valid.astype(f32).reshape(row_count, 1)
    weighted = row_weight * error
    local_loss = jnp.sum(weighted * error)
    local_count = jnp.sum(row_weight)

    grad_out = 2.0 * weighted
    dsecond_gain = jnp.sum(grad_out * hat_two, axis=0)
    dsecond_shift = jnp.sum(grad_out, axis=0)
    grad_two = norm_back(grad_out * g_second, hat_two, inv_two)
    grad_ffn = grad_two.astype(bf16)
    douter_bias = jnp.sum(grad_ffn, axis=0, dtype=f32)
    douter_weight = dot_tn(hidden, grad_ffn).astype(bf16)
    grad_pre = (dot_nt(grad_ffn, w_outer) * slope).astype(bf16)
    dinner_bias = jnp.sum(grad_pre, axis=0, dtype=f32)
    dinner_weight = dot_tn(first_low, grad_pre).astype(bf16)
    grad_first = grad_two + dot_nt(grad_pre, w_inner)
    dfirst_gain = jnp.sum(grad_first * hat_one, axis=0)
    dfirst_shift = jnp.sum(grad_first, axis=0)
    grad_one = norm_back(grad_first * g_first, hat_one, inv_one)
    grad_branch = grad_one.astype(bf16)

    zero = jnp.zeros((width,), f32)
    scalars = jnp.concatenate([jnp.stack([local_loss, local_count]), jnp.zeros((width - 2,), f32)])
    vec = jnp.concatenate(
        [zero, zero, zero, dfirst_gain, dfirst_shift,
         douter_bias, dsecond_gain, dsecond_shift, dinner_bias, scalars]
    ).reshape(-1, width)
    vec = jnp.pad(vec, ((0, 16 - vec.shape[0]), (0, 0)))

    r_inn, r_out, r_mix, r_qkv, r_ig, r_vec = back(
        nz,
        dinner_weight.reshape(nz, rz, wide),
        douter_weight.reshape(nz, 4 * rz, width),
        grad_branch,
        w_mix,
        blocks.reshape(n_seq, row_count, cols),
        qkv, lse, feat, xa, pw, vec,
    )
    flat = r_vec.reshape(-1)
    spot = 8 * width + wide
    count = flat[spot + 1]
    scale = total_slots / count
    loss_value = flat[spot] / count
    shard = lax.axis_index("shard")

    def vec_out(i):
        return lax.dynamic_slice_in_dim(flat, i * width + shard * rz, rz, axis=0) * scale

    size = inner_bias.shape[0]
    dinner_bias = lax.dynamic_slice_in_dim(flat, 8 * width + shard * size, size, axis=0) * scale

    def full(w):
        return w.astype(f32) * scale

    def heads_out(i):
        part = r_qkv[:, :, i * cols : (i + 1) * cols].transpose(1, 0, 2).reshape(rz, width)
        return full(part)

    input_grad = (grad_one.reshape(trees, local_len, width) + r_ig.astype(f32)) * scale
    return (
        layer_out, loss_value, input_grad,
        heads_out(0), vec_out(0), heads_out(1), heads_out(2), vec_out(1),
        full(r_mix), vec_out(2), vec_out(3), vec_out(4),
        full(r_inn), dinner_bias, full(r_out), vec_out(5), vec_out(6), vec_out(7),
    )


def solution(mesh):
    rows = P(("replica", "shard"), "seq", None)
    line = P(("replica", "shard"), "seq")
    mat = P("shard", None)
    row = P("shard")
    placed = (
        rows, rows, line, P(("replica", "shard"), None), line,
        mat, row, mat, mat, row, mat, row, row, row, mat, row, mat, row, row, row,
    )
    return jax.shard_map(
        functools.partial(per_device, mesh.shape["shard"]),
        mesh=mesh,
        in_specs=placed,
        out_specs=(
            rows, P(), rows,
            mat, row, mat, mat, row, mat, row, row, row, mat, row, mat, row, row, row,
        ),
        check_vma=False,
    )
```

```python
import functools

import jax
import jax.numpy as jnp
from jax import lax
from jax.experimental import pallas as pl
from jax.experimental.pallas import tpu as pltpu
from jax.sharding import PartitionSpec as P

HEADS = 12
HD = 64
NSEG = 8
MESH = pl.DeviceIdType.MESH
BIG = 1e30
norm_eps = 1e-12
f32 = jnp.float32
bf16 = jnp.bfloat16
VMEM_LIMIT = 60 * 1024 * 1024


class Place:
    def __init__(self, nz):
        self.nz = nz
        self.x = lax.axis_index("replica")
        self.z = lax.axis_index("shard")
        self.q = lax.axis_index("seq")
        self.y = self.q // 2
        self.c = self.q % 2
        x, z, y, c = self.x, self.z, self.y, self.c
        self.core = (x, z, 2 * y + 1 - c)
        self.ynb = (x, z, 2 * (1 - y) + c)
        self.xnb = (1 - x, z, self.q)
        self.right = (x, z + 1, self.q)
        self.left = (x, z - 1, self.q)

    def greet(self, more):
        bar = pltpu.get_barrier_semaphore()
        for peer in [self.core, self.ynb, self.xnb] + more:
            pl.semaphore_signal(bar, inc=1, device_id=peer, device_id_type=MESH)

        @pl.when(self.z > 0)
        def _():
            pl.semaphore_signal(bar, inc=1, device_id=self.left, device_id_type=MESH)

        @pl.when(self.z < self.nz - 1)
        def _():
            pl.semaphore_signal(bar, inc=1, device_id=self.right, device_id_type=MESH)

        peers = 3 + len(more) + (self.z > 0).astype(jnp.int32) + (self.z < self.nz - 1).astype(jnp.int32)
        pl.semaphore_wait(bar, peers)


def rcopy(src, dst, ssem, rsem, dev):
    return pltpu.make_async_remote_copy(
        src_ref=src, dst_ref=dst, send_sem=ssem, recv_sem=rsem, device_id=dev, device_id_type=MESH
    )


def both(a, b):
    return jnp.logical_and(a, b)


def dot_nt(a, b):
    return lax.dot_general(a, b, (((1,), (1,)), ((), ())), preferred_element_type=f32)


def dot_tn(a, b):
    return lax.dot_general(a, b, (((0,), (0,)), ((), ())), preferred_element_type=f32)


def dot_nn(a, b):
    return jnp.dot(a, b, preferred_element_type=f32)


def add_to(dst, src):
    dst[...] = (dst[...].astype(f32) + src[...].astype(f32)).astype(dst.dtype)


def lanes(start, size):
    return pl.ds(pl.multiple_of(start, 128), size)


def rows_at(start, size):
    return pl.ds(pl.multiple_of(start, 8), size)


def row_mean(v):
    return jnp.sum(v, axis=1, keepdims=True) * (1.0 / v.shape[1])


def norm_back(grad_hat, hat, inv):
    return inv * (grad_hat - row_mean(grad_hat) - hat * row_mean(grad_hat * hat))


def fold(v):
    return jnp.sum(v.reshape(v.shape[0] // 8, 8, v.shape[1]), axis=0)


def total_row(v):
    return jnp.sum(v, axis=0, keepdims=True)


QB = 256
RB = 32
DMA = pltpu.SemaphoreType.DMA
V = pltpu.VMEM


def spread_send(way, s, z, nz):
    if way == 0:
        return both(z >= s - 1, z < nz - 1), z - s + 1
    return both(z <= nz - s, z > 0), z + s - 1


def spread_get(way, s, z, nz):
    if way == 0:
        return z >= s, z - s
    return z <= nz - 1 - s, z + s


def whole_body(
    nz, x_hbm, tea_hbm, seg_ref, valid_ref, par_ref, wq_hbm, wk_hbm, wv_hbm, sm_ref, bi_ref, mix_hbm, inn_hbm, out_hbm,
    y_hbm, one_hbm, xa_hbm, o_inn, o_out, o_mix, o_qkv, o_ig, o_vec,
    bits, hid, slp, mixa, inna, outa, pw, qkv, lse, feat, att, blocks, tok, A1, A2, A3, fl, gb, gp, tea, vm, inv1, mixg,
    gat, dk, dv, ci, co, cm, cg, xi, yo, yi, xo, yg, zi, zo, zm, zq, aq, xm, ym, xq, v_in, v_z, v_acc, sma, bia, tga,
    vecs, binner, loc, sav, rel, xs, xr, zs, zr, ys, yr, ns, nr, cs, cr, hs, hr,
    gs_, gr_, ks, kr, ds_, dr_, s1, r1, s2, r2, bs, br, es, er, vs, vr,
):
    p = Place(nz)
    z, c, y, x, q = p.z, p.c, p.y, p.x, p.q
    rz, width = mix_hbm.shape
    wide = inn_hbm.shape[1]
    trees, length = x_hbm.shape[0], x_hbm.shape[1]
    full = qkv.shape[1]
    count = trees * length
    n = width // 4
    heads = n // HD
    chunks = wide // width
    h2, w2, w4, w8 = width // 2, wide // 2, wide // 4, wide // 8
    cross = (x, z, 2 * (1 - y) + 1 - c)
    qy = 2 * (1 - y) + c
    o4 = 4 * rz

    load = [
        pltpu.make_async_copy(x_hbm, hid.at[:, q], loc.at[0]),
        pltpu.make_async_copy(wq_hbm, slp.at[0, pl.ds(0, rz)], loc.at[1]),
        pltpu.make_async_copy(wk_hbm, slp.at[0, pl.ds(256, rz)], loc.at[2]),
        pltpu.make_async_copy(wv_hbm, slp.at[0, pl.ds(512, rz)], loc.at[3]),
        pltpu.make_async_copy(mix_hbm, mixa.at[rows_at(z * rz, rz)], loc.at[4]),
        pltpu.make_async_copy(inn_hbm, inna.at[z], loc.at[5]),
        pltpu.make_async_copy(out_hbm, outa.at[rows_at(z * o4, o4)], loc.at[6]),
        pltpu.make_async_copy(tea_hbm, tea, loc.at[7]),
    ]
    for cp in load:
        cp.start()
    for t in range(trees):
        seg = seg_ref[t : t + 1, :]
        tga[q, 0:1, t * length : (t + 1) * length] = jnp.where(
            valid_ref[t : t + 1, :] == 1, seg, seg + NSEG
        )
    p.greet([cross])

    x_core = rcopy(hid.at[:, q], hid.at[:, q], xs.at[0], xr.at[0], p.core)
    x_y = rcopy(hid.at[:, q], hid.at[:, q], xs.at[1], xr.at[1], p.ynb)
    x_on = rcopy(hid.at[:, qy], hid.at[:, qy], xs.at[2], xr.at[2], p.core)
    t_core = rcopy(tga.at[q], tga.at[q], xs.at[3], xr.at[3], p.core)
    t_y = rcopy(tga.at[q], tga.at[q], xs.at[4], xr.at[4], p.ynb)
    t_on = rcopy(tga.at[qy], tga.at[qy], xs.at[5], xr.at[5], p.core)
    t_y.start()
    t_core.start()
    load[0].wait()
    x_y.start()
    x_core.start()

    back = lax.rem(width - q * n, width)
    for i in range(3):
        load[1 + i].wait()
        turned = pltpu.roll(slp[0, i * 256 : i * 256 + rz].astype(f32), back, 1)
        for h in range(heads):
            pw[z, :, (3 * h + i) * HD : (3 * h + i + 1) * HD] = turned[:, h * HD : (h + 1) * HD].astype(bf16)
    sma[z] = pltpu.roll(sm_ref[...], z * rz, 1).astype(bf16)
    bia[z] = pltpu.roll(bi_ref[...], z * (wide // nz), 1).astype(bf16)

    def at_row(ref, b, size):
        return ref.at[rows_at(b * size, size)]

    there = {
        0: lambda b: pw.at[b],
        1: lambda b: sma.at[b],
        2: lambda b: bia.at[b],
        3: lambda b: mixa.at[rows_at(b * rz, rz), lanes(c * h2, h2)],
        4: lambda b: inna.at[b, :, lanes(c * w2 + x * w4, w4)],
        5: lambda b: outa.at[rows_at(b * o4 + (2 * x + y) * rz, rz), lanes(c * h2, h2)],
    }

    def zcopy(k, way, s, b):
        dev = p.right if way == 0 else p.left
        return rcopy(there[k](b), there[k](b), zs.at[k, way, s], zr.at[k, way, s], dev)

    def start_step(k, s):
        for way in (0, 1):
            cond, b = spread_send(way, s, z, nz)

            @pl.when(both(cond, s <= nz - 1))
            def _():
                zcopy(k, way, s, b).start()

    def each(s, fn):
        for way in (0, 1):
            cond, b = spread_get(way, s, z, nz)

            @pl.when(cond)
            def _():
                fn(way, b)

    def take(k, s):
        each(s, lambda way, b: zcopy(k, way, s, b).wait_recv())

    def inn_half_of(b, xx):
        return inna.at[b, :, lanes(c * w2 + xx * w4, w4)]

    def out_half_of(b, xx):
        return outa.at[rows_at(b * o4 + 2 * xx * rz, 2 * rz), lanes(c * h2, h2)]

    def y_copy(b):
        return rcopy(there[5](b), there[5](b), ys.at[b], yr.at[b], p.ynb)

    def x_copy(k, b):
        piece = inn_half_of(b, x) if k == 0 else out_half_of(b, x)
        return rcopy(piece, piece, ns.at[k, b], nr.at[k, b], p.xnb)

    def core_copy(k, b, part):
        if k == 2:
            piece = there[3](b)
        else:
            xx = x if part == 0 else 1 - x
            piece = inn_half_of(b, xx) if k == 0 else out_half_of(b, xx)
        return rcopy(piece, piece, cs.at[k, part, b], cr.at[k, part, b], p.core)

    for k in (0, 1, 2):
        start_step(k, 1)

    def small_step(s, carry):
        for k in (0, 1, 2):
            take(k, s)
        for k in (0, 1, 2):
            start_step(k, s + 1)
        return carry

    lax.fori_loop(1, nz - 1, small_step, 0)
    for i in (4, 5, 6, 7):
        load[i].wait()
    for k in (3, 4, 5):
        start_step(k, 1)
    for k in (0, 1, 2):
        take(k, nz - 1)

    def mix_step(s):
        def got(way, b):
            zcopy(3, way, s, b).wait_recv()
            core_copy(2, b, 0).start()

        each(s, got)
        start_step(3, s + 1)

    def inn_step(s):
        def got(way, b):
            zcopy(4, way, s, b).wait_recv()
            x_copy(0, b).start()
            core_copy(0, b, 0).start()

        each(s, got)
        start_step(4, s + 1)

    def out_step(s):
        def got(way, b):
            zcopy(5, way, s, b).wait_recv()
            y_copy(b).start()

        each(s, got)
        start_step(5, s + 1)

    def out_from_y(s):
        def got(way, b):
            y_copy(b).wait_recv()
            x_copy(1, b).start()
            core_copy(1, b, 0).start()

        each(s, got)

    def from_x(k, s):
        def got(way, b):
            x_copy(k, b).wait_recv()
            core_copy(k, b, 1).start()

        each(s, got)

    def from_core(k, s):
        def got(way, b):
            core_copy(k, b, 0).wait_recv()
            if k < 2:
                core_copy(k, b, 1).wait_recv()

        each(s, got)

    def all_steps(*fns):
        def one(s, carry):
            for fn in fns:
                fn(s)
            return carry

        lax.fori_loop(1, nz, one, 0)

    placed = nz == 4

    def vsum(i, carry):
        return carry[0] + sma[i].astype(f32), carry[1] + bia[i].astype(f32)

    small, inner_bias = lax.fori_loop(0, nz, vsum, (jnp.zeros(vecs.shape, f32), jnp.zeros(binner.shape, f32)))
    vecs[...] = small
    binner[...] = inner_bias
    turned = pltpu.roll(small, back, 1)
    bias = []
    for h in range(heads):
        cols = slice(h * HD, (h + 1) * HD)
        bias += [turned[0:1, cols], jnp.zeros((1, HD), f32), turned[1:2, cols]]
    bias = jnp.concatenate(bias, axis=1)

    t_y.wait_recv()
    t_on.start()
    x_y.wait_recv()
    x_on.start()
    t_core.wait()
    x_core.wait()
    t_on.wait()

    row = lax.broadcasted_iota(jnp.int32, (16, 4 * HD), 0)
    lane = lax.broadcasted_iota(jnp.int32, (16, 4 * HD), 1)
    trow = lax.broadcasted_iota(jnp.int32, (16, full), 0)
    vrow = lax.broadcasted_iota(jnp.int32, (16, length), 0)
    ones = jnp.ones((16, 128), bf16)
    for t in range(trees):
        bits[t, 0] = jnp.int32(1)
        for s in range(1, NSEG):
            bits[t, s] = bits[t, par_ref[t, s]] + (1 << s)
        seen = jnp.zeros((16, 4 * HD), jnp.int32)
        for a in range(NSEG):
            seen = jnp.where(row == a, bits[t, a], seen)
        at = jnp.clip(lane - HD, 0, NSEG)
        unseen = ((seen >> at) & 1) == 0
        q_side = both(both(row < NSEG, both(lane >= HD, lane <= HD + NSEG)), unseen)
        k_side = both(row <= NSEG, lane == row + 3 * HD)
        table = jnp.where(q_side, -BIG, jnp.where(k_side, 1.0, 0.0)).astype(bf16)
        tag = jnp.concatenate(
            [tga[j, 0:1, t * length : (t + 1) * length] for j in range(full // length)], axis=1
        )
        gone = tag >= NSEG
        seg = jnp.where(gone, tag - NSEG, tag)
        seg = jnp.broadcast_to(seg, (16, full))
        gone = jnp.broadcast_to(jnp.where(gone, 1, 0), (16, full))
        hot = jnp.where(trow == NSEG, gone, jnp.where(trow == seg, 1, 0)).astype(f32).astype(bf16)
        feat[t] = dot_tn(hot, table).astype(bf16)
        here = jnp.broadcast_to(valid_ref[t : t + 1, :], (16, length))
        here = jnp.where(vrow == 0, here, 0).astype(f32).astype(bf16)
        vm[t * length : (t + 1) * length] = dot_tn(here, ones)

    x_on.wait()
    x_y.wait_send()
    t_y.wait_send()
    saves = [
        pltpu.make_async_copy(hid.at[t, j], xa_hbm.at[pl.ds((t * 4 + j) * length, length)], sav.at[t, j])
        for t in range(trees)
        for j in range(4)
    ]
    for cp in saves:
        cp.start()
    w_heads = pw[...].reshape(width, 3 * n)
    for t in range(trees):
        qkv[t] = (dot_nn(hid[t].reshape(full, width), w_heads) + bias).astype(bf16)

    if placed:
        mix_step(1)
        inn_step(1)

    def part(h, i):
        return slice((3 * h + i) * HD, (3 * h + i + 1) * HD)

    def queries_of(t, rows, h):
        return jnp.concatenate([qkv[t, rows, part(h, 0)] * 0.125, feat[t, rows, HD : 2 * HD]], axis=1)

    def keys_of(t, h):
        return jnp.concatenate([qkv[t, :, part(h, 1)], feat[t, :, 3 * HD : 4 * HD]], axis=1)

    def token_rows(j):
        return pl.ds(pl.multiple_of(j * length, length), length)

    def send_heads(t, d):
        to = lax.rem(q + d, 4)
        return rcopy(
            att.at[t, token_rows(to)], blocks.at[q, t], hs.at[t, d - 1], hr.at[t, d - 1], (x, z, to)
        )

    events = [
        [lambda: out_step(1)],
        [],
        [lambda: mix_step(2)],
        [lambda: from_x(0, 1), lambda: out_from_y(1)],
        [],
        [lambda: inn_step(2)],
    ]
    for t in range(trees):
        for h in range(heads):
            keys = keys_of(t, h)
            values = qkv[t, :, part(h, 2)]

            def block(i, carry):
                rows = pl.ds(pl.multiple_of(i * QB, QB), QB)
                s = dot_nt(queries_of(t, rows, h), keys)
                peak = jnp.max(s, axis=1, keepdims=True)
                e = jnp.exp(s - peak)
                total = jnp.sum(e, axis=1, keepdims=True)
                o = dot_nn(e.astype(bf16), values) / total
                att[t, rows, h * HD : (h + 1) * HD] = o.astype(bf16)
                lse[t, rows, h : h + 1] = peak + jnp.log(total)
                return carry

            lax.fori_loop(0, full // QB, block, 0)
            if placed:
                for fn in events.pop(0):
                    fn()
        for d in (1, 2, 3):
            send_heads(t, d).start()
    for t in range(trees):
        blocks[q, t] = att[t, token_rows(q)]
    if placed:
        out_step(2)
        mix_step(3)
    else:
        all_steps(mix_step)
    for t in range(trees):
        for d in (1, 2, 3):
            send_heads(t, d).wait()
    if placed:
        from_x(1, 1)

    for j in range(4):
        tok[:, j * n : (j + 1) * n] = blocks[j].reshape(count, n)
    all_steps(functools.partial(from_core, 2))
    A3[...] = dot_nn(tok[...], mixa[...])
    if placed:
        out_from_y(2)
        from_x(0, 2)
        inn_step(3)

    def rows_of(i):
        return pl.ds(pl.multiple_of(i * RB, RB), RB)

    per = length // RB

    def first_norm(i, carry):
        rows = rows_of(i)
        own = hid[i // per, q, rows_of(i % per)].astype(f32)
        r1 = own + A3[rows] + vecs[2:3]
        center = r1 - row_mean(r1)
        inv = lax.rsqrt(row_mean(center * center) + norm_eps)
        hat = center * inv
        A1[rows] = hat
        inv1[rows] = jnp.broadcast_to(inv, (RB, 128))
        fl[rows] = (hat * vecs[3:4] + vecs[4:5]).astype(bf16)
        return carry

    lax.fori_loop(0, count // RB, first_norm, 0)
    for cp in saves:
        cp.wait()
    if placed:
        out_step(3)
        from_x(1, 2)
        from_x(0, 3)
    else:
        all_steps(inn_step, functools.partial(from_x, 0), out_step, out_from_y, functools.partial(from_x, 1))
    all_steps(functools.partial(from_core, 0))

    def inner_chunk(j):
        return inna[:, :, j * width : (j + 1) * width].reshape(width, width)

    def hid_chunk(j):
        return hid[j // 2, 2 * (j % 2) : 2 * (j % 2) + 2].reshape(count, width)

    for j in range(chunks):
        A3[...] = dot_nn(fl[...], inner_chunk(j))

        def gelu(i, carry):
            rows = rows_of(i)
            pre = A3[rows] + binner[0:1, j * width : (j + 1) * width]
            cdf = 0.5 + 0.5 * lax.erf(pre * (0.5**0.5))
            hid[j // 2, 2 * (j % 2) + i // per, rows_of(i % per)] = (pre * cdf).astype(bf16)
            slope = cdf + pre * jnp.exp(-0.5 * pre * pre) * 0.3989422804014327
            slp[j // 2, pl.ds(pl.multiple_of((j % 2) * count + i * RB, RB), RB)] = slope.astype(bf16)
            return carry

        lax.fori_loop(0, count // RB, gelu, 0)
        if placed and j == 0:
            out_from_y(3)
        if placed and j == 2:
            from_x(1, 3)
    all_steps(functools.partial(from_core, 1))
    for j in range(chunks):
        more = dot_nn(hid_chunk(j), outa[j * width : (j + 1) * width])
        if j == 0:
            A2[...] = more
        else:
            A2[...] += more

    def drain(s, carry):
        for k in range(6):
            for way in (0, 1):
                cond, b = spread_send(way, s, z, nz)

                @pl.when(cond)
                def _():
                    zcopy(k, way, s, b).wait_send()

        def end(way, b):
            y_copy(b).wait_send()
            core_copy(2, b, 0).wait_send()
            for k in (0, 1):
                x_copy(k, b).wait_send()
                core_copy(k, b, 0).wait_send()
                core_copy(k, b, 1).wait_send()

        each(s, end)
        return carry

    lax.fori_loop(1, nz, drain, 0)

    zero = jnp.zeros((8, width), f32)

    def second_norm(i, carry):
        loss, dgain, dshift, dbias = carry
        rows = rows_of(i)
        first = A1[rows] * vecs[3:4] + vecs[4:5]
        r2 = first + A2[rows] + vecs[5:6]
        center = r2 - row_mean(r2)
        inv = lax.rsqrt(row_mean(center * center) + norm_eps)
        hat = center * inv
        out = hat * vecs[6:7] + vecs[7:8]
        err = out - tea[rows].astype(f32)
        tea[rows] = out.astype(bf16)
        weighted = vm[rows, 0:1] * err
        grad = 2.0 * weighted
        g2 = norm_back(grad * vecs[6:7], hat, inv)
        A2[rows] = g2
        low = g2.astype(bf16)
        gb[rows] = low
        return (
            loss + fold(weighted * err),
            dgain + fold(grad * hat),
            dshift + fold(grad),
            dbias + fold(low.astype(f32)),
        )

    loss, dgain, dshift, dbias = lax.fori_loop(0, count // RB, second_norm, (zero, zero, zero, zero))
    put_y = pltpu.make_async_copy(tea, y_hbm, loc.at[0])
    put_y.start()
    v_acc[...] = jnp.zeros_like(v_acc)
    spot = 8 + chunks
    v_acc[5:6] = total_row(dbias)
    v_acc[6:7] = total_row(dgain)
    v_acc[7:8] = total_row(dshift)
    v_acc[spot : spot + 1] = total_row(loss)
    v_acc[spot + 1 : spot + 2, 0:128] = total_row(vm[...])

    def c_out(d):
        return rcopy(outa.at[rows_at(d * o4, o4), lanes((1 - c) * h2, h2)], co.at[d], ds_.at[0, d], dr_.at[0, d], p.core)

    def c_inn(k):
        src = inna.at[:, :, lanes(((1 - c) * 2 + k) * width, width)]
        return rcopy(src, ci.at[:, :, pl.ds(k * width, width)], ds_.at[1, k], dr_.at[1, k], p.core)

    def out_y(d):
        src = co.at[d, rows_at((1 - y) * 2 * rz, 2 * rz)]
        return rcopy(src, yo.at[d], s1.at[0, d], r1.at[0, d], p.ynb)

    def inn_x(d):
        return rcopy(ci.at[d, :, lanes((1 - x) * w4, w4)], xi.at[d], s1.at[1, d], r1.at[1, d], p.xnb)

    def out_x(d):
        src = yo.at[d, rows_at((1 - x) * rz, rz)]
        return rcopy(src, xo.at[d], s2.at[0, d], r2.at[0, d], p.xnb)

    def inn_y(d):
        return rcopy(xi.at[d, :, lanes((1 - y) * w8, w8)], yi.at[d], s2.at[1, d], r2.at[1, d], p.ynb)

    def span(lo, hi, fn):
        if hi - lo == 1:
            fn(lo)
            return

        def one(i, carry):
            fn(i)
            return carry

        lax.fori_loop(lo, hi, one, 0)

    def of_chunk(j, fn):
        span(j * nz // chunks, (j + 1) * nz // chunks, fn)

    def group(g, fn):
        def pair(i):
            fn(nz - 1 - i)
            fn(i)

        span(g * nz // 4, (g + 1) * nz // 4, pair)

    def out_chip(d):
        c_out(d).wait()
        for j in range(4):
            add_to(co.at[d, j * rz : (j + 1) * rz], outa.at[rows_at(d * o4 + j * rz, rz), lanes(c * h2, h2)])
        out_y(d).start()

    def inn_chip(k):
        c_inn(k).wait()

        def one(d):
            for j in range(2):
                spot = slice(k * width + j * h2, k * width + (j + 1) * h2)
                add_to(ci.at[d, :, spot], inna.at[d, :, lanes(c * w2 + k * width + j * h2, h2)])

        group(0, one)
        group(1, one)

    def out_half(d):
        out_y(d).wait()
        add_to(yo.at[d, :rz], co.at[d, rows_at(y * 2 * rz, rz)])
        add_to(yo.at[d, rz:], co.at[d, rows_at(y * 2 * rz + rz, rz)])
        out_x(d).start()

    def inn_half(d):
        inn_x(d).wait()
        add_to(xi.at[d, :, :w8], ci.at[d, :, lanes(x * w4, w8)])
        add_to(xi.at[d, :, w8:], ci.at[d, :, lanes(x * w4 + w8, w8)])
        inn_y(d).start()

    def out_quarter(d):
        out_x(d).wait()
        add_to(xo.at[d], yo.at[d, rows_at(x * rz, rz)])

    def inn_quarter(d):
        inn_y(d).wait()
        add_to(yi.at[d], xi.at[d, :, lanes(y * w8, w8)])

    order = [chunks - 1, 0] + list(range(chunks - 2, 0, -1))
    for step, j in enumerate(order):
        A3[...] = dot_nt(gb[...], outa[j * width : (j + 1) * width])

        def slopes(i, carry):
            rows = rows_of(i)
            slope = slp[j // 2, pl.ds(pl.multiple_of((j % 2) * count + i * RB, RB), RB)]
            low = (A3[rows] * slope.astype(f32)).astype(bf16)
            gp[rows] = low
            return carry + fold(low.astype(f32))

        v_acc[8 + j : 9 + j] = total_row(lax.fori_loop(0, count // RB, slopes, zero))
        outa[j * width : (j + 1) * width] = dot_tn(hid_chunk(j), gb[...]).astype(bf16)
        of_chunk(j, lambda d: c_out(d).start())
        A2[...] += dot_nt(gp[...], inner_chunk(j))
        inna[:, :, j * width : (j + 1) * width] = dot_tn(fl[...], gp[...]).astype(bf16).reshape(nz, rz, width)

        @pl.when(c == 1 - j // 2)
        def _():
            c_inn(j % 2).start()

        if step > 0:
            of_chunk(order[step - 1], out_chip)

    def first_back(i, carry):
        dgain, dshift, dbias = carry
        rows = rows_of(i)
        grad = A2[rows]
        hat = A1[rows]
        g1 = norm_back(grad * vecs[3:4], hat, inv1[rows, 0:1])
        A2[rows] = g1
        low = g1.astype(bf16)
        gb[rows] = low
        return dgain + fold(grad * hat), dshift + fold(grad), dbias + fold(low.astype(f32))

    dgain, dshift, dbias = lax.fori_loop(0, count // RB, first_back, (zero, zero, zero))
    v_acc[2:3] = total_row(dbias)
    v_acc[3:4] = total_row(dgain)
    v_acc[4:5] = total_row(dshift)
    put_one = pltpu.make_async_copy(A2, one_hbm, loc.at[1])
    put_one.start()

    for j in range(4):
        part_j = dot_nt(gb[...], mixa[j * n : (j + 1) * n]).astype(bf16)
        for t in range(trees):
            att[t, j * length : (j + 1) * length] = part_j[t * length : (t + 1) * length]

    def send_grads(d):
        to = lax.rem(q + d, 4)
        return rcopy(att.at[:, token_rows(to)], gat.at[:, token_rows(q)], gs_.at[d - 1], gr_.at[d - 1], (x, z, to))

    for d in (1, 2, 3):
        send_grads(d).start()
    for t in range(trees):
        gat[t, token_rows(q)] = att[t, token_rows(q)]

    for k in (0, 1):
        inn_chip(k)
    for g in (0, 1):
        group(g, lambda d: inn_x(d).start())
    of_chunk(order[-1], out_chip)
    reload = [
        pltpu.make_async_copy(
            xa_hbm.at[pl.ds(i * length, length)], outa.at[pl.ds(i * length, length)], rel.at[i]
        )
        for i in range(trees * 4)
    ]
    for cp in reload:
        cp.start()
    mixg[...] = dot_tn(tok[...], gb[...]).astype(bf16)
    c_mix = rcopy(mixg.at[:, lanes((1 - c) * h2, h2)], cm, ks.at[3], kr.at[3], p.core)
    c_mix.start()

    def chain(k, acc, buf):
        def copy(way, s, d):
            dev = p.right if way == 0 else p.left
            return rcopy(acc(d), buf(way, d), bs.at[k, way, s], br.at[k, way, s], dev)

        def sending(way, s):
            if way == 0:
                d = z + nz - s
                return both(d <= nz - 1, z < nz - 1), d
            d = z - nz + s
            return both(d >= 0, z > 0), d

        def getting(way, s):
            if way == 0:
                d = z - 1 + nz - s
                return both(d <= nz - 1, z > 0), d
            d = z + 1 - nz + s
            return both(d >= 0, z < nz - 1), d

        def send(s):
            for way in (0, 1):
                ok, d = sending(way, s)

                @pl.when(both(ok, s <= nz - 1))
                def _():
                    copy(way, s, d).start()

        def get(s):
            for way in (0, 1):
                ok, d = getting(way, s)

                @pl.when(ok)
                def _():
                    copy(way, s, d).wait_recv()
                    add_to(acc(d), buf(way, d))

        def drain(s, carry):
            for way in (0, 1):
                ok, d = sending(way, s)

                @pl.when(ok)
                def _():
                    copy(way, s, d).wait_send()

            return carry

        return send, get, lambda: lax.fori_loop(1, nz, drain, 0)

    def step_of(ch, s):
        ch[1](s)
        ch[0](s + 1)

    mix_chain = chain(3, lambda d: cm.at[rows_at(d * rz, rz)], lambda way, d: zm.at[way, d])
    inn_chain = chain(4, lambda d: yi.at[d], lambda way, d: zi.at[way, d])
    out_chain = chain(5, lambda d: xo.at[d], lambda way, d: zo.at[way, d])

    def head_chain(h):
        return chain(h, lambda d: aq.at[h, d], lambda way, d: zq.at[h, way, d])

    qkv_chains = [head_chain(h) for h in range(heads)]

    c_mix.wait()

    def mix_sum(i, carry):
        block = rows_at(i * rz, rz)
        add_to(cm.at[block], mixg.at[block, lanes(c * h2, h2)])
        return carry

    lax.fori_loop(0, nz, mix_sum, 0)
    mix_chain[0](1)
    for d in (1, 2, 3):
        send_grads(d).wait()

    def head_weights(h):
        cols = slice(3 * h * HD, 3 * (h + 1) * HD)
        grad = dot_tn(outa[0:full], slp[0, :, cols])
        for t in range(1, trees):
            grad = grad + dot_tn(outa[t * full : (t + 1) * full], slp[t, :, cols])
        aq[h] = grad.astype(bf16).reshape(nz, rz, 3 * HD)
        qkv_chains[h][0](1)

    def q_x(h):
        return rcopy(aq.at[h, z], xq.at[h], es.at[13 + h], er.at[13 + h], p.xnb)

    def q_y(h):
        return rcopy(o_qkv.at[h, q], o_qkv.at[h, q], es.at[16 + h], er.at[16 + h], p.ynb)

    def q_core(h):
        return rcopy(o_qkv.at[h, q], o_qkv.at[h, q], es.at[19 + h], er.at[19 + h], p.core)

    def q_on(h):
        return rcopy(o_qkv.at[h, qy], o_qkv.at[h, qy], es.at[22 + h], er.at[22 + h], p.core)

    def q_sum(h):
        q_x(h).wait()
        o_qkv[h, q] = (aq[h, z].astype(f32) + xq[h].astype(f32)).astype(bf16)
        q_y(h).start()
        q_core(h).start()

    x_m = rcopy(cm.at[rows_at(z * rz, rz)], xm, es.at[1], er.at[1], p.xnb)
    y_m = rcopy(xm, ym, es.at[4], er.at[4], p.ynb)

    def big_step(s):
        step_of(inn_chain, s)
        step_of(out_chain, s)

    def first_big():
        inn_chain[0](1)
        out_chain[0](1)

    if placed:
        events = [
            [lambda: step_of(mix_chain, 1), lambda: group(0, inn_half)],
            [lambda: step_of(mix_chain, 2), lambda: group(0, out_half), lambda: head_weights(0)],
            [lambda: group(1, inn_half), lambda: group(1, out_half), lambda: step_of(mix_chain, 3), x_m.start],
            [
                lambda: group(0, inn_quarter), lambda: group(0, out_quarter), first_big,
                lambda: step_of(qkv_chains[0], 1), lambda: head_weights(1),
            ],
            [
                lambda: group(1, inn_quarter), lambda: group(1, out_quarter),
                lambda: step_of(qkv_chains[0], 2), lambda: big_step(1), lambda: step_of(qkv_chains[1], 1),
            ],
            [
                lambda: step_of(qkv_chains[0], 3), lambda: q_x(0).start(),
                lambda: big_step(2), lambda: step_of(qkv_chains[1], 2), lambda: head_weights(2),
            ],
        ]
    else:
        events = [[], [], [], [], [], []]
    for cp in reload:
        cp.wait()
    put_one.wait()
    for h in range(heads):
        for t in range(trees):
            key = qkv[t, :, part(h, 1)]
            keys = keys_of(t, h)
            values = qkv[t, :, part(h, 2)]
            dk[...] = jnp.zeros_like(dk)
            dv[...] = jnp.zeros_like(dv)

            def block(i, carry):
                rows = pl.ds(pl.multiple_of(i * QB, QB), QB)
                s = dot_nt(queries_of(t, rows, h), keys)
                probs = jnp.exp(s - lse[t, rows, h : h + 1])
                grad = gat[t, rows, h * HD : (h + 1) * HD]
                dp = dot_nt(grad, values)
                inner = jnp.sum(probs * dp, axis=1, keepdims=True)
                ds = (probs * (dp - inner)).astype(bf16)
                dv[...] += dot_tn(probs.astype(bf16), grad)
                dk[...] += dot_tn(ds, qkv[t, rows, part(h, 0)])
                slp[t, rows, part(h, 0)] = (dot_nn(ds, key) * 0.125).astype(bf16)
                return carry

            lax.fori_loop(0, full // QB, block, 0)
            slp[t, :, part(h, 1)] = (dk[...] * 0.125).astype(bf16)
            slp[t, :, part(h, 2)] = dv[...].astype(bf16)
            for fn in events.pop(0):
                fn()
    if not placed:

        def slow_mix(s):
            step_of(mix_chain, s)

        def slow_big(s):
            big_step(s)
            for h in range(heads):
                step_of(qkv_chains[h], s)

        all_steps(slow_mix)
        x_m.start()
        for g in (0, 1):
            group(g, inn_half)
            group(g, out_half)
        for g in (0, 1):
            group(g, inn_quarter)
            group(g, out_quarter)
        first_big()
        for h in range(heads):
            head_weights(h)
        all_steps(slow_big)
        q_x(0).start()

    for j in range(4):
        for t in range(trees):
            hid[t, j] = dot_nt(slp[t, j * length : (j + 1) * length, : 3 * n], w_heads_of(pw, width)).astype(bf16)
    c_ig0 = rcopy(hid.at[:, 1 - c], cg.at[0], ks.at[0], kr.at[0], p.core)
    c_ig1 = rcopy(hid.at[:, 3 - c], cg.at[1], ks.at[1], kr.at[1], p.core)
    c_ig0.start()
    c_ig1.start()

    dbias = jnp.zeros((1, 3 * n), f32)
    for t in range(trees):
        dbias = dbias + jnp.sum(slp[t, :, : 3 * n].astype(f32), axis=0, keepdims=True)
    gap = jnp.zeros((1, width - n), f32)
    mine = [
        jnp.concatenate([dbias[:, part(h, i)] for h in range(heads)] + [gap], axis=1) for i in (0, 2)
    ]
    mine = pltpu.roll(jnp.concatenate(mine + [jnp.zeros((6, width), f32)], axis=0), q * n, 1)
    v_acc[0:8] = v_acc[0:8] + mine
    v_c = rcopy(v_acc, v_in.at[0], ks.at[2], kr.at[2], p.core)
    v_c.start()

    c_ig0.wait()
    c_ig1.wait()
    for b in range(2):
        add_to(cg.at[b], hid.at[:, 2 * b + c])
    ig_y = rcopy(cg.at[1 - y], yg, ks.at[4], kr.at[4], p.ynb)
    ig_y.start()

    v_c.wait()
    v_acc[...] = v_acc[...] + v_in[0]
    v_x = rcopy(v_acc, v_in.at[1], vs.at[0], vr.at[0], p.xnb)
    v_x.start()

    x_m.wait()
    add_to(xm, cm.at[rows_at(z * rz, rz)])
    y_m.start()

    def i_at(xx, yy):
        return o_inn.at[:, lanes(c * w2 + xx * w4 + yy * w8, w8)]

    def i_half(xx):
        return o_inn.at[:, lanes(c * w2 + xx * w4, w4)]

    def o_at(xx, yy):
        return o_out.at[rows_at((2 * yy + xx) * rz, rz), lanes(c * h2, h2)]

    def o_half(yy):
        return o_out.at[rows_at(2 * yy * rz, 2 * rz), lanes(c * h2, h2)]

    if placed:
        big_step(3)
    own_i = pltpu.make_async_copy(yi.at[z], i_at(x, y), loc.at[2])
    own_o = pltpu.make_async_copy(xo.at[z], o_at(x, y), loc.at[3])
    own_i.start()
    own_o.start()
    i_y = rcopy(yi.at[z], i_at(x, y), es.at[5], er.at[5], p.ynb)
    o_x = rcopy(xo.at[z], o_at(x, y), es.at[6], er.at[6], p.xnb)
    i_y.start()
    o_x.start()
    if placed:
        step_of(qkv_chains[1], 3)
        q_x(1).start()
        step_of(qkv_chains[2], 1)
    else:
        q_x(1).start()
    q_sum(0)
    v_x.wait()
    v_acc[...] = v_acc[...] + v_in[1]
    v_y = rcopy(v_acc, v_in.at[2], vs.at[1], vr.at[1], p.ynb)
    v_y.start()
    own_i.wait()
    own_o.wait()
    i_y.wait()
    i_x = rcopy(i_half(x), i_half(x), es.at[9], er.at[9], p.xnb)
    i_x.start()
    o_x.wait()
    o_y = rcopy(o_half(y), o_half(y), es.at[10], er.at[10], p.ynb)
    o_y.start()
    if placed:
        step_of(qkv_chains[2], 2)
    q_sum(1)
    y_m.wait()
    o_mix[:, lanes(c * h2, h2)] = (xm[...].astype(f32) + ym[...].astype(f32)).astype(bf16)
    m_core = rcopy(
        o_mix.at[:, lanes(c * h2, h2)], o_mix.at[:, lanes(c * h2, h2)], es.at[7], er.at[7], p.core
    )
    m_core.start()
    v_y.wait()
    v_acc[...] = v_acc[...] + v_in[2]
    v_z[z] = v_acc[...]

    def vcopy(way, s, b):
        dev = p.right if way == 0 else p.left
        return rcopy(v_z.at[b], v_z.at[b], bs.at[6, way, s], br.at[6, way, s], dev)

    def v_send(s):
        for way in (0, 1):
            ok, b = spread_send(way, s, z, nz)

            @pl.when(both(ok, s <= nz - 1))
            def _():
                vcopy(way, s, b).start()

    def v_get(s):
        for way in (0, 1):
            ok, b = spread_get(way, s, z, nz)

            @pl.when(ok)
            def _():
                vcopy(way, s, b).wait_recv()

        v_send(s + 1)

    v_send(1)
    if placed:
        step_of(qkv_chains[2], 3)
    q_x(2).start()
    all_steps(v_get)
    q_sum(2)
    ig_y.wait()
    o_ig[...] = (cg[y].astype(f32) + yg[...].astype(f32)).astype(o_ig.dtype)

    def v_sum(i, carry):
        return carry + v_z[i]

    o_vec[...] = lax.fori_loop(0, nz, v_sum, jnp.zeros(o_vec.shape, f32))
    i_x.wait()
    i_all = o_inn.at[:, lanes(c * w2, w2)]
    i_core = rcopy(i_all, i_all, es.at[11], er.at[11], p.core)
    i_core.start()
    o_y.wait()
    o_all = o_out.at[:, lanes(c * h2, h2)]
    o_core = rcopy(o_all, o_all, es.at[12], er.at[12], p.core)
    o_core.start()
    for h in range(heads):
        q_y(h).wait()
        q_on(h).start()
    for cp in [m_core, i_core, o_core, put_y] + [q_core(h) for h in range(heads)] + [q_on(h) for h in range(heads)]:
        cp.wait()
    for ch in qkv_chains + [mix_chain, inn_chain, out_chain]:
        ch[2]()

    def vdrain(s, carry):
        for way in (0, 1):
            ok, b = spread_send(way, s, z, nz)

            @pl.when(ok)
            def _():
                vcopy(way, s, b).wait_send()

        return carry

    lax.fori_loop(1, nz, vdrain, 0)


def w_heads_of(pw, width):
    return pw[...].reshape(width, pw.shape[2])


def whole(nz, tokens, teacher, seg, valid, par, wq, wk, wv, small, binner, mix, inn, out):
    trees, length, width = tokens.shape
    rz, wide = mix.shape[0], inn.shape[1]
    full, count, n = 4 * length, trees * length, width // 4
    heads = n // HD
    h2, w2, w4, w8 = width // 2, wide // 2, wide // 4, wide // 8
    vmem = pl.BlockSpec(memory_space=pltpu.VMEM)
    anyspace = pl.BlockSpec(memory_space=pl.ANY)
    shape = jax.ShapeDtypeStruct
    vec = (16, width)
    most = max(nz, 4)
    return pl.pallas_call(
        functools.partial(whole_body, nz),
        out_shape=(
            shape((count, width), bf16),
            shape((count, width), f32),
            shape((trees * full, width), bf16),
            shape((rz, wide), bf16),
            shape((4 * rz, width), bf16),
            shape((rz, width), bf16),
            shape((heads, 4, rz, 3 * HD), bf16),
            shape((trees, length, width), bf16),
            shape(vec, f32),
        ),
        in_specs=[anyspace] * 2 + [vmem] * 2 + [pl.BlockSpec(memory_space=pltpu.SMEM)] + [anyspace] * 3 + [vmem] * 2 + [anyspace] * 3,
        out_specs=[anyspace] * 5 + [vmem] * 4,
        scratch_shapes=[
            pltpu.SMEM((trees, NSEG), jnp.int32),
            V((trees, 4, length, width), bf16),
            V((trees, full, width), bf16),
            V((width, width), bf16),
            V((nz, rz, wide), bf16),
            V((wide, width), bf16),
            V((nz, rz, 3 * n), bf16),
            V((trees, full, 3 * n), bf16),
            V((trees, full, 8), f32),
            V((trees, full, 4 * HD), bf16),
            V((trees, full, n), bf16),
            V((4, trees, length, n), bf16),
            V((count, width), bf16),
            V((count, width), f32),
            V((count, width), f32),
            V((count, width), f32),
            V((count, width), bf16),
            V((count, width), bf16),
            V((count, width), bf16),
            V((count, width), bf16),
            V((count, 128), f32),
            V((count, 128), f32),
            V((width, width), bf16),
            V((trees, full, n), bf16),
            V((full, HD), f32),
            V((full, HD), f32),
            V((nz, rz, w2), bf16),
            V((nz, 4 * rz, h2), bf16),
            V((width, h2), bf16),
            V((2, trees, length, width), bf16),
            V((nz, rz, w4), bf16),
            V((nz, 2 * rz, h2), bf16),
            V((nz, rz, w8), bf16),
            V((nz, rz, h2), bf16),
            V((trees, length, width), bf16),
            V((2, nz, rz, w8), bf16),
            V((2, nz, rz, h2), bf16),
            V((2, nz, rz, h2), bf16),
            V((heads, 2, nz, rz, 3 * HD), bf16),
            V((heads, nz, rz, 3 * HD), bf16),
            V((rz, h2), bf16),
            V((rz, h2), bf16),
            V((heads, rz, 3 * HD), bf16),
            V((3,) + vec, f32),
            V((nz,) + vec, f32),
            V(vec, f32),
            V((nz, 16, width), bf16),
            V((nz, 8, wide), bf16),
            V((4, 8, count), jnp.int32),
            V(vec, f32),
            V((8, wide), f32),
            DMA((8,)), DMA((trees, 4)), DMA((trees * 4,)),
            DMA((6,)), DMA((6,)),
            DMA((6, 2, nz)), DMA((6, 2, nz)),
            DMA((nz,)), DMA((nz,)),
            DMA((2, nz)), DMA((2, nz)),
            DMA((3, 2, nz)), DMA((3, 2, nz)),
            DMA((trees, 3)), DMA((trees, 3)),
            DMA((3,)), DMA((3,)),
            DMA((5,)), DMA((5,)),
            DMA((2, most)), DMA((2, most)),
            DMA((2, nz)), DMA((2, nz)),
            DMA((2, nz)), DMA((2, nz)),
            DMA((7, 2, nz)), DMA((7, 2, nz)),
            DMA((25,)), DMA((25,)),
            DMA((2,)), DMA((2,)),
        ],
        compiler_params=pltpu.CompilerParams(
            collective_id=1, has_side_effects=True, vmem_limit_bytes=63 * 1024 * 1024
        ),
        name="whole",
    )(tokens, teacher, seg, valid, par, wq, wk, wv, small, binner, mix, inn, out)


def finish_body(
    slots, spot, inn, out, mix, qkv, ig, one, vec,
    o_inn, o_out, o_mix, o_q, o_k, o_v, o_ig,
    b_inn, b_out, b_mix, b_q, b_k, b_v, b_ig, sem,
):
    scale = slots / vec[spot : spot + 1, 0:1]
    copies = []

    def put(i, buf, dst):
        cp = pltpu.make_async_copy(buf, dst, sem.at[i])
        cp.start()
        copies.append(cp)

    def scaled(dst, src):
        step = 64 if src.shape[0] % 64 == 0 else src.shape[0]

        def part(i, carry):
            rows = pl.ds(pl.multiple_of(i * step, step), step)
            dst[rows] = src[rows].astype(f32) * scale
            return carry

        lax.fori_loop(0, src.shape[0] // step, part, 0)

    scaled(b_inn, inn)
    put(0, b_inn, o_inn)
    scaled(b_out, out)
    put(1, b_out, o_out)
    for t in range(ig.shape[0]):

        def part(i, carry):
            rows = pl.ds(pl.multiple_of(i * 64, 64), 64)
            b_ig[t, rows] = (one[t, rows] + ig[t, rows].astype(f32)) * scale
            return carry

        lax.fori_loop(0, ig.shape[1] // 64, part, 0)
    put(2, b_ig, o_ig)
    for i, (buf, dst) in enumerate(((b_q, o_q), (b_k, o_k), (b_v, o_v))):
        for j in range(4):
            for h in range(qkv.shape[0]):
                at = (j * qkv.shape[0] + h) * HD
                buf[:, at : at + HD] = qkv[h, j, :, i * HD : (i + 1) * HD].astype(f32) * scale
        put(3 + i, buf, dst)
    scaled(b_mix, mix)
    put(6, b_mix, o_mix)
    for cp in copies:
        cp.wait()


def finish(slots, spot, inn, out, mix, qkv, ig, one, vec):
    rz, width = mix.shape
    vm = pl.BlockSpec(memory_space=pltpu.VMEM)
    anyspace = pl.BlockSpec(memory_space=pl.ANY)
    shapes = [inn.shape, out.shape, mix.shape, mix.shape, mix.shape, mix.shape, ig.shape]
    return pl.pallas_call(
        functools.partial(finish_body, slots, spot),
        out_shape=tuple(jax.ShapeDtypeStruct(sh, f32) for sh in shapes),
        in_specs=[vm] * 7,
        out_specs=[anyspace] * 7,
        scratch_shapes=[V(sh, f32) for sh in shapes] + [DMA((7,))],
        compiler_params=pltpu.CompilerParams(vmem_limit_bytes=32 * 1024 * 1024),
        name="finish",
    )(inn, out, mix, qkv, ig, one, vec)


def per_device(
    nz,
    tokens, teacher, seg_ids, parent_seg, valid,
    query_weight, query_bias, key_weight, value_weight, value_bias,
    mix_weight, mix_bias, first_gain, first_shift,
    inner_weight, inner_bias, outer_weight, outer_bias, second_gain, second_shift,
):
    trees, local_len, width = tokens.shape
    n_seq = lax.axis_size("seq")
    row_count = trees * local_len
    total_slots = row_count * lax.axis_size("replica") * nz * n_seq
    rz = mix_weight.shape[0]
    wide = inner_weight.shape[1]

    small = jnp.zeros((16, width), f32)
    vectors = (query_bias, value_bias, mix_bias, first_gain, first_shift, outer_bias, second_gain, second_shift)
    for i, v in enumerate(vectors):
        small = small + jnp.pad(v.astype(f32)[None], ((i, 15 - i), (0, width - rz)))
    binner = jnp.pad(inner_bias.astype(f32)[None], ((0, 7), (0, wide - inner_bias.shape[0])))

    layer_out, grad_one, _, r_inn, r_out, r_mix, r_qkv, r_ig, r_vec = whole(
        nz, tokens, teacher.reshape(row_count, width), seg_ids, valid, parent_seg,
        query_weight, key_weight, value_weight, small, binner, mix_weight, inner_weight, outer_weight,
    )
    layer_out = layer_out.reshape(trees, local_len, width)
    flat = r_vec.reshape(-1)
    spot = 8 + wide // width
    count = r_vec[spot + 1, 0]
    scale = total_slots / count
    loss_value = jnp.sum(r_vec[spot]) / count
    shard = lax.axis_index("shard")

    def vec_out(i):
        return lax.dynamic_slice_in_dim(flat, i * width + shard * rz, rz, axis=0) * scale

    size = inner_bias.shape[0]
    dinner_bias = lax.dynamic_slice_in_dim(flat, 8 * width + shard * size, size, axis=0) * scale

    dinner, douter, dmix, dquery, dkey, dvalue, input_grad = finish(
        total_slots, spot + 1, r_inn, r_out, r_mix, r_qkv, r_ig,
        grad_one.reshape(trees, local_len, width), r_vec,
    )
    return (
        layer_out, loss_value, input_grad,
        dquery, vec_out(0), dkey, dvalue, vec_out(1),
        dmix, vec_out(2), vec_out(3), vec_out(4),
        dinner, dinner_bias, douter, vec_out(5), vec_out(6), vec_out(7),
    )


def solution(mesh):
    rows = P(("replica", "shard"), "seq", None)
    line = P(("replica", "shard"), "seq")
    mat = P("shard", None)
    row = P("shard")
    placed = (
        rows, rows, line, P(("replica", "shard"), None), line,
        mat, row, mat, mat, row, mat, row, row, row, mat, row, mat, row, row, row,
    )
    return jax.shard_map(
        functools.partial(per_device, mesh.shape["shard"]),
        mesh=mesh,
        in_specs=placed,
        out_specs=(
            rows, P(), rows,
            mat, row, mat, mat, row, mat, row, row, row, mat, row, mat, row, row, row,
        ),
        check_vma=False,
    )
```

```python
import functools

import jax
import jax.numpy as jnp
from jax import lax
from jax.experimental import pallas as pl
from jax.experimental.pallas import tpu as pltpu
from jax.sharding import PartitionSpec as P

HEADS = 12
HD = 64
NSEG = 8
MESH = pl.DeviceIdType.MESH
BIG = 1e30
norm_eps = 1e-12
f32 = jnp.float32
bf16 = jnp.bfloat16
VMEM_LIMIT = 63 * 1024 * 1024


class Place:
    def __init__(self, nz):
        self.nz = nz
        self.x = lax.axis_index("replica")
        self.z = lax.axis_index("shard")
        self.q = lax.axis_index("seq")
        self.y = self.q // 2
        self.c = self.q % 2
        x, z, y, c = self.x, self.z, self.y, self.c
        self.core = (x, z, 2 * y + 1 - c)
        self.ynb = (x, z, 2 * (1 - y) + c)
        self.xnb = (1 - x, z, self.q)
        self.right = (x, z + 1, self.q)
        self.left = (x, z - 1, self.q)

    def greet(self, more):
        bar = pltpu.get_barrier_semaphore()
        for peer in [self.core, self.ynb, self.xnb] + more:
            pl.semaphore_signal(bar, inc=1, device_id=peer, device_id_type=MESH)

        @pl.when(self.z > 0)
        def _():
            pl.semaphore_signal(bar, inc=1, device_id=self.left, device_id_type=MESH)

        @pl.when(self.z < self.nz - 1)
        def _():
            pl.semaphore_signal(bar, inc=1, device_id=self.right, device_id_type=MESH)

        peers = 3 + len(more) + (self.z > 0).astype(jnp.int32) + (self.z < self.nz - 1).astype(jnp.int32)
        pl.semaphore_wait(bar, peers)


def rcopy(src, dst, ssem, rsem, dev):
    return pltpu.make_async_remote_copy(
        src_ref=src, dst_ref=dst, send_sem=ssem, recv_sem=rsem, device_id=dev, device_id_type=MESH
    )


def both(a, b):
    return jnp.logical_and(a, b)


def dot_nt(a, b):
    return lax.dot_general(a, b, (((1,), (1,)), ((), ())), preferred_element_type=f32)


def dot_tn(a, b):
    return lax.dot_general(a, b, (((0,), (0,)), ((), ())), preferred_element_type=f32)


def dot_nn(a, b):
    return jnp.dot(a, b, preferred_element_type=f32)


def add_to(dst, src):
    dst[...] = (dst[...].astype(f32) + src[...].astype(f32)).astype(dst.dtype)


def lanes(start, size):
    return pl.ds(pl.multiple_of(start, 128), size)


def rows_at(start, size):
    return pl.ds(pl.multiple_of(start, 8), size)


def row_mean(v):
    return jnp.sum(v, axis=1, keepdims=True) * (1.0 / v.shape[1])


def norm_back(grad_hat, hat, inv):
    return inv * (grad_hat - row_mean(grad_hat) - hat * row_mean(grad_hat * hat))


def fold(v):
    return jnp.sum(v.reshape(v.shape[0] // 8, 8, v.shape[1]), axis=0)


def total_row(v):
    return jnp.sum(v, axis=0, keepdims=True)


QB = 256
RB = 32
DMA = pltpu.SemaphoreType.DMA
V = pltpu.VMEM


def spread_send(way, s, z, nz):
    if way == 0:
        return both(z >= s - 1, z < nz - 1), z - s + 1
    return both(z <= nz - s, z > 0), z + s - 1


def spread_get(way, s, z, nz):
    if way == 0:
        return z >= s, z - s
    return z <= nz - 1 - s, z + s


def whole_body(
    nz, x_hbm, tea_hbm, seg_ref, valid_ref, par_ref, wq_hbm, wk_hbm, wv_hbm, *more,
):
    vectors, (mix_hbm, inn_hbm, out_hbm) = more[:9], more[9:12]
    (
        y_hbm, one_hbm, xa_hbm, o_inn, o_out, o_mix, o_qkv, o_ig, o_vec, bits, hid, slp, mixa, inna, outa, pw, qkv,
        lse, feat, att, blocks, tok, A1, A2, A3, fl, gb, gp, tea, vm, inv1, mixg, gat, dk, dv, ci, co, cm, cg, xi, yo,
        yi, xo, yg, zi, zo, zm, zq, aq, xm, ym, xq, v_in, v_z, v_acc, sma, bia, tga, vecs, binner, loc, sav, rel, xs,
        xr, zs, zr, fs, fr, cs, cr, hs, hr, gs_, gr_, ks, kr, ds_, dr_, s1, r1, s2, r2, is_, ir, ps, pr, bs, br, es, er, vs, vr,
    ) = more[12:]
    p = Place(nz)
    z, c, y, x, q = p.z, p.c, p.y, p.x, p.q
    rz, width = mix_hbm.shape
    wide = inn_hbm.shape[1]
    trees, length = x_hbm.shape[0], x_hbm.shape[1]
    full = qkv.shape[1]
    count = trees * length
    n = width // 4
    heads = n // HD
    chunks = wide // width
    h2, w2, w4, w8 = width // 2, wide // 2, wide // 4, wide // 8
    cross = (x, z, 2 * (1 - y) + 1 - c)
    qy = 2 * (1 - y) + c
    o4 = 4 * rz

    load = [
        pltpu.make_async_copy(x_hbm, hid.at[:, q], loc.at[0]),
        pltpu.make_async_copy(wq_hbm, slp.at[0, pl.ds(0, rz)], loc.at[1]),
        pltpu.make_async_copy(wk_hbm, slp.at[0, pl.ds(256, rz)], loc.at[2]),
        pltpu.make_async_copy(wv_hbm, slp.at[0, pl.ds(512, rz)], loc.at[3]),
        pltpu.make_async_copy(mix_hbm, mixa.at[rows_at(z * rz, rz)], loc.at[4]),
        pltpu.make_async_copy(inn_hbm, inna.at[z], loc.at[5]),
        pltpu.make_async_copy(out_hbm, outa.at[rows_at(z * o4, o4)], loc.at[6]),
        pltpu.make_async_copy(tea_hbm, tea, loc.at[7]),
    ]
    for cp in load:
        cp.start()
    for t in range(trees):
        seg = seg_ref[t : t + 1, :]
        tga[q, 0:1, t * length : (t + 1) * length] = jnp.where(
            valid_ref[t : t + 1, :] == 1, seg, seg + NSEG
        )
    p.greet([cross])

    def x_core(t):
        return rcopy(hid.at[t, q], hid.at[t, q], xs.at[2 + t], xr.at[2 + t], p.core)

    def x_y(t):
        return rcopy(hid.at[t, q], hid.at[t, q], xs.at[2 + trees + t], xr.at[2 + trees + t], p.ynb)

    def x_on(t):
        return rcopy(hid.at[t, qy], hid.at[t, qy], xs.at[2 + 2 * trees + t], xr.at[2 + 2 * trees + t], p.core)

    t_core = rcopy(tga.at[q], tga.at[q], xs.at[0], xr.at[0], p.core)
    t_y = rcopy(tga.at[q], tga.at[q], xs.at[1], xr.at[1], p.ynb)
    t_on = rcopy(tga.at[qy], tga.at[qy], xs.at[2 + 3 * trees], xr.at[2 + 3 * trees], p.core)
    t_y.start()
    t_core.start()
    load[0].wait()
    for t in range(trees):
        x_y(t).start()
    for t in range(trees):
        x_core(t).start()

    back = lax.rem(width - q * n, width)
    for i in range(3):
        load[1 + i].wait()
        turned = pltpu.roll(slp[0, i * 256 : i * 256 + rz].astype(f32), back, 1)
        for h in range(heads):
            pw[z, :, (3 * h + i) * HD : (3 * h + i + 1) * HD] = turned[:, h * HD : (h + 1) * HD].astype(bf16)
    def row_of(ref, size):
        own = ref[...].astype(f32).reshape(1, ref.shape[0])
        if ref.shape[0] == size:
            return own
        return jnp.concatenate([own, jnp.zeros((1, size - ref.shape[0]), f32)], axis=1)

    small = jnp.concatenate([row_of(v, width) for v in vectors[:8]] + [jnp.zeros((8, width), f32)], axis=0)
    sma[z] = pltpu.roll(small, z * rz, 1).astype(bf16)
    binner[...] = jnp.concatenate([row_of(vectors[8], wide), jnp.zeros((7, wide), f32)], axis=0)
    bia[z] = pltpu.roll(binner[...], z * (wide // nz), 1).astype(bf16)

    def at_row(ref, b, size):
        return ref.at[rows_at(b * size, size)]

    def piece_of(k, b, xx, yy):
        if k == 0:
            return inna.at[b, :, lanes(c * w2 + (2 * xx + yy) * w8, w8)]
        return outa.at[rows_at(b * o4 + (2 * xx + yy) * rz, rz), lanes(c * h2, h2)]

    there = {
        0: lambda b: pw.at[b],
        1: lambda b: sma.at[b],
        2: lambda b: bia.at[b],
        3: lambda b: mixa.at[rows_at(b * rz, rz), lanes(c * h2, h2)],
        4: lambda b: piece_of(0, b, x, y),
        5: lambda b: piece_of(1, b, x, y),
    }

    def zcopy(k, way, s, b):
        dev = p.right if way == 0 else p.left
        return rcopy(there[k](b), there[k](b), zs.at[k, way, s], zr.at[k, way, s], dev)

    def start_step(k, s):
        for way in (0, 1):
            cond, b = spread_send(way, s, z, nz)

            @pl.when(both(cond, s <= nz - 1))
            def _():
                zcopy(k, way, s, b).start()

    def each(s, fn):
        for way in (0, 1):
            cond, b = spread_get(way, s, z, nz)

            @pl.when(cond)
            def _():
                fn(way, b)

    def take(k, s):
        each(s, lambda way, b: zcopy(k, way, s, b).wait_recv())

    def to_y(k, b):
        return rcopy(piece_of(k, b, x, y), piece_of(k, b, x, y), fs.at[k, 0, b], fr.at[k, 0, b], p.ynb)

    def to_x(k, b):
        return rcopy(piece_of(k, b, x, y), piece_of(k, b, x, y), fs.at[k, 1, b], fr.at[k, 1, b], p.xnb)

    def onward(k, b):
        piece = piece_of(0, b, x, 1 - y) if k == 0 else piece_of(1, b, 1 - x, y)
        return rcopy(piece, piece, fs.at[k, 2, b], fr.at[k, 2, b], p.xnb if k == 0 else p.ynb)

    def core_copy(k, b, part):
        if k == 2:
            piece = there[3](b)
        else:
            piece = piece_of(k, b, x if part % 2 == 0 else 1 - x, y if part < 2 else 1 - y)
        return rcopy(piece, piece, cs.at[k, part, b], cr.at[k, part, b], p.core)

    for k in (0, 1, 2):
        start_step(k, 1)

    def small_step(s, carry):
        for k in (0, 1, 2):
            take(k, s)
        for k in (0, 1, 2):
            start_step(k, s + 1)
        return carry

    lax.fori_loop(1, nz - 1, small_step, 0)
    for i in (4, 5, 6, 7):
        load[i].wait()
    for k in (4, 3, 5):
        start_step(k, 1)
    for k in (0, 1, 2):
        take(k, nz - 1)

    def mix_step(s):
        def got(way, b):
            zcopy(3, way, s, b).wait_recv()
            core_copy(2, b, 0).start()

        each(s, got)
        start_step(3, s + 1)

    def z_step(k, s):
        def got(way, b):
            zcopy(4 + k, way, s, b).wait_recv()
            first, second = (to_y, to_x) if k == 0 else (to_x, to_y)
            first(k, b).start()
            second(k, b).start()

        each(s, got)
        start_step(4 + k, s + 1)
        each(s, lambda way, b: core_copy(k, b, 0).start())

    def pass_on(k, s):
        def got(way, b):
            (to_y if k == 0 else to_x)(k, b).wait_recv()
            onward(k, b).start()
            core_copy(k, b, 2 if k == 0 else 1).start()

        each(s, got)

    def rest_of(k, s):
        def got(way, b):
            (to_x if k == 0 else to_y)(k, b).wait_recv()
            core_copy(k, b, 1 if k == 0 else 2).start()
            onward(k, b).wait_recv()
            core_copy(k, b, 3).start()

        each(s, got)

    def from_core(k, s):
        def got(way, b):
            for part in range(4 if k < 2 else 1):
                core_copy(k, b, part).wait_recv()

        each(s, got)

    def all_steps(*fns):
        def one(s, carry):
            for fn in fns:
                fn(s)
            return carry

        lax.fori_loop(1, nz, one, 0)

    placed = nz == 4

    def vsum(i, carry):
        return carry[0] + sma[i].astype(f32), carry[1] + bia[i].astype(f32)

    small, inner_bias = lax.fori_loop(0, nz, vsum, (jnp.zeros(vecs.shape, f32), jnp.zeros(binner.shape, f32)))
    vecs[...] = small
    binner[...] = inner_bias
    turned = pltpu.roll(small, back, 1)
    bias = []
    for h in range(heads):
        cols = slice(h * HD, (h + 1) * HD)
        bias += [turned[0:1, cols], jnp.zeros((1, HD), f32), turned[1:2, cols]]
    bias = jnp.concatenate(bias, axis=1)

    t_y.wait_recv()
    t_on.start()
    t_core.wait()
    t_on.wait()

    row = lax.broadcasted_iota(jnp.int32, (16, 4 * HD), 0)
    lane = lax.broadcasted_iota(jnp.int32, (16, 4 * HD), 1)
    trow = lax.broadcasted_iota(jnp.int32, (16, full), 0)
    vrow = lax.broadcasted_iota(jnp.int32, (16, length), 0)
    ones = jnp.ones((16, 128), bf16)
    for t in range(trees):
        bits[t, 0] = jnp.int32(1)
        for s in range(1, NSEG):
            bits[t, s] = bits[t, par_ref[t, s]] + (1 << s)
        seen = jnp.zeros((16, 4 * HD), jnp.int32)
        for a in range(NSEG):
            seen = jnp.where(row == a, bits[t, a], seen)
        at = jnp.clip(lane - HD, 0, NSEG)
        unseen = ((seen >> at) & 1) == 0
        q_side = both(both(row < NSEG, both(lane >= HD, lane <= HD + NSEG)), unseen)
        k_side = both(row <= NSEG, lane == row + 3 * HD)
        table = jnp.where(q_side, -BIG, jnp.where(k_side, 1.0, 0.0)).astype(bf16)
        tag = jnp.concatenate(
            [tga[j, 0:1, t * length : (t + 1) * length] for j in range(full // length)], axis=1
        )
        gone = tag >= NSEG
        seg = jnp.where(gone, tag - NSEG, tag)
        seg = jnp.broadcast_to(seg, (16, full))
        gone = jnp.broadcast_to(jnp.where(gone, 1, 0), (16, full))
        hot = jnp.where(trow == NSEG, gone, jnp.where(trow == seg, 1, 0)).astype(f32).astype(bf16)
        feat[t] = dot_tn(hot, table).astype(bf16)
        here = jnp.broadcast_to(valid_ref[t : t + 1, :], (16, length))
        here = jnp.where(vrow == 0, here, 0).astype(f32).astype(bf16)
        vm[t * length : (t + 1) * length] = dot_tn(here, ones)

    t_y.wait_send()
    w_heads = w_heads_of(pw, width)
    saves = []

    def project(t):
        x_core(t).wait()
        x_on(t).wait()
        for j in range(4):
            cp = pltpu.make_async_copy(
                hid.at[t, j], xa_hbm.at[pl.ds((t * 4 + j) * length, length)], sav.at[t, j]
            )
            cp.start()
            saves.append(cp)
        qkv[t] = (dot_nn(hid[t].reshape(full, width), w_heads) + bias).astype(bf16)

    for t in range(trees):
        x_y(t).wait()
        x_on(t).start()
        if t == 0:
            project(0)


    def part(h, i):
        return slice((3 * h + i) * HD, (3 * h + i + 1) * HD)

    def queries_of(t, rows, h):
        return jnp.concatenate([qkv[t, rows, part(h, 0)] * 0.125, feat[t, rows, HD : 2 * HD]], axis=1)

    def keys_of(t, h):
        return jnp.concatenate([qkv[t, :, part(h, 1)], feat[t, :, 3 * HD : 4 * HD]], axis=1)

    def token_rows(j):
        return pl.ds(pl.multiple_of(j * length, length), length)

    def send_heads(t, d):
        to = lax.rem(q + d, 4)
        return rcopy(
            att.at[t, token_rows(to)], blocks.at[q, t], hs.at[t, d - 1], hr.at[t, d - 1], (x, z, to)
        )

    def run_at(slots, first, i):
        for k in range(full // QB):
            fns = slots.get(first + k, [])
            if fns:

                @pl.when(i == k)
                def _():
                    for fn, *args in fns:
                        fn(*args)

    slots = {
        1: [(z_step, 0, 1)],
        5: [(mix_step, 1)],
        9: [(pass_on, 0, 1)],
        10: [(z_step, 1, 1)],
        13: [(z_step, 0, 2)],
        14: [(mix_step, 2)],
        17: [(pass_on, 1, 1)],
        18: [(z_step, 1, 2)],
        21: [(pass_on, 0, 2)],
        22: [(z_step, 0, 3)],
    }
    if not placed:
        slots = {}
    per_head = full // QB
    for t in range(trees):
        if t > 0:
            project(t)
        for h in range(heads):
            keys = keys_of(t, h)
            values = qkv[t, :, part(h, 2)]

            def block(i, carry):
                rows = pl.ds(pl.multiple_of(i * QB, QB), QB)
                s = dot_nt(queries_of(t, rows, h), keys)
                peak = jnp.max(s, axis=1, keepdims=True)
                e = jnp.exp(s - peak)
                total = jnp.sum(e, axis=1, keepdims=True)
                o = dot_nn(e.astype(bf16), values) / total
                att[t, rows, h * HD : (h + 1) * HD] = o.astype(bf16)
                lse[t, rows, h : h + 1] = peak + jnp.log(total)
                run_at(slots, (t * heads + h) * per_head, i)
                return carry

            lax.fori_loop(0, full // QB, block, 0)
        for d in (1, 2, 3):
            send_heads(t, d).start()
    for t in range(trees):
        blocks[q, t] = att[t, token_rows(q)]
    if placed:
        mix_step(3)
        pass_on(1, 2)
        pass_on(0, 3)
        z_step(1, 3)
    else:
        all_steps(mix_step)
    for t in range(trees):
        for d in (1, 2, 3):
            send_heads(t, d).wait()

    for j in range(4):
        tok[:, j * n : (j + 1) * n] = blocks[j].reshape(count, n)
    all_steps(functools.partial(from_core, 2))
    A3[...] = dot_nn(tok[...], mixa[...])
    if placed:
        rest_of(0, 1)
        rest_of(0, 2)

    def rows_of(i):
        return pl.ds(pl.multiple_of(i * RB, RB), RB)

    per = length // RB

    def first_norm(i, carry):
        rows = rows_of(i)
        own = hid[i // per, q, rows_of(i % per)].astype(f32)
        r1 = own + A3[rows] + vecs[2:3]
        center = r1 - row_mean(r1)
        inv = lax.rsqrt(row_mean(center * center) + norm_eps)
        hat = center * inv
        A1[rows] = hat
        inv1[rows] = jnp.broadcast_to(inv, (RB, 128))
        fl[rows] = (hat * vecs[3:4] + vecs[4:5]).astype(bf16)
        return carry

    lax.fori_loop(0, count // RB, first_norm, 0)
    for cp in saves:
        cp.wait()
    if placed:
        pass_on(1, 3)
        rest_of(0, 3)
    else:
        for k in (0, 1):
            all_steps(*[functools.partial(fn, k) for fn in (z_step, pass_on, rest_of)])
    all_steps(functools.partial(from_core, 0))

    def inner_chunk(j):
        return inna[:, :, j * width : (j + 1) * width].reshape(width, width)

    def hid_chunk(j):
        return hid[j // 2, 2 * (j % 2) : 2 * (j % 2) + 2].reshape(count, width)

    for j in range(chunks):
        A3[...] = dot_nn(fl[...], inner_chunk(j))

        def gelu(i, carry):
            rows = rows_of(i)
            pre = A3[rows] + binner[0:1, j * width : (j + 1) * width]
            cdf = 0.5 + 0.5 * lax.erf(pre * (0.5**0.5))
            hid[j // 2, 2 * (j % 2) + i // per, rows_of(i % per)] = (pre * cdf).astype(bf16)
            slope = cdf + pre * jnp.exp(-0.5 * pre * pre) * 0.3989422804014327
            slp[j // 2, pl.ds(pl.multiple_of((j % 2) * count + i * RB, RB), RB)] = slope.astype(bf16)
            return carry

        lax.fori_loop(0, count // RB, gelu, 0)
        if placed and j == 0:
            rest_of(1, 1)
            rest_of(1, 2)
        if placed and j == 2:
            rest_of(1, 3)
    all_steps(functools.partial(from_core, 1))
    for j in range(chunks):
        more = dot_nn(hid_chunk(j), outa[j * width : (j + 1) * width])
        if j == 0:
            A2[...] = more
        else:
            A2[...] += more

    def drain(s, carry):
        for k in range(6):
            for way in (0, 1):
                cond, b = spread_send(way, s, z, nz)

                @pl.when(cond)
                def _():
                    zcopy(k, way, s, b).wait_send()

        def end(way, b):
            core_copy(2, b, 0).wait_send()
            for k in (0, 1):
                to_y(k, b).wait_send()
                to_x(k, b).wait_send()
                onward(k, b).wait_send()
                for part in range(4):
                    core_copy(k, b, part).wait_send()

        each(s, end)
        return carry

    lax.fori_loop(1, nz, drain, 0)

    zero = jnp.zeros((8, width), f32)

    def second_norm(i, carry):
        loss, dgain, dshift, dbias = carry
        rows = rows_of(i)
        first = A1[rows] * vecs[3:4] + vecs[4:5]
        r2 = first + A2[rows] + vecs[5:6]
        center = r2 - row_mean(r2)
        inv = lax.rsqrt(row_mean(center * center) + norm_eps)
        hat = center * inv
        out = hat * vecs[6:7] + vecs[7:8]
        err = out - tea[rows].astype(f32)
        tea[rows] = out.astype(bf16)
        weighted = vm[rows, 0:1] * err
        grad = 2.0 * weighted
        g2 = norm_back(grad * vecs[6:7], hat, inv)
        A2[rows] = g2
        low = g2.astype(bf16)
        gb[rows] = low
        return (
            loss + fold(weighted * err),
            dgain + fold(grad * hat),
            dshift + fold(grad),
            dbias + fold(low.astype(f32)),
        )

    loss, dgain, dshift, dbias = lax.fori_loop(0, count // RB, second_norm, (zero, zero, zero, zero))
    put_y = pltpu.make_async_copy(tea, y_hbm, loc.at[0])
    put_y.start()
    v_acc[...] = jnp.zeros_like(v_acc)
    spot = 8 + chunks
    v_acc[5:6] = total_row(dbias)
    v_acc[6:7] = total_row(dgain)
    v_acc[7:8] = total_row(dshift)
    v_acc[spot : spot + 1] = total_row(loss)
    v_acc[spot + 1 : spot + 2, 0:128] = total_row(vm[...])

    def c_out(d):
        return rcopy(outa.at[rows_at(d * o4, o4), lanes((1 - c) * h2, h2)], co.at[d], ds_.at[0, d], dr_.at[0, d], p.core)

    def chunk_of(core, k):
        return (chunks - 1) * core + (1 - 2 * core) * k

    def c_inn(k):
        src = inna.at[:, :, lanes(chunk_of(1 - c, k) * width, width)]
        return rcopy(src, ci.at[:, :, pl.ds(k * width, width)], ds_.at[1, k], dr_.at[1, k], p.core)

    def out_y(d):
        src = co.at[d, rows_at((1 - y) * 2 * rz, 2 * rz)]
        return rcopy(src, yo.at[d], s1.at[0, d], r1.at[0, d], p.ynb)

    def inn_x(d, k):
        src = ci.at[d, :, lanes(k * width + (1 - x) * w8, w8)]
        return rcopy(src, xi.at[d, :, pl.ds(k * w8, w8)], s1.at[1 + k, d], r1.at[1 + k, d], p.xnb)

    def out_x(d):
        src = yo.at[d, rows_at((1 - x) * rz, rz)]
        return rcopy(src, xo.at[d], s2.at[0, d], r2.at[0, d], p.xnb)

    def inn_y(d):
        return rcopy(xi.at[d, :, lanes((1 - y) * w8, w8)], yi.at[d], s2.at[1, d], r2.at[1, d], p.ynb)

    def span(lo, hi, fn):
        if hi - lo == 1:
            fn(lo)
            return

        def one(i, carry):
            fn(i)
            return carry

        lax.fori_loop(lo, hi, one, 0)

    def of_chunk(j, fn):
        span(j * nz // chunks, (j + 1) * nz // chunks, fn)

    def group(g, fn):
        def pair(i):
            fn(nz - 1 - i)
            fn(i)

        span(g * nz // 4, (g + 1) * nz // 4, pair)

    def out_chip(d):
        c_out(d).wait()
        for j in range(4):
            add_to(co.at[d, j * rz : (j + 1) * rz], outa.at[rows_at(d * o4 + j * rz, rz), lanes(c * h2, h2)])
        out_y(d).start()

    def inn_chip(g, k):
        if g == 0:
            c_inn(k).wait()

        def one(d):
            for j in range(2):
                at = slice(k * width + j * h2, k * width + (j + 1) * h2)
                add_to(ci.at[d, :, at], inna.at[d, :, lanes(chunk_of(c, k) * width + j * h2, h2)])
            inn_x(d, k).start()

        group(g, one)

    def out_half(d):
        out_y(d).wait()
        add_to(yo.at[d, :rz], co.at[d, rows_at(y * 2 * rz, rz)])
        add_to(yo.at[d, rz:], co.at[d, rows_at(y * 2 * rz + rz, rz)])
        out_x(d).start()

    def inn_half(g, k):
        def one(d):
            inn_x(d, k).wait()
            add_to(xi.at[d, :, k * w8 : (k + 1) * w8], ci.at[d, :, lanes(k * width + x * w8, w8)])

        group(g, one)

    def inn_other(g):
        group(g, lambda d: inn_y(d).start())

    def out_quarter(d):
        out_x(d).wait()
        add_to(xo.at[d], yo.at[d, rows_at(x * rz, rz)])

    def inn_quarter(d):
        inn_y(d).wait()
        add_to(yi.at[d], xi.at[d, :, lanes(y * w8, w8)])

    order = [3, 0, 2, 1]
    for step, j in enumerate(order):
        A3[...] = dot_nt(gb[...], outa[j * width : (j + 1) * width])

        def slopes(i, carry):
            rows = rows_of(i)
            slope = slp[j // 2, pl.ds(pl.multiple_of((j % 2) * count + i * RB, RB), RB)]
            low = (A3[rows] * slope.astype(f32)).astype(bf16)
            gp[rows] = low
            return carry + fold(low.astype(f32))

        v_acc[8 + j : 9 + j] = total_row(lax.fori_loop(0, count // RB, slopes, zero))
        outa[j * width : (j + 1) * width] = dot_tn(hid_chunk(j), gb[...]).astype(bf16)
        of_chunk(j, lambda d: c_out(d).start())
        A2[...] += dot_nt(gp[...], inner_chunk(j))
        inna[:, :, j * width : (j + 1) * width] = dot_tn(fl[...], gp[...]).astype(bf16).reshape(nz, rz, width)

        @pl.when(c == 1 - j // 2)
        def _():
            c_inn(step // 2).start()

        if step in (1, 2):
            of_chunk(order[step - 1], out_chip)
        if step == 2:
            inn_chip(0, 0)
            inn_chip(1, 0)

    def first_back(i, carry):
        dgain, dshift, dbias = carry
        rows = rows_of(i)
        grad = A2[rows]
        hat = A1[rows]
        g1 = norm_back(grad * vecs[3:4], hat, inv1[rows, 0:1])
        A2[rows] = g1
        low = g1.astype(bf16)
        gb[rows] = low
        return dgain + fold(grad * hat), dshift + fold(grad), dbias + fold(low.astype(f32))

    dgain, dshift, dbias = lax.fori_loop(0, count // RB, first_back, (zero, zero, zero))
    v_acc[2:3] = total_row(dbias)
    v_acc[3:4] = total_row(dgain)
    v_acc[4:5] = total_row(dshift)
    put_one = pltpu.make_async_copy(A2, one_hbm, loc.at[1])
    put_one.start()

    for j in range(4):
        part_j = dot_nt(gb[...], mixa[j * n : (j + 1) * n]).astype(bf16)
        for t in range(trees):
            att[t, j * length : (j + 1) * length] = part_j[t * length : (t + 1) * length]

    def send_grads(d):
        to = lax.rem(q + d, 4)
        return rcopy(att.at[:, token_rows(to)], gat.at[:, token_rows(q)], gs_.at[d - 1], gr_.at[d - 1], (x, z, to))

    for d in (1, 2, 3):
        send_grads(d).start()
    for t in range(trees):
        gat[t, token_rows(q)] = att[t, token_rows(q)]

    of_chunk(order[0], out_half)
    inn_chip(0, 1)
    of_chunk(order[1], out_half)
    inn_chip(1, 1)
    of_chunk(order[2], out_chip)
    reload = [
        pltpu.make_async_copy(
            xa_hbm.at[pl.ds(i * length, length)], outa.at[pl.ds(i * length, length)], rel.at[i]
        )
        for i in range(trees * 4)
    ]

    def out_last():
        of_chunk(order[-1], out_chip)
        for cp in reload:
            cp.start()

    def reloaded():
        for cp in reload:
            cp.wait()

    mixg[...] = dot_tn(tok[...], gb[...]).astype(bf16)
    c_mix = rcopy(mixg.at[:, lanes((1 - c) * h2, h2)], cm, ks.at[3], kr.at[3], p.core)
    c_mix.start()

    def chain(k, acc, buf):
        def copy(way, s, d):
            dev = p.right if way == 0 else p.left
            return rcopy(acc(d), buf(way, d), bs.at[k, way, s], br.at[k, way, s], dev)

        def sending(way, s):
            if way == 0:
                d = z + nz - s
                return both(d <= nz - 1, z < nz - 1), d
            d = z - nz + s
            return both(d >= 0, z > 0), d

        def getting(way, s):
            if way == 0:
                d = z - 1 + nz - s
                return both(d <= nz - 1, z > 0), d
            d = z + 1 - nz + s
            return both(d >= 0, z < nz - 1), d

        def send(s):
            for way in (0, 1):
                ok, d = sending(way, s)

                @pl.when(both(ok, s <= nz - 1))
                def _():
                    copy(way, s, d).start()

        def get(s):
            for way in (0, 1):
                ok, d = getting(way, s)

                @pl.when(ok)
                def _():
                    copy(way, s, d).wait_recv()
                    add_to(acc(d), buf(way, d))

        def drain(s, carry):
            for way in (0, 1):
                ok, d = sending(way, s)

                @pl.when(ok)
                def _():
                    copy(way, s, d).wait_send()

            return carry

        return send, get, lambda: lax.fori_loop(1, nz, drain, 0)

    def step_of(ch, s):
        ch[1](s)
        ch[0](s + 1)

    mix_chain = chain(3, lambda d: cm.at[rows_at(d * rz, rz)], lambda way, d: zm.at[way, d])
    inn_chain = chain(4, lambda d: yi.at[d], lambda way, d: zi.at[way, d])
    out_chain = chain(5, lambda d: xo.at[d], lambda way, d: zo.at[way, d])

    def head_chain(h):
        return chain(h, lambda d: aq.at[h, d], lambda way, d: zq.at[h, way, d])

    qkv_chains = [head_chain(h) for h in range(heads)]

    c_mix.wait()

    def mix_sum(i, carry):
        block = rows_at(i * rz, rz)
        add_to(cm.at[block], mixg.at[block, lanes(c * h2, h2)])
        return carry

    lax.fori_loop(0, nz, mix_sum, 0)
    mix_chain[0](1)
    for d in (1, 2, 3):
        send_grads(d).wait()

    def head_weights(h):
        cols = slice(3 * h * HD, 3 * (h + 1) * HD)
        grad = dot_tn(outa[0:full], slp[0, :, cols])
        for t in range(1, trees):
            grad = grad + dot_tn(outa[t * full : (t + 1) * full], slp[t, :, cols])
        aq[h] = grad.astype(bf16).reshape(nz, rz, 3 * HD)
        qkv_chains[h][0](1)

    def q_x(h):
        return rcopy(aq.at[h, z], xq.at[h], es.at[13 + h], er.at[13 + h], p.xnb)

    def q_y(h):
        return rcopy(o_qkv.at[h, q], o_qkv.at[h, q], es.at[16 + h], er.at[16 + h], p.ynb)

    def q_core(h):
        return rcopy(o_qkv.at[h, q], o_qkv.at[h, q], es.at[19 + h], er.at[19 + h], p.core)

    def q_on(h):
        return rcopy(o_qkv.at[h, qy], o_qkv.at[h, qy], es.at[22 + h], er.at[22 + h], p.core)

    def q_sum(h):
        q_x(h).wait()
        o_qkv[h, q] = (aq[h, z].astype(f32) + xq[h].astype(f32)).astype(bf16)
        q_y(h).start()
        q_core(h).start()

    x_m = rcopy(cm.at[rows_at(z * rz, rz)], xm, es.at[1], er.at[1], p.xnb)
    y_m = rcopy(xm, ym, es.at[4], er.at[4], p.ynb)

    def big_step(s):
        step_of(inn_chain, s)
        step_of(out_chain, s)

    def first_big():
        inn_chain[0](1)
        out_chain[0](1)

    def ig_of(t):
        for j in range(4):
            rows = slice(j * length, (j + 1) * length)
            hid[t, j] = dot_nt(slp[t, rows, : 3 * n], w_heads_of(pw, width)).astype(bf16)
        for b in range(2):
            c_ig(t, b).start()

    def c_ig(t, b):
        return rcopy(hid.at[t, 2 * b + 1 - c], cg.at[b, t], is_.at[b, t], ir.at[b, t], p.core)

    def ig_y(t):
        return rcopy(cg.at[1 - y, t], yg.at[t], is_.at[2, t], ir.at[2, t], p.ynb)

    def ig_chip(t):
        for b in range(2):
            c_ig(t, b).wait()
            add_to(cg.at[b, t], hid.at[t, 2 * b + c])
        ig_y(t).start()

    def ig_end(t):
        ig_y(t).wait()
        o_ig[t] = (cg[y, t].astype(f32) + yg[t].astype(f32)).astype(o_ig.dtype)

    def done_piece(k, xx, yy):
        if k == 0:
            return o_inn.at[:, lanes(chunk_of(c, yy) * width + xx * w8, w8)]
        return o_out.at[rows_at((2 * yy + xx) * rz, rz), lanes(c * h2, h2)]

    def own_done(k):
        return pltpu.make_async_copy((yi if k == 0 else xo).at[z], done_piece(k, x, y), loc.at[2 + k])

    def done_y(k):
        return rcopy((yi if k == 0 else xo).at[z], done_piece(k, x, y), ps.at[k, 0], pr.at[k, 0], p.ynb)

    def done_x(k):
        return rcopy((yi if k == 0 else xo).at[z], done_piece(k, x, y), ps.at[k, 1], pr.at[k, 1], p.xnb)

    def done_on(k):
        return rcopy(done_piece(k, x, 1 - y), done_piece(k, x, 1 - y), ps.at[k, 2], pr.at[k, 2], p.xnb)

    def done_core(k, part):
        piece = done_piece(k, x if part % 2 == 0 else 1 - x, y if part < 2 else 1 - y)
        src = (yi if k == 0 else xo).at[z] if part == 0 else piece
        return rcopy(src, piece, ps.at[k, 3 + part], pr.at[k, 3 + part], p.core)

    def big_own():
        for k in (0, 1):
            own_done(k).start()
            done_y(k).start()
            done_x(k).start()
            done_core(k, 0).start()

    def big_on():
        for k in (0, 1):
            done_y(k).wait()
            done_on(k).start()
            done_core(k, 2).start()

    def big_end():
        for k in (0, 1):
            done_x(k).wait()
            done_core(k, 1).start()
        for k in (0, 1):
            done_on(k).wait()
            done_core(k, 3).start()

    def mix_end():
        x_m.wait()
        add_to(xm, cm.at[rows_at(z * rz, rz)])
        y_m.start()

    def quarters(g):
        group(g, out_quarter)
        group(g, inn_quarter)

    def head_step(h, s):
        step_of(qkv_chains[h], s)

    def q_start(h):
        q_x(h).start()

    slots = {
        0: [(inn_half, 0, 0), (inn_half, 1, 0)],
        4: [(inn_half, 0, 1), (inn_other, 0), (of_chunk, order[2], out_half), (out_last,)],
        5: [(step_of, mix_chain, 1)],
        8: [(group, 0, out_quarter)],
        9: [(inn_half, 1, 1), (inn_other, 1)],
        10: [(group, 0, inn_quarter), (first_big,)],
        11: [(step_of, mix_chain, 2)],
        12: [(ig_of, 0)],
        13: [(of_chunk, order[-1], out_half)],
        14: [(ig_chip, 0)],
        15: [(step_of, mix_chain, 3), (lambda: x_m.start(),)],
        16: [(quarters, 1), (big_step, 1)],
        17: [(reloaded,), (head_weights, 0)],
        19: [(mix_end,)],
        20: [(head_step, 0, 1)],
        21: [(big_step, 2), (head_weights, 1)],
    }
    if not placed:
        slots = {}
    put_one.wait()
    for t in range(trees):
        for h in range(heads):
            key = qkv[t, :, part(h, 1)]
            keys = keys_of(t, h)
            values = qkv[t, :, part(h, 2)]
            dk[...] = jnp.zeros_like(dk)
            dv[...] = jnp.zeros_like(dv)

            def block(i, carry):
                rows = pl.ds(pl.multiple_of(i * QB, QB), QB)
                s = dot_nt(queries_of(t, rows, h), keys)
                probs = jnp.exp(s - lse[t, rows, h : h + 1])
                grad = gat[t, rows, h * HD : (h + 1) * HD]
                dp = dot_nt(grad, values)
                inner = jnp.sum(probs * dp, axis=1, keepdims=True)
                ds = (probs * (dp - inner)).astype(bf16)
                dv[...] += dot_tn(probs.astype(bf16), grad)
                dk[...] += dot_tn(ds, qkv[t, rows, part(h, 0)])
                slp[t, rows, part(h, 0)] = (dot_nn(ds, key) * 0.125).astype(bf16)
                run_at(slots, (t * heads + h) * per_head, i)
                return carry

            lax.fori_loop(0, full // QB, block, 0)
            slp[t, :, part(h, 1)] = (dk[...] * 0.125).astype(bf16)
            slp[t, :, part(h, 2)] = dv[...].astype(bf16)
    if not placed:

        def slow_mix(s):
            step_of(mix_chain, s)

        def slow_big(s):
            big_step(s)
            for h in range(heads):
                step_of(qkv_chains[h], s)

        of_chunk(order[2], out_half)
        out_last()
        all_steps(slow_mix)
        x_m.start()
        for g in (0, 1):
            inn_half(g, 0)
            inn_half(g, 1)
            inn_other(g)
        reloaded()
        of_chunk(order[-1], out_half)
        for g in (0, 1):
            quarters(g)
        mix_end()
        ig_of(0)
        ig_chip(0)
        first_big()
        for h in range(heads):
            head_weights(h)
        all_steps(slow_big)
        q_x(0).start()
        big_own()
        big_on()

    dbias = jnp.zeros((1, 3 * n), f32)
    for t in range(trees):
        dbias = dbias + jnp.sum(slp[t, :, : 3 * n].astype(f32), axis=0, keepdims=True)
    gap = jnp.zeros((1, width - n), f32)
    mine = [
        jnp.concatenate([dbias[:, part(h, i)] for h in range(heads)] + [gap], axis=1) for i in (0, 2)
    ]
    mine = pltpu.roll(jnp.concatenate(mine + [jnp.zeros((6, width), f32)], axis=0), q * n, 1)
    v_acc[0:8] = v_acc[0:8] + mine
    v_c = rcopy(v_acc, v_in.at[0], ks.at[2], kr.at[2], p.core)
    v_x = rcopy(v_acc, v_in.at[1], vs.at[0], vr.at[0], p.xnb)
    v_y = rcopy(v_acc, v_in.at[2], vs.at[1], vr.at[1], p.ynb)
    def vcopy(way, s, b):
        dev = p.right if way == 0 else p.left
        return rcopy(v_z.at[b], v_z.at[b], bs.at[6, way, s], br.at[6, way, s], dev)

    def v_send(s):
        for way in (0, 1):
            ok, b = spread_send(way, s, z, nz)

            @pl.when(both(ok, s <= nz - 1))
            def _():
                vcopy(way, s, b).start()

    def v_get(s):
        for way in (0, 1):
            ok, b = spread_get(way, s, z, nz)

            @pl.when(ok)
            def _():
                vcopy(way, s, b).wait_recv()

        v_send(s + 1)

    v_c.start()
    if placed:
        head_weights(2)
    v_c.wait()
    v_acc[...] = v_acc[...] + v_in[0]
    v_x.start()
    ig_of(1)
    if placed:
        head_step(0, 2)
    v_x.wait()
    v_acc[...] = v_acc[...] + v_in[1]
    v_y.start()
    if placed:
        big_step(3)
        big_own()
    ig_chip(1)
    if placed:
        head_step(1, 1)
    v_y.wait()
    v_acc[...] = v_acc[...] + v_in[2]
    v_z[z] = v_acc[...]
    v_send(1)
    if placed:
        head_step(0, 3)
        q_start(0)
        head_step(2, 1)
    y_m.wait()
    o_mix[:, lanes(c * h2, h2)] = (xm[...].astype(f32) + ym[...].astype(f32)).astype(bf16)
    m_core = rcopy(
        o_mix.at[:, lanes(c * h2, h2)], o_mix.at[:, lanes(c * h2, h2)], es.at[7], er.at[7], p.core
    )
    m_core.start()
    ig_end(0)
    if placed:
        head_step(1, 2)
        v_get(1)
        big_on()
    q_sum(0)
    if placed:
        head_step(2, 2)
        head_step(1, 3)
    q_start(1)
    if placed:
        v_get(2)
        head_step(2, 3)
    q_start(2)
    q_sum(1)
    if placed:
        v_get(3)
    else:
        all_steps(v_get)
    q_sum(2)
    big_end()
    ig_end(1)

    def v_sum(i, carry):
        return carry + v_z[i]

    o_vec[...] = lax.fori_loop(0, nz, v_sum, jnp.zeros(o_vec.shape, f32))
    for h in range(heads):
        q_y(h).wait()
        q_on(h).start()
    for cp in [m_core, put_y] + [q_core(h) for h in range(heads)] + [q_on(h) for h in range(heads)]:
        cp.wait()
    for k in (0, 1):
        own_done(k).wait()
        for part_ in range(4):
            done_core(k, part_).wait()
    for ch in qkv_chains + [mix_chain, inn_chain, out_chain]:
        ch[2]()

    def vdrain(s, carry):
        for way in (0, 1):
            ok, b = spread_send(way, s, z, nz)

            @pl.when(ok)
            def _():
                vcopy(way, s, b).wait_send()

        return carry

    lax.fori_loop(1, nz, vdrain, 0)


def w_heads_of(pw, width):
    return pw[...].reshape(width, pw.shape[2])


def whole(nz, tokens, teacher, seg, valid, par, wq, wk, wv, vectors, mix, inn, out):
    trees, length, width = tokens.shape
    rz, wide = mix.shape[0], inn.shape[1]
    full, count, n = 4 * length, trees * length, width // 4
    heads = n // HD
    h2, w2, w4, w8 = width // 2, wide // 2, wide // 4, wide // 8
    vmem = pl.BlockSpec(memory_space=pltpu.VMEM)
    anyspace = pl.BlockSpec(memory_space=pl.ANY)
    shape = jax.ShapeDtypeStruct
    vec = (16, width)
    most = max(nz, 4)
    return pl.pallas_call(
        functools.partial(whole_body, nz),
        out_shape=(
            shape((count, width), bf16),
            shape((count, width), f32),
            shape((trees * full, width), bf16),
            shape((rz, wide), bf16),
            shape((4 * rz, width), bf16),
            shape((rz, width), bf16),
            shape((heads, 4, rz, 3 * HD), bf16),
            shape((trees, length, width), bf16),
            shape(vec, f32),
        ),
        in_specs=[anyspace] * 2 + [vmem] * 2 + [pl.BlockSpec(memory_space=pltpu.SMEM)] + [anyspace] * 3 + [vmem] * 9 + [anyspace] * 3,
        out_specs=[anyspace] * 5 + [vmem] * 4,
        scratch_shapes=[
            pltpu.SMEM((trees, NSEG), jnp.int32),
            V((trees, 4, length, width), bf16),
            V((trees, full, width), bf16),
            V((width, width), bf16),
            V((nz, rz, wide), bf16),
            V((wide, width), bf16),
            V((nz, rz, 3 * n), bf16),
            V((trees, full, 3 * n), bf16),
            V((trees, full, 8), f32),
            V((trees, full, 4 * HD), bf16),
            V((trees, full, n), bf16),
            V((4, trees, length, n), bf16),
            V((count, width), bf16),
            V((count, width), f32),
            V((count, width), f32),
            V((count, width), f32),
            V((count, width), bf16),
            V((count, width), bf16),
            V((count, width), bf16),
            V((count, width), bf16),
            V((count, 128), f32),
            V((count, 128), f32),
            V((width, width), bf16),
            V((trees, full, n), bf16),
            V((full, HD), f32),
            V((full, HD), f32),
            V((nz, rz, w2), bf16),
            V((nz, 4 * rz, h2), bf16),
            V((width, h2), bf16),
            V((2, trees, length, width), bf16),
            V((nz, rz, w4), bf16),
            V((nz, 2 * rz, h2), bf16),
            V((nz, rz, w8), bf16),
            V((nz, rz, h2), bf16),
            V((trees, length, width), bf16),
            V((2, nz, rz, w8), bf16),
            V((2, nz, rz, h2), bf16),
            V((2, nz, rz, h2), bf16),
            V((heads, 2, nz, rz, 3 * HD), bf16),
            V((heads, nz, rz, 3 * HD), bf16),
            V((rz, h2), bf16),
            V((rz, h2), bf16),
            V((heads, rz, 3 * HD), bf16),
            V((3,) + vec, f32),
            V((nz,) + vec, f32),
            V(vec, f32),
            V((nz, 16, width), bf16),
            V((nz, 8, wide), bf16),
            V((4, 8, count), jnp.int32),
            V(vec, f32),
            V((8, wide), f32),
            DMA((8,)), DMA((trees, 4)), DMA((trees * 4,)),
            DMA((3 + 3 * trees,)), DMA((3 + 3 * trees,)),
            DMA((6, 2, nz)), DMA((6, 2, nz)),
            DMA((2, 3, nz)), DMA((2, 3, nz)),
            DMA((3, 4, nz)), DMA((3, 4, nz)),
            DMA((trees, 3)), DMA((trees, 3)),
            DMA((3,)), DMA((3,)),
            DMA((5,)), DMA((5,)),
            DMA((2, most)), DMA((2, most)),
            DMA((3, nz)), DMA((3, nz)),
            DMA((2, nz)), DMA((2, nz)),
            DMA((3, trees)), DMA((3, trees)),
            DMA((2, 7)), DMA((2, 7)),
            DMA((7, 2, nz)), DMA((7, 2, nz)),
            DMA((25,)), DMA((25,)),
            DMA((2,)), DMA((2,)),
        ],
        compiler_params=pltpu.CompilerParams(
            collective_id=1, has_side_effects=True, vmem_limit_bytes=VMEM_LIMIT
        ),
        name="whole",
    )(tokens, teacher, seg, valid, par, wq, wk, wv, *vectors, mix, inn, out)


def finish_body(
    slots, spot, h_inn, h_out, h_mix, h_qkv, h_ig, h_one, vec,
    o_inn, o_out, o_mix, o_q, o_k, o_v, o_ig,
    inn, out, mix, qkv, ig, one, b_inn, b_out, b_mix, b_q, b_k, b_v, b_ig, get, put,
):
    sources = ((h_inn, inn), (h_out, out), (h_one, one), (h_ig, ig), (h_qkv, qkv), (h_mix, mix))
    loads = [pltpu.make_async_copy(a, b, get.at[i]) for i, (a, b) in enumerate(sources)]
    for cp in loads:
        cp.start()
    scale = slots / vec[spot : spot + 1, 0:1]
    stores = []

    def send(buf, dst):
        cp = pltpu.make_async_copy(buf, dst, put.at[len(stores)])
        cp.start()
        stores.append(cp)

    def each(size, fn):
        step = 64 if size % 64 == 0 else size

        def part(i, carry):
            fn(pl.ds(pl.multiple_of(i * step, step), step))
            return carry

        lax.fori_loop(0, size // step, part, 0)

    def scaled(dst, src):
        def part(rows):
            dst[rows] = src[rows].astype(f32) * scale

        each(src.shape[0], part)

    loads[0].wait()
    scaled(b_inn, inn)
    send(b_inn, o_inn)
    loads[1].wait()
    scaled(b_out, out)
    send(b_out, o_out)
    loads[2].wait()
    loads[3].wait()
    for t in range(ig.shape[0]):

        def part(rows):
            b_ig[t, rows] = (one[t, rows] + ig[t, rows].astype(f32)) * scale

        each(ig.shape[1], part)
    send(b_ig, o_ig)
    loads[4].wait()
    for i, (buf, dst) in enumerate(((b_q, o_q), (b_k, o_k), (b_v, o_v))):
        for j in range(4):
            for h in range(qkv.shape[0]):
                at = (j * qkv.shape[0] + h) * HD
                buf[:, at : at + HD] = qkv[h, j, :, i * HD : (i + 1) * HD].astype(f32) * scale
        send(buf, dst)
    loads[5].wait()
    scaled(b_mix, mix)
    send(b_mix, o_mix)
    for cp in stores:
        cp.wait()


def finish(slots, spot, inn, out, mix, qkv, ig, one, vec):
    vmem = pl.BlockSpec(memory_space=pltpu.VMEM)
    anyspace = pl.BlockSpec(memory_space=pl.ANY)
    shapes = [inn.shape, out.shape, mix.shape, mix.shape, mix.shape, mix.shape, ig.shape]
    return pl.pallas_call(
        functools.partial(finish_body, slots, spot),
        out_shape=tuple(jax.ShapeDtypeStruct(sh, f32) for sh in shapes),
        in_specs=[anyspace] * 6 + [vmem],
        out_specs=[anyspace] * 7,
        scratch_shapes=[V(a.shape, a.dtype) for a in (inn, out, mix, qkv, ig, one)]
        + [V(sh, f32) for sh in shapes]
        + [DMA((6,)), DMA((7,))],
        compiler_params=pltpu.CompilerParams(vmem_limit_bytes=VMEM_LIMIT),
        name="finish",
    )(inn, out, mix, qkv, ig, one, vec)


def per_device(
    nz,
    tokens, teacher, seg_ids, parent_seg, valid,
    query_weight, query_bias, key_weight, value_weight, value_bias,
    mix_weight, mix_bias, first_gain, first_shift,
    inner_weight, inner_bias, outer_weight, outer_bias, second_gain, second_shift,
):
    trees, local_len, width = tokens.shape
    n_seq = lax.axis_size("seq")
    row_count = trees * local_len
    total_slots = row_count * lax.axis_size("replica") * nz * n_seq
    rz = mix_weight.shape[0]
    wide = inner_weight.shape[1]

    vectors = (
        query_bias, value_bias, mix_bias, first_gain, first_shift, outer_bias, second_gain, second_shift, inner_bias
    )

    layer_out, grad_one, _, r_inn, r_out, r_mix, r_qkv, r_ig, r_vec = whole(
        nz, tokens, teacher.reshape(row_count, width), seg_ids, valid, parent_seg,
        query_weight, key_weight, value_weight, vectors, mix_weight, inner_weight, outer_weight,
    )
    layer_out = layer_out.reshape(trees, local_len, width)
    flat = r_vec.reshape(-1)
    spot = 8 + wide // width
    count = r_vec[spot + 1, 0]
    scale = total_slots / count
    loss_value = jnp.sum(r_vec[spot]) / count
    shard = lax.axis_index("shard")

    def vec_out(i):
        return lax.dynamic_slice_in_dim(flat, i * width + shard * rz, rz, axis=0) * scale

    size = inner_bias.shape[0]
    dinner_bias = lax.dynamic_slice_in_dim(flat, 8 * width + shard * size, size, axis=0) * scale

    dinner, douter, dmix, dquery, dkey, dvalue, input_grad = finish(
        total_slots, spot + 1, r_inn, r_out, r_mix, r_qkv, r_ig,
        grad_one.reshape(trees, local_len, width), r_vec,
    )
    return (
        layer_out, loss_value, input_grad,
        dquery, vec_out(0), dkey, dvalue, vec_out(1),
        dmix, vec_out(2), vec_out(3), vec_out(4),
        dinner, dinner_bias, douter, vec_out(5), vec_out(6), vec_out(7),
    )


def solution(mesh):
    rows = P(("replica", "shard"), "seq", None)
    line = P(("replica", "shard"), "seq")
    mat = P("shard", None)
    row = P("shard")
    placed = (
        rows, rows, line, P(("replica", "shard"), None), line,
        mat, row, mat, mat, row, mat, row, row, row, mat, row, mat, row, row, row,
    )
    return jax.shard_map(
        functools.partial(per_device, mesh.shape["shard"]),
        mesh=mesh,
        in_specs=placed,
        out_specs=(
            rows, P(), rows,
            mat, row, mat, mat, row, mat, row, row, row, mat, row, mat, row, row, row,
        ),
        check_vma=False,
    )
```

```python
import functools

import jax
import jax.numpy as jnp
from jax import lax
from jax.experimental import pallas as pl
from jax.experimental.pallas import tpu as pltpu
from jax.sharding import PartitionSpec as P

HEADS = 12
HD = 64
NSEG = 8
MESH = pl.DeviceIdType.MESH
BIG = 1e30
norm_eps = 1e-12
f32 = jnp.float32
bf16 = jnp.bfloat16
VMEM_LIMIT = 63 * 1024 * 1024


class Place:
    def __init__(self, nz):
        self.nz = nz
        self.x = lax.axis_index("replica")
        self.z = lax.axis_index("shard")
        self.q = lax.axis_index("seq")
        self.y = self.q // 2
        self.c = self.q % 2
        x, z, y, c = self.x, self.z, self.y, self.c
        self.core = (x, z, 2 * y + 1 - c)
        self.ynb = (x, z, 2 * (1 - y) + c)
        self.xnb = (1 - x, z, self.q)
        self.right = (x, z + 1, self.q)
        self.left = (x, z - 1, self.q)

    def greet(self, more):
        bar = pltpu.get_barrier_semaphore()
        for peer in [self.core, self.ynb, self.xnb] + more:
            pl.semaphore_signal(bar, inc=1, device_id=peer, device_id_type=MESH)

        @pl.when(self.z > 0)
        def _():
            pl.semaphore_signal(bar, inc=1, device_id=self.left, device_id_type=MESH)

        @pl.when(self.z < self.nz - 1)
        def _():
            pl.semaphore_signal(bar, inc=1, device_id=self.right, device_id_type=MESH)

        peers = 3 + len(more) + (self.z > 0).astype(jnp.int32) + (self.z < self.nz - 1).astype(jnp.int32)
        pl.semaphore_wait(bar, peers)


def rcopy(src, dst, ssem, rsem, dev):
    return pltpu.make_async_remote_copy(
        src_ref=src, dst_ref=dst, send_sem=ssem, recv_sem=rsem, device_id=dev, device_id_type=MESH
    )


def both(a, b):
    return jnp.logical_and(a, b)


def dot_nt(a, b):
    return lax.dot_general(a, b, (((1,), (1,)), ((), ())), preferred_element_type=f32)


def dot_tn(a, b):
    return lax.dot_general(a, b, (((0,), (0,)), ((), ())), preferred_element_type=f32)


def dot_nn(a, b):
    return jnp.dot(a, b, preferred_element_type=f32)


def add_to(dst, src):
    dst[...] = (dst[...].astype(f32) + src[...].astype(f32)).astype(dst.dtype)


def lanes(start, size):
    return pl.ds(pl.multiple_of(start, 128), size)


def rows_at(start, size):
    return pl.ds(pl.multiple_of(start, 8), size)


def row_mean(v):
    return jnp.sum(v, axis=1, keepdims=True) * (1.0 / v.shape[1])


def norm_back(grad_hat, hat, inv):
    return inv * (grad_hat - row_mean(grad_hat) - hat * row_mean(grad_hat * hat))


def fold(v):
    return jnp.sum(v.reshape(v.shape[0] // 8, 8, v.shape[1]), axis=0)


def total_row(v):
    return jnp.sum(v, axis=0, keepdims=True)


QB = 256
RB = 32
DMA = pltpu.SemaphoreType.DMA
V = pltpu.VMEM


def spread_send(way, s, z, nz):
    if way == 0:
        return both(z >= s - 1, z < nz - 1), z - s + 1
    return both(z <= nz - s, z > 0), z + s - 1


def spread_get(way, s, z, nz):
    if way == 0:
        return z >= s, z - s
    return z <= nz - 1 - s, z + s


def whole_body(
    nz, x_hbm, tea_hbm, seg_ref, valid_ref, par_ref, wq_hbm, wk_hbm, wv_hbm, *more,
):
    vectors, (mix_hbm, inn_hbm, out_hbm) = more[:9], more[9:12]
    (
        y_hbm, one_hbm, xa_hbm, o_inn, o_out, o_mix, o_qkv, o_ig, o_vec, bits, hid, slp, mixa, inna, outa, pw, qkv,
        lse, feat, att, blocks, tok, A1, A2, A3, fl, gb, gp, tea, vm, inv1, mixg, gsend, gat, dk, dv, ci, co, cm, cg, xi, yo,
        yi, xo, yg, zi, zo, zm, zq, aq, xm, ym, xq, v_in, v_z, v_acc, sma, tga, vecs, loc, sav, rel, px, pr2, xs,
        xr, zs, zr, fs, fr, cs, cr, hs, hr, gs_, gr_, ks, kr, ds_, dr_, s1, r1, s2, r2, is_, ir, ps, pr, bs, br, es, er, vs, vr,
    ) = more[12:]
    p = Place(nz)
    z, c, y, x, q = p.z, p.c, p.y, p.x, p.q
    rz, width = mix_hbm.shape
    wide = inn_hbm.shape[1]
    trees, length = x_hbm.shape[0], x_hbm.shape[1]
    full = qkv.shape[1]
    count = trees * length
    n = width // 4
    heads = n // HD
    chunks = wide // width
    h2, w2, w4, w8 = width // 2, wide // 2, wide // 4, wide // 8
    cross = (x, z, 2 * (1 - y) + 1 - c)
    qy = 2 * (1 - y) + c
    o4 = 4 * rz

    load = [
        pltpu.make_async_copy(x_hbm, hid.at[:, q], loc.at[0]),
        pltpu.make_async_copy(wq_hbm, slp.at[0, pl.ds(0, rz)], loc.at[1]),
        pltpu.make_async_copy(wk_hbm, slp.at[0, pl.ds(256, rz)], loc.at[2]),
        pltpu.make_async_copy(wv_hbm, slp.at[0, pl.ds(512, rz)], loc.at[3]),
        pltpu.make_async_copy(mix_hbm, mixa.at[rows_at(z * rz, rz)], loc.at[4]),
        pltpu.make_async_copy(inn_hbm, inna.at[z], loc.at[5]),
        pltpu.make_async_copy(out_hbm, outa.at[rows_at(z * o4, o4)], loc.at[6]),
        pltpu.make_async_copy(tea_hbm, tea, loc.at[7]),
    ]
    for cp in load:
        cp.start()
    for t in range(trees):
        seg = seg_ref[t : t + 1, :]
        tga[q, 0:1, t * length : (t + 1) * length] = jnp.where(
            valid_ref[t : t + 1, :] == 1, seg, seg + NSEG
        )
    p.greet([cross])

    def x_core(t):
        return rcopy(hid.at[t, q], hid.at[t, q], xs.at[2 + t], xr.at[2 + t], p.core)

    def x_y(t):
        return rcopy(hid.at[t, q], hid.at[t, q], xs.at[2 + trees + t], xr.at[2 + trees + t], p.ynb)

    def x_on(t):
        return rcopy(hid.at[t, qy], hid.at[t, qy], xs.at[2 + 2 * trees + t], xr.at[2 + 2 * trees + t], p.core)

    t_core = rcopy(tga.at[q], tga.at[q], xs.at[0], xr.at[0], p.core)
    t_y = rcopy(tga.at[q], tga.at[q], xs.at[1], xr.at[1], p.ynb)
    t_on = rcopy(tga.at[qy], tga.at[qy], xs.at[2 + 3 * trees], xr.at[2 + 3 * trees], p.core)
    t_y.start()
    t_core.start()
    load[0].wait()
    for t in range(trees):
        x_y(t).start()
    for t in range(trees):
        x_core(t).start()

    parts, rows_in = pw.shape[1], pw.shape[2]
    back = lax.rem(width - q * n, width)
    for i in range(3):
        load[1 + i].wait()
        turned = pltpu.roll(slp[0, i * 256 : i * 256 + rz].astype(f32), back, 1)
        for h in range(heads):
            for half in range(parts):
                own = turned[half * rows_in : (half + 1) * rows_in, h * HD : (h + 1) * HD]
                pw[z, half, :, (3 * h + i) * HD : (3 * h + i + 1) * HD] = own.astype(bf16)
    def row_of(ref, size):
        own = ref[...].astype(f32).reshape(1, ref.shape[0])
        if ref.shape[0] == size:
            return own
        return jnp.concatenate([own, jnp.zeros((1, size - ref.shape[0]), f32)], axis=1)

    small = jnp.concatenate([row_of(v, width) for v in vectors[:8]], axis=0)
    wide_row = jnp.concatenate([row_of(vectors[8], wide), jnp.zeros((7, wide), f32)], axis=0)
    wide_row = pltpu.roll(wide_row, z * (wide // nz), 1)
    sma[z] = jnp.concatenate(
        [pltpu.roll(small, z * rz, 1)]
        + [wide_row[0:1, j * width : (j + 1) * width] for j in range(chunks)]
        + [jnp.zeros((8 - chunks, width), f32)],
        axis=0,
    ).astype(bf16)

    def at_row(ref, b, size):
        return ref.at[rows_at(b * size, size)]

    def piece_of(k, b, xx, yy):
        if k == 0:
            return inna.at[b, :, lanes(c * w2 + (2 * xx + yy) * w8, w8)]
        return outa.at[rows_at(b * o4 + (2 * xx + yy) * rz, rz), lanes(c * h2, h2)]

    there = {
        0: lambda b: pw.at[b, x if parts == 2 else 0],
        1: lambda b: sma.at[b],
        3: lambda b: mixa.at[rows_at(b * rz, rz), lanes(c * h2, h2)],
        4: lambda b: piece_of(0, b, x, y),
        5: lambda b: piece_of(1, b, x, y),
    }

    def zcopy(k, way, s, b):
        dev = p.right if way == 0 else p.left
        return rcopy(there[k](b), there[k](b), zs.at[k, way, s], zr.at[k, way, s], dev)

    def start_step(k, s):
        for way in (0, 1):
            cond, b = spread_send(way, s, z, nz)

            @pl.when(both(cond, s <= nz - 1))
            def _():
                zcopy(k, way, s, b).start()

    def each(s, fn):
        for way in (0, 1):
            cond, b = spread_get(way, s, z, nz)

            @pl.when(cond)
            def _():
                fn(way, b)

    def take(k, s):
        each(s, lambda way, b: zcopy(k, way, s, b).wait_recv())

    def to_y(k, b):
        return rcopy(piece_of(k, b, x, y), piece_of(k, b, x, y), fs.at[k, 0, b], fr.at[k, 0, b], p.ynb)

    def to_x(k, b):
        return rcopy(piece_of(k, b, x, y), piece_of(k, b, x, y), fs.at[k, 1, b], fr.at[k, 1, b], p.xnb)

    def onward(k, b):
        return rcopy(piece_of(k, b, x, 1 - y), piece_of(k, b, x, 1 - y), fs.at[k, 2, b], fr.at[k, 2, b], p.xnb)

    def core_copy(k, b, part):
        if k == 2:
            piece = there[3](b)
        else:
            piece = piece_of(k, b, x if part % 2 == 0 else 1 - x, y if part < 2 else 1 - y)
        return rcopy(piece, piece, cs.at[k, part, b], cr.at[k, part, b], p.core)

    def pw_x(b):
        return rcopy(pw.at[b, x], pw.at[b, x], px.at[b], pr2.at[b], p.xnb)

    for k in (0, 1):
        start_step(k, 1)

    def small_step(s, carry):
        for k in (0, 1):
            take(k, s)
        for k in (0, 1):
            start_step(k, s + 1)
        if parts == 2:
            each(s, lambda way, b: pw_x(b).start())
        return carry

    lax.fori_loop(1, nz - 1, small_step, 0)
    for i in (4, 5, 6, 7):
        load[i].wait()
    for k in (4, 3, 5):
        start_step(k, 1)
    for k in (0, 1):
        take(k, nz - 1)
    if parts == 2:
        each(nz - 1, lambda way, b: pw_x(b).start())

    def mix_step(s):
        def got(way, b):
            zcopy(3, way, s, b).wait_recv()
            core_copy(2, b, 0).start()

        each(s, got)
        start_step(3, s + 1)

    def z_step(k, s):
        def got(way, b):
            zcopy(4 + k, way, s, b).wait_recv()
            to_y(k, b).start()
            if k == 0:
                to_x(k, b).start()

        each(s, got)
        start_step(4 + k, s + 1)
        each(s, lambda way, b: core_copy(k, b, 0).start())

    def pass_on(k, s):
        def got(way, b):
            to_y(k, b).wait_recv()
            if k == 1:
                to_x(k, b).start()
            onward(k, b).start()
            core_copy(k, b, 2).start()

        each(s, got)

    def rest_of(k, s):
        def got(way, b):
            to_x(k, b).wait_recv()
            core_copy(k, b, 1).start()
            onward(k, b).wait_recv()
            core_copy(k, b, 3).start()

        each(s, got)

    def from_core(k, s):
        def got(way, b):
            for part in range(4 if k < 2 else 1):
                core_copy(k, b, part).wait_recv()

        each(s, got)

    def all_steps(*fns):
        def one(s, carry):
            for fn in fns:
                fn(s)
            return carry

        lax.fori_loop(1, nz, one, 0)

    placed = nz == 4

    small = lax.fori_loop(0, nz, lambda i, v: v + sma[i].astype(f32), jnp.zeros(vecs.shape, f32))
    vecs[...] = small
    turned = pltpu.roll(small, back, 1)
    bias = []
    for h in range(heads):
        cols = slice(h * HD, (h + 1) * HD)
        bias += [turned[0:1, cols], jnp.zeros((1, HD), f32), turned[1:2, cols]]
    bias = jnp.concatenate(bias, axis=1)

    t_y.wait_recv()
    t_on.start()
    t_core.wait()
    t_on.wait()

    row = lax.broadcasted_iota(jnp.int32, (16, 4 * HD), 0)
    lane = lax.broadcasted_iota(jnp.int32, (16, 4 * HD), 1)
    trow = lax.broadcasted_iota(jnp.int32, (16, full), 0)
    vrow = lax.broadcasted_iota(jnp.int32, (16, length), 0)
    ones = jnp.ones((16, 128), bf16)
    for t in range(trees):
        bits[t, 0] = jnp.int32(1)
        for s in range(1, NSEG):
            bits[t, s] = bits[t, par_ref[t, s]] + (1 << s)
        seen = jnp.zeros((16, 4 * HD), jnp.int32)
        for a in range(NSEG):
            seen = jnp.where(row == a, bits[t, a], seen)
        at = jnp.clip(lane - HD, 0, NSEG)
        unseen = ((seen >> at) & 1) == 0
        q_side = both(both(row < NSEG, both(lane >= HD, lane <= HD + NSEG)), unseen)
        k_side = both(row <= NSEG, lane == row + 3 * HD)
        table = jnp.where(q_side, -BIG, jnp.where(k_side, 1.0, 0.0)).astype(bf16)
        tag = jnp.concatenate(
            [tga[j, 0:1, t * length : (t + 1) * length] for j in range(full // length)], axis=1
        )
        gone = tag >= NSEG
        seg = jnp.where(gone, tag - NSEG, tag)
        seg = jnp.broadcast_to(seg, (16, full))
        gone = jnp.broadcast_to(jnp.where(gone, 1, 0), (16, full))
        hot = jnp.where(trow == NSEG, gone, jnp.where(trow == seg, 1, 0)).astype(f32).astype(bf16)
        feat[t] = dot_tn(hot, table).astype(bf16)
        here = jnp.broadcast_to(valid_ref[t : t + 1, :], (16, length))
        here = jnp.where(vrow == 0, here, 0).astype(f32).astype(bf16)
        vm[t * length : (t + 1) * length] = dot_tn(here, ones)

    t_y.wait_send()
    if parts == 2:
        all_steps(lambda s: each(s, lambda way, b: pw_x(b).wait()))
    w_heads = w_heads_of(pw, width)
    saves = []

    def project(t):
        x_core(t).wait()
        x_on(t).wait()
        for j in range(4):
            cp = pltpu.make_async_copy(
                hid.at[t, j], xa_hbm.at[pl.ds((t * 4 + j) * length, length)], sav.at[t, j]
            )
            cp.start()
            saves.append(cp)
        qkv[t] = (dot_nn(hid[t].reshape(full, width), w_heads) + bias).astype(bf16)

    for t in range(trees):
        x_y(t).wait()
        x_on(t).start()
        if t == 0:
            project(0)


    def part(h, i):
        return slice((3 * h + i) * HD, (3 * h + i + 1) * HD)

    def queries_of(t, rows, h):
        return jnp.concatenate([qkv[t, rows, part(h, 0)] * 0.125, feat[t, rows, HD : 2 * HD]], axis=1)

    def keys_of(t, h):
        return jnp.concatenate([qkv[t, :, part(h, 1)], feat[t, :, 3 * HD : 4 * HD]], axis=1)

    def token_rows(j):
        return pl.ds(pl.multiple_of(j * length, length), length)

    def send_heads(t, d):
        to = lax.rem(q + d, 4)
        return rcopy(
            att.at[t, token_rows(to)], blocks.at[q, t], hs.at[t, d - 1], hr.at[t, d - 1], (x, z, to)
        )

    def run_at(slots, first, i):
        for k in range(full // QB):
            fns = slots.get(first + k, [])
            if fns:

                @pl.when(i == k)
                def _():
                    for fn, *args in fns:
                        fn(*args)

    slots = {
        1: [(z_step, 0, 1)],
        5: [(mix_step, 1)],
        9: [(pass_on, 0, 1)],
        12: [(z_step, 0, 2)],
        13: [(z_step, 1, 1)],
        14: [(mix_step, 2)],
        19: [(z_step, 1, 2)],
        20: [(pass_on, 0, 2)],
        22: [(z_step, 0, 3)],
    }
    if not placed:
        slots = {}
    per_head = full // QB
    for t in range(trees):
        if t > 0:
            project(t)
        for h in range(heads):
            keys = keys_of(t, h)
            values = qkv[t, :, part(h, 2)]

            def block(i, carry):
                rows = pl.ds(pl.multiple_of(i * QB, QB), QB)
                s = dot_nt(queries_of(t, rows, h), keys)
                peak = jnp.max(s, axis=1, keepdims=True)
                e = jnp.exp(s - peak)
                total = jnp.sum(e, axis=1, keepdims=True)
                o = dot_nn(e.astype(bf16), values) / total
                att[t, rows, h * HD : (h + 1) * HD] = o.astype(bf16)
                lse[t, rows, h : h + 1] = peak + jnp.log(total)
                run_at(slots, (t * heads + h) * per_head, i)
                return carry

            lax.fori_loop(0, full // QB, block, 0)
        for d in (1, 2, 3):
            send_heads(t, d).start()
    for t in range(trees):
        blocks[q, t] = att[t, token_rows(q)]
    if placed:
        pass_on(1, 1)
        mix_step(3)
        pass_on(0, 3)
    else:
        all_steps(mix_step)
    for t in range(trees):
        for d in (1, 2, 3):
            send_heads(t, d).wait()

    for j in range(4):
        tok[:, j * n : (j + 1) * n] = blocks[j].reshape(count, n)
    all_steps(functools.partial(from_core, 2))
    A3[...] = dot_nn(tok[...], mixa[...])
    if placed:
        z_step(1, 3)
        pass_on(1, 2)
        rest_of(0, 1)
        rest_of(0, 2)

    def rows_of(i):
        return pl.ds(pl.multiple_of(i * RB, RB), RB)

    per = length // RB

    def first_norm(i, carry):
        rows = rows_of(i)
        own = hid[i // per, q, rows_of(i % per)].astype(f32)
        r1 = own + A3[rows] + vecs[2:3]
        center = r1 - row_mean(r1)
        inv = lax.rsqrt(row_mean(center * center) + norm_eps)
        hat = center * inv
        A1[rows] = hat
        inv1[rows] = jnp.broadcast_to(inv, (RB, 128))
        fl[rows] = (hat * vecs[3:4] + vecs[4:5]).astype(bf16)
        return carry

    lax.fori_loop(0, count // RB, first_norm, 0)
    for cp in saves:
        cp.wait()
    if placed:
        pass_on(1, 3)
        rest_of(0, 3)
    else:
        for k in (0, 1):
            all_steps(*[functools.partial(fn, k) for fn in (z_step, pass_on, rest_of)])
    all_steps(functools.partial(from_core, 0))

    def inner_chunk(j):
        return inna[:, :, j * width : (j + 1) * width].reshape(width, width)

    def hid_chunk(j):
        return hid[j // 2, 2 * (j % 2) : 2 * (j % 2) + 2].reshape(count, width)

    for j in range(chunks):
        A3[...] = dot_nn(fl[...], inner_chunk(j))

        def gelu(i, carry):
            rows = rows_of(i)
            pre = A3[rows] + vecs[8 + j : 9 + j]
            cdf = 0.5 + 0.5 * lax.erf(pre * (0.5**0.5))
            hid[j // 2, 2 * (j % 2) + i // per, rows_of(i % per)] = (pre * cdf).astype(bf16)
            slope = cdf + pre * jnp.exp(-0.5 * pre * pre) * 0.3989422804014327
            slp[j // 2, pl.ds(pl.multiple_of((j % 2) * count + i * RB, RB), RB)] = slope.astype(bf16)
            return carry

        lax.fori_loop(0, count // RB, gelu, 0)
        if placed and j == 1:
            rest_of(1, 1)
        if placed and j == 2:
            rest_of(1, 2)
            rest_of(1, 3)
    all_steps(functools.partial(from_core, 1))
    for j in range(chunks):
        more = dot_nn(hid_chunk(j), outa[j * width : (j + 1) * width])
        if j == 0:
            A2[...] = more
        else:
            A2[...] += more

    def drain(s, carry):
        for k in (0, 1, 3, 4, 5):
            for way in (0, 1):
                cond, b = spread_send(way, s, z, nz)

                @pl.when(cond)
                def _():
                    zcopy(k, way, s, b).wait_send()

        def end(way, b):
            core_copy(2, b, 0).wait_send()
            for k in (0, 1):
                to_y(k, b).wait_send()
                to_x(k, b).wait_send()
                onward(k, b).wait_send()
                for part in range(4):
                    core_copy(k, b, part).wait_send()

        each(s, end)
        return carry

    lax.fori_loop(1, nz, drain, 0)

    zero = jnp.zeros((8, width), f32)

    def second_norm(i, carry):
        loss, dgain, dshift, dbias = carry
        rows = rows_of(i)
        first = A1[rows] * vecs[3:4] + vecs[4:5]
        r2 = first + A2[rows] + vecs[5:6]
        center = r2 - row_mean(r2)
        inv = lax.rsqrt(row_mean(center * center) + norm_eps)
        hat = center * inv
        out = hat * vecs[6:7] + vecs[7:8]
        err = out - tea[rows].astype(f32)
        tea[rows] = out.astype(bf16)
        weighted = vm[rows, 0:1] * err
        grad = 2.0 * weighted
        g2 = norm_back(grad * vecs[6:7], hat, inv)
        A2[rows] = g2
        low = g2.astype(bf16)
        gb[rows] = low
        return (
            loss + fold(weighted * err),
            dgain + fold(grad * hat),
            dshift + fold(grad),
            dbias + fold(low.astype(f32)),
        )

    loss, dgain, dshift, dbias = lax.fori_loop(0, count // RB, second_norm, (zero, zero, zero, zero))
    put_y = pltpu.make_async_copy(tea, y_hbm, loc.at[0])
    put_y.start()
    v_acc[...] = jnp.zeros_like(v_acc)
    spot = 8 + chunks
    v_acc[5:6] = total_row(dbias)
    v_acc[6:7] = total_row(dgain)
    v_acc[7:8] = total_row(dshift)
    v_acc[spot : spot + 1] = total_row(loss)
    v_acc[spot + 1 : spot + 2, 0:128] = total_row(vm[...])

    def c_out(d):
        return rcopy(outa.at[rows_at(d * o4, o4), lanes((1 - c) * h2, h2)], co.at[d], ds_.at[0, d], dr_.at[0, d], p.core)

    def chunk_of(core, k):
        return (chunks - 1) * core + (1 - 2 * core) * k

    def c_inn(k):
        src = inna.at[:, :, lanes(chunk_of(1 - c, k) * width, width)]
        return rcopy(src, ci.at[:, :, pl.ds(k * width, width)], ds_.at[1, k], dr_.at[1, k], p.core)

    def out_y(d):
        src = co.at[d, rows_at((1 - y) * 2 * rz, 2 * rz)]
        return rcopy(src, yo.at[d], s1.at[0, d], r1.at[0, d], p.ynb)

    def inn_x(d, k):
        src = ci.at[d, :, lanes(k * width + (1 - x) * w8, w8)]
        return rcopy(src, xi.at[d, :, pl.ds(k * w8, w8)], s1.at[1 + k, d], r1.at[1 + k, d], p.xnb)

    def out_x(d):
        src = yo.at[d, rows_at((1 - x) * rz, rz)]
        return rcopy(src, xo.at[d], s2.at[0, d], r2.at[0, d], p.xnb)

    def inn_y(d):
        return rcopy(xi.at[d, :, lanes((1 - y) * w8, w8)], yi.at[d], s2.at[1, d], r2.at[1, d], p.ynb)

    def span(lo, hi, fn):
        if hi - lo == 1:
            fn(lo)
            return

        def one(i, carry):
            fn(i)
            return carry

        lax.fori_loop(lo, hi, one, 0)

    def of_chunk(j, fn):
        span(j * nz // chunks, (j + 1) * nz // chunks, fn)

    def group(g, fn):
        def pair(i):
            fn(nz - 1 - i)
            fn(i)

        span(g * nz // 4, (g + 1) * nz // 4, pair)

    def out_chip(d):
        c_out(d).wait()
        for j in range(4):
            add_to(co.at[d, j * rz : (j + 1) * rz], outa.at[rows_at(d * o4 + j * rz, rz), lanes(c * h2, h2)])
        out_y(d).start()

    def inn_chip(g, k):
        if g == 0:
            c_inn(k).wait()

        def one(d):
            for j in range(2):
                at = slice(k * width + j * h2, k * width + (j + 1) * h2)
                add_to(ci.at[d, :, at], inna.at[d, :, lanes(chunk_of(c, k) * width + j * h2, h2)])
            inn_x(d, k).start()

        group(g, one)

    def out_half(d):
        out_y(d).wait()
        add_to(yo.at[d, :rz], co.at[d, rows_at(y * 2 * rz, rz)])
        add_to(yo.at[d, rz:], co.at[d, rows_at(y * 2 * rz + rz, rz)])
        out_x(d).start()

    def inn_half(g, k):
        def one(d):
            inn_x(d, k).wait()
            add_to(xi.at[d, :, k * w8 : (k + 1) * w8], ci.at[d, :, lanes(k * width + x * w8, w8)])

        group(g, one)

    def inn_other(g):
        group(g, lambda d: inn_y(d).start())

    def out_quarter(d):
        out_x(d).wait()
        add_to(xo.at[d], yo.at[d, rows_at(x * rz, rz)])

    def inn_quarter(d):
        inn_y(d).wait()
        add_to(yi.at[d], xi.at[d, :, lanes(y * w8, w8)])

    order = [3, 0, 2, 1]
    for step, j in enumerate(order):
        A3[...] = dot_nt(gb[...], outa[j * width : (j + 1) * width])

        def slopes(i, carry):
            rows = rows_of(i)
            slope = slp[j // 2, pl.ds(pl.multiple_of((j % 2) * count + i * RB, RB), RB)]
            low = (A3[rows] * slope.astype(f32)).astype(bf16)
            gp[rows] = low
            return carry + fold(low.astype(f32))

        v_acc[8 + j : 9 + j] = total_row(lax.fori_loop(0, count // RB, slopes, zero))
        outa[j * width : (j + 1) * width] = dot_tn(hid_chunk(j), gb[...]).astype(bf16)
        of_chunk(j, lambda d: c_out(d).start())
        A2[...] += dot_nt(gp[...], inner_chunk(j))
        inna[:, :, j * width : (j + 1) * width] = dot_tn(fl[...], gp[...]).astype(bf16).reshape(nz, rz, width)

        @pl.when(c == 1 - j // 2)
        def _():
            c_inn(step // 2).start()

        if step == 1:
            of_chunk(order[0], out_chip)
        if step == 2:
            inn_chip(0, 0)
            inn_chip(1, 0)

    def first_back(i, carry):
        dgain, dshift, dbias = carry
        rows = rows_of(i)
        grad = A2[rows]
        hat = A1[rows]
        g1 = norm_back(grad * vecs[3:4], hat, inv1[rows, 0:1])
        A2[rows] = g1
        low = g1.astype(bf16)
        gb[rows] = low
        return dgain + fold(grad * hat), dshift + fold(grad), dbias + fold(low.astype(f32))

    dgain, dshift, dbias = lax.fori_loop(0, count // RB, first_back, (zero, zero, zero))
    v_acc[2:3] = total_row(dbias)
    v_acc[3:4] = total_row(dgain)
    v_acc[4:5] = total_row(dshift)
    put_one = pltpu.make_async_copy(A2, one_hbm, loc.at[1])
    put_one.start()

    for j in range(4):
        part_j = dot_nt(gb[...], mixa[j * n : (j + 1) * n]).astype(bf16)
        for t in range(trees):
            gsend[j * length : (j + 1) * length, t * n : (t + 1) * n] = part_j[t * length : (t + 1) * length]

    def send_grads(d):
        to = lax.rem(q + d, 4)
        return rcopy(gsend.at[token_rows(to)], gat.at[token_rows(q)], gs_.at[d - 1], gr_.at[d - 1], (x, z, to))

    for d in (1, 2, 3):
        send_grads(d).start()
    gat[token_rows(q)] = gsend[token_rows(q)]

    of_chunk(order[0], out_half)
    inn_chip(0, 1)
    of_chunk(order[1], out_chip)
    inn_chip(1, 1)
    of_chunk(order[2], out_chip)
    reload = [
        pltpu.make_async_copy(
            xa_hbm.at[pl.ds(i * length, length)], outa.at[pl.ds(i * length, length)], rel.at[i]
        )
        for i in range(trees * 4)
    ]

    def out_last():
        of_chunk(order[-1], out_chip)
        for cp in reload:
            cp.start()

    def reloaded():
        for cp in reload:
            cp.wait()

    mixg[...] = dot_tn(tok[...], gb[...]).astype(bf16)
    c_mix = rcopy(mixg.at[:, lanes((1 - c) * h2, h2)], cm, ks.at[3], kr.at[3], p.core)
    c_mix.start()

    def chain(k, acc, buf):
        def copy(way, s, d):
            dev = p.right if way == 0 else p.left
            return rcopy(acc(d), buf(way, d), bs.at[k, way, s], br.at[k, way, s], dev)

        def sending(way, s):
            if way == 0:
                d = z + nz - s
                return both(d <= nz - 1, z < nz - 1), d
            d = z - nz + s
            return both(d >= 0, z > 0), d

        def getting(way, s):
            if way == 0:
                d = z - 1 + nz - s
                return both(d <= nz - 1, z > 0), d
            d = z + 1 - nz + s
            return both(d >= 0, z < nz - 1), d

        def send(s):
            for way in (0, 1):
                ok, d = sending(way, s)

                @pl.when(both(ok, s <= nz - 1))
                def _():
                    copy(way, s, d).start()

        def get(s):
            for way in (0, 1):
                ok, d = getting(way, s)

                @pl.when(ok)
                def _():
                    copy(way, s, d).wait_recv()
                    add_to(acc(d), buf(way, d))

        def drain(s, carry):
            for way in (0, 1):
                ok, d = sending(way, s)

                @pl.when(ok)
                def _():
                    copy(way, s, d).wait_send()

            return carry

        return send, get, lambda: lax.fori_loop(1, nz, drain, 0)

    def step_of(ch, s):
        ch[1](s)
        ch[0](s + 1)

    mix_chain = chain(3, lambda d: cm.at[rows_at(d * rz, rz)], lambda way, d: zm.at[way, d])
    inn_chain = chain(4, lambda d: yi.at[d], lambda way, d: zi.at[way, d])
    out_chain = chain(5, lambda d: xo.at[d], lambda way, d: zo.at[way, d])

    def head_chain(h):
        return chain(h, lambda d: aq.at[h, d], lambda way, d: zq.at[h, way, d])

    qkv_chains = [head_chain(h) for h in range(heads)]

    c_mix.wait()

    def mix_sum(i, carry):
        block = rows_at(i * rz, rz)
        add_to(cm.at[block], mixg.at[block, lanes(c * h2, h2)])
        return carry

    lax.fori_loop(0, nz, mix_sum, 0)
    mix_chain[0](1)
    for d in (1, 2, 3):
        send_grads(d).wait()

    def head_weights(h):
        cols = slice(3 * h * HD, 3 * (h + 1) * HD)
        grad = dot_tn(outa[0:full], slp[0, :, cols])
        for t in range(1, trees):
            grad = grad + dot_tn(outa[t * full : (t + 1) * full], slp[t, :, cols])
        aq[h] = grad.astype(bf16).reshape(nz, rz, 3 * HD)
        qkv_chains[h][0](1)

    def q_x(h):
        return rcopy(aq.at[h, z], xq.at[h], es.at[13 + h], er.at[13 + h], p.xnb)

    def q_y(h):
        return rcopy(o_qkv.at[h, q], o_qkv.at[h, q], es.at[16 + h], er.at[16 + h], p.ynb)

    def q_core(h):
        return rcopy(o_qkv.at[h, q], o_qkv.at[h, q], es.at[19 + h], er.at[19 + h], p.core)

    def q_on(h):
        return rcopy(o_qkv.at[h, qy], o_qkv.at[h, qy], es.at[22 + h], er.at[22 + h], p.core)

    def q_sum(h):
        q_x(h).wait()
        o_qkv[h, q] = (aq[h, z].astype(f32) + xq[h].astype(f32)).astype(bf16)
        q_y(h).start()
        q_core(h).start()

    x_m = rcopy(cm.at[rows_at(z * rz, rz)], xm, es.at[1], er.at[1], p.xnb)
    y_m = rcopy(xm, ym, es.at[4], er.at[4], p.ynb)

    def big_step(s):
        step_of(inn_chain, s)
        step_of(out_chain, s)

    def first_big():
        inn_chain[0](1)
        out_chain[0](1)

    def ig_of(t):
        for j in range(4):
            rows = slice(j * length, (j + 1) * length)
            hid[t, j] = dot_nt(slp[t, rows, : 3 * n], w_heads_of(pw, width)).astype(bf16)
        for b in range(2):
            c_ig(t, b).start()

    def c_ig(t, b):
        return rcopy(hid.at[t, 2 * b + 1 - c], cg.at[b, t], is_.at[b, t], ir.at[b, t], p.core)

    def ig_y(t):
        return rcopy(cg.at[1 - y, t], yg.at[t], is_.at[2, t], ir.at[2, t], p.ynb)

    def ig_chip(t):
        for b in range(2):
            c_ig(t, b).wait()
            add_to(cg.at[b, t], hid.at[t, 2 * b + c])
        ig_y(t).start()

    def ig_end(t):
        ig_y(t).wait()
        o_ig[t] = (cg[y, t].astype(f32) + yg[t].astype(f32)).astype(o_ig.dtype)

    def done_piece(k, xx, yy):
        if k == 0:
            return o_inn.at[:, lanes(chunk_of(c, yy) * width + xx * w8, w8)]
        return o_out.at[rows_at((2 * yy + xx) * rz, rz), lanes(c * h2, h2)]

    def own_done(k):
        return pltpu.make_async_copy((yi if k == 0 else xo).at[z], done_piece(k, x, y), loc.at[2 + k])

    def done_y(k):
        return rcopy((yi if k == 0 else xo).at[z], done_piece(k, x, y), ps.at[k, 0], pr.at[k, 0], p.ynb)

    def done_x(k):
        return rcopy((yi if k == 0 else xo).at[z], done_piece(k, x, y), ps.at[k, 1], pr.at[k, 1], p.xnb)

    def done_on(k):
        return rcopy(done_piece(k, x, 1 - y), done_piece(k, x, 1 - y), ps.at[k, 2], pr.at[k, 2], p.xnb)

    def done_core(k, part):
        piece = done_piece(k, x if part % 2 == 0 else 1 - x, y if part < 2 else 1 - y)
        src = (yi if k == 0 else xo).at[z] if part == 0 else piece
        return rcopy(src, piece, ps.at[k, 3 + part], pr.at[k, 3 + part], p.core)

    def big_own():
        for k in (0, 1):
            own_done(k).start()
            done_y(k).start()
            done_x(k).start()
            done_core(k, 0).start()

    def big_on():
        for k in (0, 1):
            done_y(k).wait()
            done_on(k).start()
            done_core(k, 2).start()

    def big_end():
        for k in (0, 1):
            done_x(k).wait()
            done_core(k, 1).start()
        for k in (0, 1):
            done_on(k).wait()
            done_core(k, 3).start()

    def mix_end():
        x_m.wait()
        add_to(xm, cm.at[rows_at(z * rz, rz)])
        y_m.start()

    def quarters(g):
        group(g, out_quarter)
        group(g, inn_quarter)

    def head_step(h, s):
        step_of(qkv_chains[h], s)

    def q_start(h):
        q_x(h).start()

    slots = {
        0: [(inn_half, 0, 0), (inn_half, 1, 0)],
        3: [(of_chunk, order[1], out_half)],
        4: [(inn_half, 0, 1), (inn_other, 0), (out_last,)],
        5: [(step_of, mix_chain, 1)],
        7: [(of_chunk, order[2], out_half)],
        8: [(inn_half, 1, 1), (inn_other, 1)],
        9: [(group, 0, out_quarter)],
        10: [(group, 0, inn_quarter), (first_big,)],
        12: [(ig_of, 0)],
        13: [(of_chunk, order[-1], out_half)],
        14: [(ig_chip, 0), (step_of, mix_chain, 2)],
        16: [(quarters, 1), (big_step, 1)],
        17: [(reloaded,), (head_weights, 0)],
        20: [(head_weights, 1)],
        21: [(head_step, 0, 1), (big_step, 2)],
        22: [(step_of, mix_chain, 3), (lambda: x_m.start(),)],
        23: [(head_step, 0, 2), (head_step, 1, 1)],
    }
    if not placed:
        slots = {}
    put_one.wait()
    for t in range(trees):
        for h in range(heads):
            key = qkv[t, :, part(h, 1)]
            keys = keys_of(t, h)
            values = qkv[t, :, part(h, 2)]
            dk[...] = jnp.zeros_like(dk)
            dv[...] = jnp.zeros_like(dv)

            def block(i, carry):
                rows = pl.ds(pl.multiple_of(i * QB, QB), QB)
                s = dot_nt(queries_of(t, rows, h), keys)
                probs = jnp.exp(s - lse[t, rows, h : h + 1])
                grad = gat[rows, t * n + h * HD : t * n + (h + 1) * HD]
                dp = dot_nt(grad, values)
                inner = jnp.sum(probs * dp, axis=1, keepdims=True)
                ds = (probs * (dp - inner)).astype(bf16)
                dv[...] += dot_tn(probs.astype(bf16), grad)
                dk[...] += dot_tn(ds, qkv[t, rows, part(h, 0)])
                slp[t, rows, part(h, 0)] = (dot_nn(ds, key) * 0.125).astype(bf16)
                run_at(slots, (t * heads + h) * per_head, i)
                return carry

            lax.fori_loop(0, full // QB, block, 0)
            slp[t, :, part(h, 1)] = (dk[...] * 0.125).astype(bf16)
            slp[t, :, part(h, 2)] = dv[...].astype(bf16)
    if not placed:

        def slow_mix(s):
            step_of(mix_chain, s)

        def slow_big(s):
            big_step(s)
            for h in range(heads):
                step_of(qkv_chains[h], s)

        of_chunk(order[1], out_half)
        of_chunk(order[2], out_half)
        out_last()
        all_steps(slow_mix)
        x_m.start()
        for g in (0, 1):
            inn_half(g, 0)
            inn_half(g, 1)
            inn_other(g)
        reloaded()
        of_chunk(order[-1], out_half)
        for g in (0, 1):
            quarters(g)
        mix_end()
        ig_of(0)
        ig_chip(0)
        first_big()
        for h in range(heads):
            head_weights(h)
        all_steps(slow_big)
        q_x(0).start()
        big_own()
        big_on()

    dbias = jnp.zeros((1, 3 * n), f32)
    for t in range(trees):
        dbias = dbias + jnp.sum(slp[t, :, : 3 * n].astype(f32), axis=0, keepdims=True)
    gap = jnp.zeros((1, width - n), f32)
    mine = [
        jnp.concatenate([dbias[:, part(h, i)] for h in range(heads)] + [gap], axis=1) for i in (0, 2)
    ]
    mine = pltpu.roll(jnp.concatenate(mine + [jnp.zeros((6, width), f32)], axis=0), q * n, 1)
    v_acc[0:8] = v_acc[0:8] + mine
    v_c = rcopy(v_acc, v_in.at[0], ks.at[2], kr.at[2], p.core)
    v_x = rcopy(v_acc, v_in.at[1], vs.at[0], vr.at[0], p.xnb)
    v_y = rcopy(v_acc, v_in.at[2], vs.at[1], vr.at[1], p.ynb)
    def vcopy(way, s, b):
        dev = p.right if way == 0 else p.left
        return rcopy(v_z.at[b], v_z.at[b], bs.at[6, way, s], br.at[6, way, s], dev)

    def v_send(s):
        for way in (0, 1):
            ok, b = spread_send(way, s, z, nz)

            @pl.when(both(ok, s <= nz - 1))
            def _():
                vcopy(way, s, b).start()

    def v_get(s):
        for way in (0, 1):
            ok, b = spread_get(way, s, z, nz)

            @pl.when(ok)
            def _():
                vcopy(way, s, b).wait_recv()

        v_send(s + 1)

    v_c.start()
    if placed:
        head_weights(2)
    v_c.wait()
    v_acc[...] = v_acc[...] + v_in[0]
    v_x.start()
    if placed:
        mix_end()
    ig_of(1)
    v_x.wait()
    v_acc[...] = v_acc[...] + v_in[1]
    v_y.start()
    if placed:
        big_step(3)
        big_own()
        for h in range(heads):
            head_step(h, 3 - h)
        q_start(0)
    ig_chip(1)
    v_y.wait()
    v_acc[...] = v_acc[...] + v_in[2]
    v_z[z] = v_acc[...]
    v_send(1)
    if placed:
        head_step(1, 3)
        head_step(2, 2)
    q_start(1)
    y_m.wait()
    o_mix[:, lanes(c * h2, h2)] = (xm[...].astype(f32) + ym[...].astype(f32)).astype(bf16)
    m_core = rcopy(
        o_mix.at[:, lanes(c * h2, h2)], o_mix.at[:, lanes(c * h2, h2)], es.at[7], er.at[7], p.core
    )
    m_core.start()
    if placed:
        head_step(2, 3)
    q_start(2)
    if placed:
        big_on()
    ig_end(0)
    q_sum(0)
    q_sum(1)
    if placed:
        v_get(1)
        v_get(2)
    q_sum(2)
    if placed:
        v_get(3)
    else:
        all_steps(v_get)
    big_end()
    ig_end(1)

    def v_sum(i, carry):
        return carry + v_z[i]

    o_vec[...] = lax.fori_loop(0, nz, v_sum, jnp.zeros(o_vec.shape, f32))
    for h in range(heads):
        q_y(h).wait()
        q_on(h).start()
    for cp in [m_core, put_y] + [q_core(h) for h in range(heads)] + [q_on(h) for h in range(heads)]:
        cp.wait()
    for k in (0, 1):
        own_done(k).wait()
        for part_ in range(4):
            done_core(k, part_).wait()
    for ch in qkv_chains + [mix_chain, inn_chain, out_chain]:
        ch[2]()

    def vdrain(s, carry):
        for way in (0, 1):
            ok, b = spread_send(way, s, z, nz)

            @pl.when(ok)
            def _():
                vcopy(way, s, b).wait_send()

        return carry

    lax.fori_loop(1, nz, vdrain, 0)


def w_heads_of(pw, width):
    return pw[...].reshape(width, pw.shape[3])


def whole(nz, tokens, teacher, seg, valid, par, wq, wk, wv, vectors, mix, inn, out):
    trees, length, width = tokens.shape
    rz, wide = mix.shape[0], inn.shape[1]
    full, count, n = 4 * length, trees * length, width // 4
    heads = n // HD
    h2, w2, w4, w8 = width // 2, wide // 2, wide // 4, wide // 8
    vmem = pl.BlockSpec(memory_space=pltpu.VMEM)
    anyspace = pl.BlockSpec(memory_space=pl.ANY)
    shape = jax.ShapeDtypeStruct
    vec = (16, width)
    most = max(nz, 4)
    parts = 2 if rz % 32 == 0 else 1
    return pl.pallas_call(
        functools.partial(whole_body, nz),
        out_shape=(
            shape((count, width), bf16),
            shape((count, width), f32),
            shape((trees * full, width), bf16),
            shape((rz, wide), bf16),
            shape((4 * rz, width), bf16),
            shape((rz, width), bf16),
            shape((heads, 4, rz, 3 * HD), bf16),
            shape((trees, length, width), bf16),
            shape(vec, f32),
        ),
        in_specs=[anyspace] * 2 + [vmem] * 2 + [pl.BlockSpec(memory_space=pltpu.SMEM)] + [anyspace] * 3 + [vmem] * 9 + [anyspace] * 3,
        out_specs=[anyspace] * 5 + [vmem] * 4,
        scratch_shapes=[
            pltpu.SMEM((trees, NSEG), jnp.int32),
            V((trees, 4, length, width), bf16),
            V((trees, full, width), bf16),
            V((width, width), bf16),
            V((nz, rz, wide), bf16),
            V((wide, width), bf16),
            V((nz, parts, rz // parts, 3 * n), bf16),
            V((trees, full, 3 * n), bf16),
            V((trees, full, 8), f32),
            V((trees, full, 4 * HD), bf16),
            V((trees, full, n), bf16),
            V((4, trees, length, n), bf16),
            V((count, width), bf16),
            V((count, width), f32),
            V((count, width), f32),
            V((count, width), f32),
            V((count, width), bf16),
            V((count, width), bf16),
            V((count, width), bf16),
            V((count, width), bf16),
            V((count, 128), f32),
            V((count, 128), f32),
            V((width, width), bf16),
            V((full, trees * n), bf16),
            V((full, trees * n), bf16),
            V((full, HD), f32),
            V((full, HD), f32),
            V((nz, rz, w2), bf16),
            V((nz, 4 * rz, h2), bf16),
            V((width, h2), bf16),
            V((2, trees, length, width), bf16),
            V((nz, rz, w4), bf16),
            V((nz, 2 * rz, h2), bf16),
            V((nz, rz, w8), bf16),
            V((nz, rz, h2), bf16),
            V((trees, length, width), bf16),
            V((2, nz, rz, w8), bf16),
            V((2, nz, rz, h2), bf16),
            V((2, nz, rz, h2), bf16),
            V((heads, 2, nz, rz, 3 * HD), bf16),
            V((heads, nz, rz, 3 * HD), bf16),
            V((rz, h2), bf16),
            V((rz, h2), bf16),
            V((heads, rz, 3 * HD), bf16),
            V((3,) + vec, f32),
            V((nz,) + vec, f32),
            V(vec, f32),
            V((nz, 16, width), bf16),
            V((4, 8, count), jnp.int32),
            V(vec, f32),
            DMA((8,)), DMA((trees, 4)), DMA((trees * 4,)),
            DMA((nz,)), DMA((nz,)),
            DMA((3 + 3 * trees,)), DMA((3 + 3 * trees,)),
            DMA((6, 2, nz)), DMA((6, 2, nz)),
            DMA((2, 3, nz)), DMA((2, 3, nz)),
            DMA((3, 4, nz)), DMA((3, 4, nz)),
            DMA((trees, 3)), DMA((trees, 3)),
            DMA((3,)), DMA((3,)),
            DMA((5,)), DMA((5,)),
            DMA((2, most)), DMA((2, most)),
            DMA((3, nz)), DMA((3, nz)),
            DMA((2, nz)), DMA((2, nz)),
            DMA((3, trees)), DMA((3, trees)),
            DMA((2, 7)), DMA((2, 7)),
            DMA((7, 2, nz)), DMA((7, 2, nz)),
            DMA((25,)), DMA((25,)),
            DMA((2,)), DMA((2,)),
        ],
        compiler_params=pltpu.CompilerParams(
            collective_id=1, has_side_effects=True, vmem_limit_bytes=VMEM_LIMIT
        ),
        name="whole",
    )(tokens, teacher, seg, valid, par, wq, wk, wv, *vectors, mix, inn, out)


def finish_body(
    slots, spot, h_inn, h_out, h_mix, h_qkv, h_ig, h_one, vec,
    o_inn, o_out, o_mix, o_q, o_k, o_v, o_ig, o_loss, o0, o1, o2, o3, o4, o5, o6, o7, o8,
    inn, out, mix, qkv, ig, one, b_inn, b_out, b_mix, b_q, b_k, b_v, b_ig, get, put,
):
    sources = ((h_inn, inn), (h_out, out), (h_one, one), (h_ig, ig), (h_qkv, qkv), (h_mix, mix))
    loads = [pltpu.make_async_copy(a, b, get.at[i]) for i, (a, b) in enumerate(sources)]
    for cp in loads:
        cp.start()
    scale = slots / vec[spot : spot + 1, 0:1]
    stores = []

    def send(buf, dst):
        cp = pltpu.make_async_copy(buf, dst, put.at[len(stores)])
        cp.start()
        stores.append(cp)

    def each(size, fn):
        step = 64 if size % 64 == 0 else size

        def part(i, carry):
            fn(pl.ds(pl.multiple_of(i * step, step), step))
            return carry

        lax.fori_loop(0, size // step, part, 0)

    def scaled(dst, src):
        def part(rows):
            dst[rows] = src[rows].astype(f32) * scale

        each(src.shape[0], part)

    shard = lax.axis_index("shard")
    count = vec[spot : spot + 1, 0:1]
    o_loss[...] = jnp.sum(vec[spot - 1 : spot], axis=1, keepdims=True) / count
    width, size = vec.shape[1], o0.shape[0]
    turned = pltpu.roll(vec[0:8], lax.rem(width - shard * size, width), 1) * scale
    for i, o in enumerate((o0, o1, o2, o3, o4, o5, o6, o7)):
        o[...] = turned[i : i + 1, :size].reshape(size)
    wide, part = (spot - 9) * width, o8.shape[0]
    row = jnp.concatenate([vec[8 + i : 9 + i] for i in range(spot - 9)], axis=1)
    row = jnp.concatenate([row, jnp.zeros((7, wide), f32)], axis=0)
    row = pltpu.roll(row, lax.rem(wide - shard * part, wide), 1) * scale
    o8[...] = row[0:1, :part].reshape(part)

    loads[0].wait()
    scaled(b_inn, inn)
    send(b_inn, o_inn)
    loads[1].wait()
    scaled(b_out, out)
    send(b_out, o_out)
    loads[2].wait()
    loads[3].wait()
    for t in range(ig.shape[0]):

        def part(rows):
            b_ig[t, rows] = (one[t, rows] + ig[t, rows].astype(f32)) * scale

        each(ig.shape[1], part)
    send(b_ig, o_ig)
    loads[4].wait()
    for i, (buf, dst) in enumerate(((b_q, o_q), (b_k, o_k), (b_v, o_v))):
        for j in range(4):
            for h in range(qkv.shape[0]):
                at = (j * qkv.shape[0] + h) * HD
                buf[:, at : at + HD] = qkv[h, j, :, i * HD : (i + 1) * HD].astype(f32) * scale
        send(buf, dst)
    loads[5].wait()
    scaled(b_mix, mix)
    send(b_mix, o_mix)
    for cp in stores:
        cp.wait()


def finish(slots, spot, inn, out, mix, qkv, ig, one, vec, sizes):
    vmem = pl.BlockSpec(memory_space=pltpu.VMEM)
    anyspace = pl.BlockSpec(memory_space=pl.ANY)
    shapes = [inn.shape, out.shape, mix.shape, mix.shape, mix.shape, mix.shape, ig.shape]
    return pl.pallas_call(
        functools.partial(finish_body, slots, spot),
        out_shape=tuple(jax.ShapeDtypeStruct(sh, f32) for sh in shapes + [(1, 1)] + [(n,) for n in sizes]),
        in_specs=[anyspace] * 6 + [vmem],
        out_specs=[anyspace] * 7 + [vmem] * 10,
        scratch_shapes=[V(a.shape, a.dtype) for a in (inn, out, mix, qkv, ig, one)]
        + [V(sh, f32) for sh in shapes]
        + [DMA((6,)), DMA((7,))],
        compiler_params=pltpu.CompilerParams(vmem_limit_bytes=VMEM_LIMIT),
        name="finish",
    )(inn, out, mix, qkv, ig, one, vec)


def per_device(
    nz,
    tokens, teacher, seg_ids, parent_seg, valid,
    query_weight, query_bias, key_weight, value_weight, value_bias,
    mix_weight, mix_bias, first_gain, first_shift,
    inner_weight, inner_bias, outer_weight, outer_bias, second_gain, second_shift,
):
    trees, local_len, width = tokens.shape
    n_seq = lax.axis_size("seq")
    row_count = trees * local_len
    total_slots = row_count * lax.axis_size("replica") * nz * n_seq
    rz = mix_weight.shape[0]
    wide = inner_weight.shape[1]

    vectors = (
        query_bias, value_bias, mix_bias, first_gain, first_shift, outer_bias, second_gain, second_shift, inner_bias
    )

    layer_out, grad_one, _, r_inn, r_out, r_mix, r_qkv, r_ig, r_vec = whole(
        nz, tokens, teacher.reshape(row_count, width), seg_ids, valid, parent_seg,
        query_weight, key_weight, value_weight, vectors, mix_weight, inner_weight, outer_weight,
    )
    layer_out = layer_out.reshape(trees, local_len, width)
    spot = 8 + wide // width
    sizes = [rz] * 8 + [inner_bias.shape[0]]
    dinner, douter, dmix, dquery, dkey, dvalue, input_grad, loss, *rows = finish(
        total_slots, spot + 1, r_inn, r_out, r_mix, r_qkv, r_ig,
        grad_one.reshape(trees, local_len, width), r_vec, sizes,
    )
    return (
        layer_out, loss[0, 0], input_grad,
        dquery, rows[0], dkey, dvalue, rows[1],
        dmix, rows[2], rows[3], rows[4],
        dinner, rows[8], douter, rows[5], rows[6], rows[7],
    )


def solution(mesh):
    rows = P(("replica", "shard"), "seq", None)
    line = P(("replica", "shard"), "seq")
    mat = P("shard", None)
    row = P("shard")
    placed = (
        rows, rows, line, P(("replica", "shard"), None), line,
        mat, row, mat, mat, row, mat, row, row, row, mat, row, mat, row, row, row,
    )
    return jax.shard_map(
        functools.partial(per_device, mesh.shape["shard"]),
        mesh=mesh,
        in_specs=placed,
        out_specs=(
            rows, P(), rows,
            mat, row, mat, mat, row, mat, row, row, row, mat, row, mat, row, row, row,
        ),
        check_vma=False,
    )
```

```python
import functools

import jax
import jax.numpy as jnp
from jax import lax
from jax.experimental import pallas as pl
from jax.experimental.pallas import tpu as pltpu
from jax.sharding import PartitionSpec as P

HEADS = 12
HD = 64
NSEG = 8
MESH = pl.DeviceIdType.MESH
BIG = 1e30
norm_eps = 1e-12
f32 = jnp.float32
bf16 = jnp.bfloat16
VMEM_LIMIT = 63 * 1024 * 1024


class Place:
    def __init__(self, nz):
        self.nz = nz
        self.x = lax.axis_index("replica")
        self.z = lax.axis_index("shard")
        self.q = lax.axis_index("seq")
        self.y = self.q // 2
        self.c = self.q % 2
        x, z, y, c = self.x, self.z, self.y, self.c
        self.core = (x, z, 2 * y + 1 - c)
        self.ynb = (x, z, 2 * (1 - y) + c)
        self.xnb = (1 - x, z, self.q)
        self.right = (x, z + 1, self.q)
        self.left = (x, z - 1, self.q)

    def greet(self, more):
        bar = pltpu.get_barrier_semaphore()
        for peer in [self.core, self.ynb, self.xnb] + more:
            pl.semaphore_signal(bar, inc=1, device_id=peer, device_id_type=MESH)

        @pl.when(self.z > 0)
        def _():
            pl.semaphore_signal(bar, inc=1, device_id=self.left, device_id_type=MESH)

        @pl.when(self.z < self.nz - 1)
        def _():
            pl.semaphore_signal(bar, inc=1, device_id=self.right, device_id_type=MESH)

        peers = 3 + len(more) + (self.z > 0).astype(jnp.int32) + (self.z < self.nz - 1).astype(jnp.int32)
        pl.semaphore_wait(bar, peers)


def rcopy(src, dst, ssem, rsem, dev):
    return pltpu.make_async_remote_copy(
        src_ref=src, dst_ref=dst, send_sem=ssem, recv_sem=rsem, device_id=dev, device_id_type=MESH
    )


def both(a, b):
    return jnp.logical_and(a, b)


def dot_nt(a, b):
    return lax.dot_general(a, b, (((1,), (1,)), ((), ())), preferred_element_type=f32)


def dot_tn(a, b):
    return lax.dot_general(a, b, (((0,), (0,)), ((), ())), preferred_element_type=f32)


def dot_nn(a, b):
    return jnp.dot(a, b, preferred_element_type=f32)


def add_to(dst, src):
    dst[...] = (dst[...].astype(f32) + src[...].astype(f32)).astype(dst.dtype)


def lanes(start, size):
    return pl.ds(pl.multiple_of(start, 128), size)


def rows_at(start, size):
    return pl.ds(pl.multiple_of(start, 8), size)


def row_mean(v):
    return jnp.sum(v, axis=1, keepdims=True) * (1.0 / v.shape[1])


def norm_back(grad_hat, hat, inv):
    return inv * (grad_hat - row_mean(grad_hat) - hat * row_mean(grad_hat * hat))


def fold(v):
    return jnp.sum(v.reshape(v.shape[0] // 8, 8, v.shape[1]), axis=0)


def total_row(v):
    return jnp.sum(v, axis=0, keepdims=True)


QB = 256
RB = 32
DMA = pltpu.SemaphoreType.DMA
V = pltpu.VMEM


def spread_send(way, s, z, nz):
    if way == 0:
        return both(z >= s - 1, z < nz - 1), z - s + 1
    return both(z <= nz - s, z > 0), z + s - 1


def spread_get(way, s, z, nz):
    if way == 0:
        return z >= s, z - s
    return z <= nz - 1 - s, z + s


def whole_body(
    nz, x_hbm, tea_hbm, seg_ref, valid_ref, par_ref, wq_hbm, wk_hbm, wv_hbm, *more,
):
    vectors, (mix_hbm, inn_hbm, out_hbm) = more[:9], more[9:12]
    (
        y_hbm, one_hbm, xa_hbm, o_inn, o_out, o_mix, o_qkv, o_ig, o_vec, bits, hid, slp, mixa, inna, outa, pw, qkv,
        lse, feat, att, blocks, tok, A1, A2, A3, fl, gb, gp, tea, vm, inv1, mixg, gsend, gat, dk, dv, ci, co, cm, cg, xi, yo,
        yi, xo, yg, zi, zo, zm, zq, aq, xm, ym, xq, v_in, v_z, v_acc, sma, tga, vecs, loc, sav, rel, px, pr2, xs,
        xr, zs, zr, fs, fr, cs, cr, hs, hr, gs_, gr_, ks, kr, ds_, dr_, s1, r1, s2, r2, is_, ir, ps, pr, bs, br, es, er, vs, vr,
    ) = more[12:]
    p = Place(nz)
    z, c, y, x, q = p.z, p.c, p.y, p.x, p.q
    rz, width = mix_hbm.shape
    wide = inn_hbm.shape[1]
    trees, length = x_hbm.shape[0], x_hbm.shape[1]
    full = qkv.shape[1]
    count = trees * length
    n = width // 4
    heads = n // HD
    chunks = wide // width
    h2, w2, w4, w8 = width // 2, wide // 2, wide // 4, wide // 8
    cross = (x, z, 2 * (1 - y) + 1 - c)
    qy = 2 * (1 - y) + c
    o4 = 4 * rz

    load = [
        pltpu.make_async_copy(x_hbm, hid.at[:, q], loc.at[0]),
        pltpu.make_async_copy(wq_hbm, slp.at[0, pl.ds(0, rz)], loc.at[1]),
        pltpu.make_async_copy(wk_hbm, slp.at[0, pl.ds(256, rz)], loc.at[2]),
        pltpu.make_async_copy(wv_hbm, slp.at[0, pl.ds(512, rz)], loc.at[3]),
        pltpu.make_async_copy(mix_hbm, mixa.at[rows_at(z * rz, rz)], loc.at[4]),
        pltpu.make_async_copy(inn_hbm, inna.at[z], loc.at[5]),
        pltpu.make_async_copy(out_hbm, outa.at[rows_at(z * o4, o4)], loc.at[6]),
        pltpu.make_async_copy(tea_hbm, tea, loc.at[7]),
    ]
    for cp in load:
        cp.start()
    for t in range(trees):
        seg = seg_ref[t : t + 1, :]
        tga[q, 0:1, t * length : (t + 1) * length] = jnp.where(
            valid_ref[t : t + 1, :] == 1, seg, seg + NSEG
        )
    p.greet([cross])

    def x_core(t):
        return rcopy(hid.at[t, q], hid.at[t, q], xs.at[2 + t], xr.at[2 + t], p.core)

    def x_y(t):
        return rcopy(hid.at[t, q], hid.at[t, q], xs.at[2 + trees + t], xr.at[2 + trees + t], p.ynb)

    def x_on(t):
        return rcopy(hid.at[t, qy], hid.at[t, qy], xs.at[2 + 2 * trees + t], xr.at[2 + 2 * trees + t], p.core)

    t_core = rcopy(tga.at[q], tga.at[q], xs.at[0], xr.at[0], p.core)
    t_y = rcopy(tga.at[q], tga.at[q], xs.at[1], xr.at[1], p.ynb)
    t_on = rcopy(tga.at[qy], tga.at[qy], xs.at[2 + 3 * trees], xr.at[2 + 3 * trees], p.core)
    t_y.start()
    t_core.start()
    load[0].wait()
    for t in range(trees):
        x_y(t).start()
    for t in range(trees):
        x_core(t).start()

    parts, rows_in = pw.shape[1], pw.shape[2]
    back = lax.rem(width - q * n, width)
    for i in range(3):
        load[1 + i].wait()
        turned = pltpu.roll(slp[0, i * 256 : i * 256 + rz].astype(f32), back, 1)
        for h in range(heads):
            for half in range(parts):
                own = turned[half * rows_in : (half + 1) * rows_in, h * HD : (h + 1) * HD]
                pw[z, half, :, (3 * h + i) * HD : (3 * h + i + 1) * HD] = own.astype(bf16)
    def row_of(ref, size):
        own = ref[...].astype(f32).reshape(1, ref.shape[0])
        if ref.shape[0] == size:
            return own
        return jnp.concatenate([own, jnp.zeros((1, size - ref.shape[0]), f32)], axis=1)

    small = jnp.concatenate([row_of(v, width) for v in vectors[:8]], axis=0)
    wide_row = jnp.concatenate([row_of(vectors[8], wide), jnp.zeros((7, wide), f32)], axis=0)
    wide_row = pltpu.roll(wide_row, z * (wide // nz), 1)
    sma[z] = jnp.concatenate(
        [pltpu.roll(small, z * rz, 1)]
        + [wide_row[0:1, j * width : (j + 1) * width] for j in range(chunks)]
        + [jnp.zeros((8 - chunks, width), f32)],
        axis=0,
    ).astype(bf16)

    def at_row(ref, b, size):
        return ref.at[rows_at(b * size, size)]

    def piece_of(k, b, xx, yy):
        if k == 0:
            return inna.at[b, :, lanes(c * w2 + (2 * xx + yy) * w8, w8)]
        return outa.at[rows_at(b * o4 + 2 * xx * rz, 2 * rz), lanes(c * h2, h2)]

    there = {
        0: lambda b: pw.at[b, x if parts == 2 else 0],
        1: lambda b: sma.at[b],
        3: lambda b: mixa.at[rows_at(b * rz, rz), lanes(c * h2, h2)],
        4: lambda b: piece_of(0, b, x, y),
        5: lambda b: piece_of(1, b, x, y),
    }

    def zcopy(k, way, s, b):
        dev = p.right if way == 0 else p.left
        return rcopy(there[k](b), there[k](b), zs.at[k, way, s], zr.at[k, way, s], dev)

    def start_step(k, s):
        for way in (0, 1):
            cond, b = spread_send(way, s, z, nz)

            @pl.when(both(cond, s <= nz - 1))
            def _():
                zcopy(k, way, s, b).start()

    def each(s, fn):
        for way in (0, 1):
            cond, b = spread_get(way, s, z, nz)

            @pl.when(cond)
            def _():
                fn(way, b)

    def take(k, s):
        each(s, lambda way, b: zcopy(k, way, s, b).wait_recv())

    def to_y(k, b):
        return rcopy(piece_of(k, b, x, y), piece_of(k, b, x, y), fs.at[k, 0, b], fr.at[k, 0, b], p.ynb)

    def to_x(k, b):
        return rcopy(piece_of(k, b, x, y), piece_of(k, b, x, y), fs.at[k, 1, b], fr.at[k, 1, b], p.xnb)

    def onward(k, b):
        return rcopy(piece_of(k, b, x, 1 - y), piece_of(k, b, x, 1 - y), fs.at[k, 2, b], fr.at[k, 2, b], p.xnb)

    def core_copy(k, b, part):
        if k == 2:
            piece = there[3](b)
        else:
            piece = piece_of(k, b, x if part % 2 == 0 else 1 - x, y if part < 2 else 1 - y)
        return rcopy(piece, piece, cs.at[k, part, b], cr.at[k, part, b], p.core)

    def pw_x(b):
        return rcopy(pw.at[b, x], pw.at[b, x], px.at[b], pr2.at[b], p.xnb)

    for k in (0, 1):
        start_step(k, 1)

    def small_step(s, carry):
        for k in (0, 1):
            take(k, s)
        for k in (0, 1):
            start_step(k, s + 1)
        if parts == 2:
            each(s, lambda way, b: pw_x(b).start())
        return carry

    lax.fori_loop(1, nz - 1, small_step, 0)
    for i in (4, 5, 6, 7):
        load[i].wait()
    for k in (4, 3, 5):
        start_step(k, 1)
    for k in (0, 1):
        take(k, nz - 1)
    if parts == 2:
        each(nz - 1, lambda way, b: pw_x(b).start())

    def mix_step(s):
        def got(way, b):
            zcopy(3, way, s, b).wait_recv()
            core_copy(2, b, 0).start()

        each(s, got)
        start_step(3, s + 1)

    def z_step(k, s):
        def got(way, b):
            zcopy(4 + k, way, s, b).wait_recv()
            if k == 0:
                to_y(k, b).start()
            to_x(k, b).start()

        each(s, got)
        start_step(4 + k, s + 1)
        each(s, lambda way, b: core_copy(k, b, 0).start())

    def pass_on(k, s):
        def got(way, b):
            to_y(k, b).wait_recv()
            onward(k, b).start()
            core_copy(k, b, 2).start()

        each(s, got)

    def rest_of(k, s):
        def got(way, b):
            to_x(k, b).wait_recv()
            core_copy(k, b, 1).start()
            if k == 0:
                onward(k, b).wait_recv()
                core_copy(k, b, 3).start()

        each(s, got)

    def from_core(k, s):
        def got(way, b):
            for part in range((4, 2, 1)[k]):
                core_copy(k, b, part).wait_recv()

        each(s, got)

    def all_steps(*fns):
        def one(s, carry):
            for fn in fns:
                fn(s)
            return carry

        lax.fori_loop(1, nz, one, 0)

    placed = nz == 4

    small = lax.fori_loop(0, nz, lambda i, v: v + sma[i].astype(f32), jnp.zeros(vecs.shape, f32))
    vecs[...] = small
    turned = pltpu.roll(small, back, 1)
    bias = []
    for h in range(heads):
        cols = slice(h * HD, (h + 1) * HD)
        bias += [turned[0:1, cols], jnp.zeros((1, HD), f32), turned[1:2, cols]]
    bias = jnp.concatenate(bias, axis=1)

    t_y.wait_recv()
    t_on.start()
    t_core.wait()
    t_on.wait()

    row = lax.broadcasted_iota(jnp.int32, (16, 4 * HD), 0)
    lane = lax.broadcasted_iota(jnp.int32, (16, 4 * HD), 1)
    trow = lax.broadcasted_iota(jnp.int32, (16, full), 0)
    vrow = lax.broadcasted_iota(jnp.int32, (16, length), 0)
    ones = jnp.ones((16, 128), bf16)
    for t in range(trees):
        bits[t, 0] = jnp.int32(1)
        for s in range(1, NSEG):
            bits[t, s] = bits[t, par_ref[t, s]] + (1 << s)
        seen = jnp.zeros((16, 4 * HD), jnp.int32)
        for a in range(NSEG):
            seen = jnp.where(row == a, bits[t, a], seen)
        at = jnp.clip(lane - HD, 0, NSEG)
        unseen = ((seen >> at) & 1) == 0
        q_side = both(both(row < NSEG, both(lane >= HD, lane <= HD + NSEG)), unseen)
        k_side = both(row <= NSEG, lane == row + 3 * HD)
        table = jnp.where(q_side, -BIG, jnp.where(k_side, 1.0, 0.0)).astype(bf16)
        tag = jnp.concatenate(
            [tga[j, 0:1, t * length : (t + 1) * length] for j in range(full // length)], axis=1
        )
        gone = tag >= NSEG
        seg = jnp.where(gone, tag - NSEG, tag)
        seg = jnp.broadcast_to(seg, (16, full))
        gone = jnp.broadcast_to(jnp.where(gone, 1, 0), (16, full))
        hot = jnp.where(trow == NSEG, gone, jnp.where(trow == seg, 1, 0)).astype(f32).astype(bf16)
        feat[t] = dot_tn(hot, table).astype(bf16)
        here = jnp.broadcast_to(valid_ref[t : t + 1, :], (16, length))
        here = jnp.where(vrow == 0, here, 0).astype(f32).astype(bf16)
        vm[t * length : (t + 1) * length] = dot_tn(here, ones)

    t_y.wait_send()
    if parts == 2:
        all_steps(lambda s: each(s, lambda way, b: pw_x(b).wait()))
    w_heads = w_heads_of(pw, width)
    saves = []

    def project(t):
        x_core(t).wait()
        x_on(t).wait()
        for j in range(4):
            cp = pltpu.make_async_copy(
                hid.at[t, j], xa_hbm.at[pl.ds((t * 4 + j) * length, length)], sav.at[t, j]
            )
            cp.start()
            saves.append(cp)
        qkv[t] = (dot_nn(hid[t].reshape(full, width), w_heads) + bias).astype(bf16)

    for t in range(trees):
        x_y(t).wait()
        x_on(t).start()
        if t == 0:
            project(0)


    def part(h, i):
        return slice((3 * h + i) * HD, (3 * h + i + 1) * HD)

    def queries_of(t, rows, h):
        return jnp.concatenate([qkv[t, rows, part(h, 0)] * 0.125, feat[t, rows, HD : 2 * HD]], axis=1)

    def keys_of(t, h):
        return jnp.concatenate([qkv[t, :, part(h, 1)], feat[t, :, 3 * HD : 4 * HD]], axis=1)

    def token_rows(j):
        return pl.ds(pl.multiple_of(j * length, length), length)

    def send_heads(t, d):
        to = lax.rem(q + d, 4)
        return rcopy(
            att.at[t, token_rows(to)], blocks.at[q, t], hs.at[t, d - 1], hr.at[t, d - 1], (x, z, to)
        )

    def run_at(slots, first, i):
        for k in range(full // QB):
            fns = slots.get(first + k, [])
            if fns:

                @pl.when(i == k)
                def _():
                    for fn, *args in fns:
                        fn(*args)

    slots = {
        1: [(z_step, 0, 1)],
        5: [(mix_step, 1)],
        9: [(pass_on, 0, 1)],
        12: [(z_step, 0, 2)],
        13: [(z_step, 1, 1)],
        14: [(mix_step, 2)],
        18: [(pass_on, 0, 2)],
        21: [(z_step, 0, 3)],
        23: [(z_step, 1, 2)],
    }
    if not placed:
        slots = {}
    per_head = full // QB
    for t in range(trees):
        if t > 0:
            project(t)
        for h in range(heads):
            keys = keys_of(t, h)
            values = qkv[t, :, part(h, 2)]

            def block(i, carry):
                rows = pl.ds(pl.multiple_of(i * QB, QB), QB)
                s = dot_nt(queries_of(t, rows, h), keys)
                peak = jnp.max(s, axis=1, keepdims=True)
                e = jnp.exp(s - peak)
                total = jnp.sum(e, axis=1, keepdims=True)
                o = dot_nn(e.astype(bf16), values) / total
                att[t, rows, h * HD : (h + 1) * HD] = o.astype(bf16)
                lse[t, rows, h : h + 1] = peak + jnp.log(total)
                run_at(slots, (t * heads + h) * per_head, i)
                return carry

            lax.fori_loop(0, full // QB, block, 0)
        for d in (1, 2, 3):
            send_heads(t, d).start()
    for t in range(trees):
        blocks[q, t] = att[t, token_rows(q)]
    if placed:
        mix_step(3)
        pass_on(0, 3)
    else:
        all_steps(mix_step)
    for t in range(trees):
        for d in (1, 2, 3):
            send_heads(t, d).wait()

    for j in range(4):
        tok[:, j * n : (j + 1) * n] = blocks[j].reshape(count, n)
    all_steps(functools.partial(from_core, 2))
    A3[...] = dot_nn(tok[...], mixa[...])
    if placed:
        rest_of(0, 1)
        rest_of(0, 2)
        z_step(1, 3)

    def rows_of(i):
        return pl.ds(pl.multiple_of(i * RB, RB), RB)

    per = length // RB

    def first_norm(i, carry):
        rows = rows_of(i)
        own = hid[i // per, q, rows_of(i % per)].astype(f32)
        r1 = own + A3[rows] + vecs[2:3]
        center = r1 - row_mean(r1)
        inv = lax.rsqrt(row_mean(center * center) + norm_eps)
        hat = center * inv
        A1[rows] = hat
        inv1[rows] = jnp.broadcast_to(inv, (RB, 128))
        fl[rows] = (hat * vecs[3:4] + vecs[4:5]).astype(bf16)
        return carry

    lax.fori_loop(0, count // RB, first_norm, 0, unroll=2)
    for cp in saves:
        cp.wait()
    if placed:
        rest_of(0, 3)
    else:
        for k in (0, 1):
            all_steps(*[functools.partial(fn, k) for fn in ((z_step, pass_on, rest_of), (z_step, rest_of))[k]])
    all_steps(functools.partial(from_core, 0))

    def inner_chunk(j):
        return inna[:, :, j * width : (j + 1) * width].reshape(width, width)

    def hid_chunk(j):
        return hid[j // 2, 2 * (j % 2) : 2 * (j % 2) + 2].reshape(count, width)

    for j in range(chunks):
        A3[...] = dot_nn(fl[...], inner_chunk(j))

        def gelu(i, carry):
            rows = rows_of(i)
            pre = A3[rows] + vecs[8 + j : 9 + j]
            cdf = 0.5 + 0.5 * lax.erf(pre * (0.5**0.5))
            hid[j // 2, 2 * (j % 2) + i // per, rows_of(i % per)] = (pre * cdf).astype(bf16)
            slope = cdf + pre * jnp.exp(-0.5 * pre * pre) * 0.3989422804014327
            slp[j // 2, pl.ds(pl.multiple_of((j % 2) * count + i * RB, RB), RB)] = slope.astype(bf16)
            return carry

        lax.fori_loop(0, count // RB, gelu, 0)
        if placed and j == 1:
            rest_of(1, 1)
        if placed and j == 2:
            rest_of(1, 2)
            rest_of(1, 3)
    all_steps(functools.partial(from_core, 1))
    for j in range(chunks):
        more = dot_nn(hid_chunk(j), outa[j * width : (j + 1) * width])
        if j == 0:
            A2[...] = more
        else:
            A2[...] += more

    def drain(s, carry):
        for k in (0, 1, 3, 4, 5):
            for way in (0, 1):
                cond, b = spread_send(way, s, z, nz)

                @pl.when(cond)
                def _():
                    zcopy(k, way, s, b).wait_send()

        def end(way, b):
            core_copy(2, b, 0).wait_send()
            to_y(0, b).wait_send()
            onward(0, b).wait_send()
            for k in (0, 1):
                to_x(k, b).wait_send()
                for part in range((4, 2)[k]):
                    core_copy(k, b, part).wait_send()

        each(s, end)
        return carry

    lax.fori_loop(1, nz, drain, 0)

    zero = jnp.zeros((8, width), f32)

    def second_norm(i, carry):
        loss, dgain, dshift, dbias = carry
        rows = rows_of(i)
        first = A1[rows] * vecs[3:4] + vecs[4:5]
        r2 = first + A2[rows] + vecs[5:6]
        center = r2 - row_mean(r2)
        inv = lax.rsqrt(row_mean(center * center) + norm_eps)
        hat = center * inv
        out = hat * vecs[6:7] + vecs[7:8]
        err = out - tea[rows].astype(f32)
        tea[rows] = out.astype(bf16)
        weighted = vm[rows, 0:1] * err
        grad = 2.0 * weighted
        g2 = norm_back(grad * vecs[6:7], hat, inv)
        A2[rows] = g2
        low = g2.astype(bf16)
        gb[rows] = low
        return (
            loss + fold(weighted * err),
            dgain + fold(grad * hat),
            dshift + fold(grad),
            dbias + fold(low.astype(f32)),
        )

    loss, dgain, dshift, dbias = lax.fori_loop(0, count // RB, second_norm, (zero, zero, zero, zero), unroll=2)
    put_y = pltpu.make_async_copy(tea, y_hbm, loc.at[0])
    put_y.start()
    v_acc[...] = jnp.zeros_like(v_acc)
    spot = 8 + chunks
    v_acc[5:6] = total_row(dbias)
    v_acc[6:7] = total_row(dgain)
    v_acc[7:8] = total_row(dshift)
    v_acc[spot : spot + 1] = total_row(loss)
    v_acc[spot + 1 : spot + 2, 0:128] = total_row(vm[...])

    def c_out(d):
        return rcopy(outa.at[rows_at(d * o4, o4), lanes((1 - c) * h2, h2)], co.at[d], ds_.at[0, d], dr_.at[0, d], p.core)

    def chunk_of(core, k):
        return (chunks - 1) * core + (1 - 2 * core) * k

    def c_inn(k):
        src = inna.at[:, :, lanes(chunk_of(1 - c, k) * width, width)]
        return rcopy(src, ci.at[:, :, pl.ds(k * width, width)], ds_.at[1, k], dr_.at[1, k], p.core)

    def out_y(d):
        src = co.at[d, rows_at((1 - y) * 2 * rz, 2 * rz)]
        return rcopy(src, yo.at[d], s1.at[0, d], r1.at[0, d], p.ynb)

    def inn_x(d, k):
        src = ci.at[d, :, lanes(k * width + (1 - x) * w8, w8)]
        return rcopy(src, xi.at[d, :, pl.ds(k * w8, w8)], s1.at[1 + k, d], r1.at[1 + k, d], p.xnb)

    def out_x(d):
        src = yo.at[d, rows_at((1 - x) * rz, rz)]
        return rcopy(src, xo.at[d], s2.at[0, d], r2.at[0, d], p.xnb)

    def inn_y(d):
        return rcopy(xi.at[d, :, lanes((1 - y) * w8, w8)], yi.at[d], s2.at[1, d], r2.at[1, d], p.ynb)

    def span(lo, hi, fn):
        if hi - lo == 1:
            fn(lo)
            return

        def one(i, carry):
            fn(i)
            return carry

        lax.fori_loop(lo, hi, one, 0)

    def of_chunk(j, fn):
        span(j * nz // chunks, (j + 1) * nz // chunks, fn)

    def group(g, fn):
        def pair(i):
            fn(nz - 1 - i)
            fn(i)

        span(g * nz // 4, (g + 1) * nz // 4, pair)

    def out_chip(d):
        c_out(d).wait()
        for j in range(4):
            add_to(co.at[d, j * rz : (j + 1) * rz], outa.at[rows_at(d * o4 + j * rz, rz), lanes(c * h2, h2)])
        out_y(d).start()

    def inn_chip(g, k):
        if g == 0:
            c_inn(k).wait()

        def one(d):
            for j in range(2):
                at = slice(k * width + j * h2, k * width + (j + 1) * h2)
                add_to(ci.at[d, :, at], inna.at[d, :, lanes(chunk_of(c, k) * width + j * h2, h2)])
            inn_x(d, k).start()

        group(g, one)

    def out_half(d):
        out_y(d).wait()
        add_to(yo.at[d, :rz], co.at[d, rows_at(y * 2 * rz, rz)])
        add_to(yo.at[d, rz:], co.at[d, rows_at(y * 2 * rz + rz, rz)])
        out_x(d).start()

    def inn_half(g, k):
        def one(d):
            inn_x(d, k).wait()
            add_to(xi.at[d, :, k * w8 : (k + 1) * w8], ci.at[d, :, lanes(k * width + x * w8, w8)])

        group(g, one)

    def inn_other(g):
        group(g, lambda d: inn_y(d).start())

    def out_quarter(d):
        out_x(d).wait()
        add_to(xo.at[d], yo.at[d, rows_at(x * rz, rz)])

    def inn_quarter(d):
        inn_y(d).wait()
        add_to(yi.at[d], xi.at[d, :, lanes(y * w8, w8)])

    order = [3, 0, 2, 1]
    for step, j in enumerate(order):
        A3[...] = dot_nt(gb[...], outa[j * width : (j + 1) * width])

        def slopes(i, carry):
            rows = rows_of(i)
            slope = slp[j // 2, pl.ds(pl.multiple_of((j % 2) * count + i * RB, RB), RB)]
            low = (A3[rows] * slope.astype(f32)).astype(bf16)
            gp[rows] = low
            return carry + fold(low.astype(f32))

        v_acc[8 + j : 9 + j] = total_row(lax.fori_loop(0, count // RB, slopes, zero))
        outa[j * width : (j + 1) * width] = dot_tn(hid_chunk(j), gb[...]).astype(bf16)
        of_chunk(j, lambda d: c_out(d).start())
        A2[...] += dot_nt(gp[...], inner_chunk(j))
        inna[:, :, j * width : (j + 1) * width] = dot_tn(fl[...], gp[...]).astype(bf16).reshape(nz, rz, width)

        @pl.when(c == 1 - j // 2)
        def _():
            c_inn(step // 2).start()

        if step == 1:
            of_chunk(order[0], out_chip)
        if step == 2:
            inn_chip(0, 0)
            inn_chip(1, 0)

    def first_back(i, carry):
        dgain, dshift, dbias = carry
        rows = rows_of(i)
        grad = A2[rows]
        hat = A1[rows]
        g1 = norm_back(grad * vecs[3:4], hat, inv1[rows, 0:1])
        A2[rows] = g1
        low = g1.astype(bf16)
        gb[rows] = low
        return dgain + fold(grad * hat), dshift + fold(grad), dbias + fold(low.astype(f32))

    dgain, dshift, dbias = lax.fori_loop(0, count // RB, first_back, (zero, zero, zero), unroll=2)
    v_acc[2:3] = total_row(dbias)
    v_acc[3:4] = total_row(dgain)
    v_acc[4:5] = total_row(dshift)
    put_one = pltpu.make_async_copy(A2, one_hbm, loc.at[1])
    put_one.start()

    for j in range(4):
        part_j = dot_nt(gb[...], mixa[j * n : (j + 1) * n]).astype(bf16)
        for t in range(trees):
            gsend[j * length : (j + 1) * length, t * n : (t + 1) * n] = part_j[t * length : (t + 1) * length]

    def send_grads(d):
        to = lax.rem(q + d, 4)
        return rcopy(gsend.at[token_rows(to)], gat.at[token_rows(q)], gs_.at[d - 1], gr_.at[d - 1], (x, z, to))

    for d in (1, 2, 3):
        send_grads(d).start()
    gat[token_rows(q)] = gsend[token_rows(q)]

    of_chunk(order[0], out_half)
    inn_chip(0, 1)
    of_chunk(order[1], out_chip)
    inn_chip(1, 1)
    of_chunk(order[2], out_chip)
    reload = [
        pltpu.make_async_copy(
            xa_hbm.at[pl.ds(i * length, length)], outa.at[pl.ds(i * length, length)], rel.at[i]
        )
        for i in range(trees * 4)
    ]

    def out_last():
        of_chunk(order[-1], out_chip)
        for cp in reload:
            cp.start()

    def reloaded():
        for cp in reload:
            cp.wait()

    mixg[...] = dot_tn(tok[...], gb[...]).astype(bf16)
    c_mix = rcopy(mixg.at[:, lanes((1 - c) * h2, h2)], cm, ks.at[3], kr.at[3], p.core)
    c_mix.start()

    def chain(k, acc, buf):
        def copy(way, s, d):
            dev = p.right if way == 0 else p.left
            return rcopy(acc(d), buf(way, d), bs.at[k, way, s], br.at[k, way, s], dev)

        def sending(way, s):
            if way == 0:
                d = z + nz - s
                return both(d <= nz - 1, z < nz - 1), d
            d = z - nz + s
            return both(d >= 0, z > 0), d

        def getting(way, s):
            if way == 0:
                d = z - 1 + nz - s
                return both(d <= nz - 1, z > 0), d
            d = z + 1 - nz + s
            return both(d >= 0, z < nz - 1), d

        def send(s):
            for way in (0, 1):
                ok, d = sending(way, s)

                @pl.when(both(ok, s <= nz - 1))
                def _():
                    copy(way, s, d).start()

        def get(s):
            for way in (0, 1):
                ok, d = getting(way, s)

                @pl.when(ok)
                def _():
                    copy(way, s, d).wait_recv()
                    add_to(acc(d), buf(way, d))

        def drain(s, carry):
            for way in (0, 1):
                ok, d = sending(way, s)

                @pl.when(ok)
                def _():
                    copy(way, s, d).wait_send()

            return carry

        return send, get, lambda: lax.fori_loop(1, nz, drain, 0)

    def step_of(ch, s):
        ch[1](s)
        ch[0](s + 1)

    mix_chain = chain(3, lambda d: cm.at[rows_at(d * rz, rz)], lambda way, d: zm.at[way, d])
    inn_chain = chain(4, lambda d: yi.at[d], lambda way, d: zi.at[way, d])
    out_chain = chain(5, lambda d: xo.at[d], lambda way, d: zo.at[way, d])

    def head_chain(h):
        return chain(h, lambda d: aq.at[h, d], lambda way, d: zq.at[h, way, d])

    qkv_chains = [head_chain(h) for h in range(heads)]

    c_mix.wait()

    def mix_sum(i, carry):
        block = rows_at(i * rz, rz)
        add_to(cm.at[block], mixg.at[block, lanes(c * h2, h2)])
        return carry

    lax.fori_loop(0, nz, mix_sum, 0)
    mix_chain[0](1)
    for d in (1, 2, 3):
        send_grads(d).wait()

    def head_weights(h):
        cols = slice(3 * h * HD, 3 * (h + 1) * HD)
        grad = dot_tn(outa[0:full], slp[0, :, cols])
        for t in range(1, trees):
            grad = grad + dot_tn(outa[t * full : (t + 1) * full], slp[t, :, cols])
        aq[h] = grad.astype(bf16).reshape(nz, rz, 3 * HD)
        qkv_chains[h][0](1)

    def q_x(h):
        return rcopy(aq.at[h, z], xq.at[h], es.at[13 + h], er.at[13 + h], p.xnb)

    def q_y(h):
        return rcopy(o_qkv.at[h, q], o_qkv.at[h, q], es.at[16 + h], er.at[16 + h], p.ynb)

    def q_core(h):
        return rcopy(o_qkv.at[h, q], o_qkv.at[h, q], es.at[19 + h], er.at[19 + h], p.core)

    def q_on(h):
        return rcopy(o_qkv.at[h, qy], o_qkv.at[h, qy], es.at[22 + h], er.at[22 + h], p.core)

    def q_sum(h):
        q_x(h).wait()
        o_qkv[h, q] = (aq[h, z].astype(f32) + xq[h].astype(f32)).astype(bf16)
        q_y(h).start()
        q_core(h).start()

    x_m = rcopy(cm.at[rows_at(z * rz, rz)], xm, es.at[1], er.at[1], p.xnb)
    y_m = rcopy(xm, ym, es.at[4], er.at[4], p.ynb)

    def big_step(s):
        step_of(inn_chain, s)
        step_of(out_chain, s)

    def first_big():
        inn_chain[0](1)
        out_chain[0](1)

    def ig_of(t):
        for j in range(4):
            rows = slice(j * length, (j + 1) * length)
            hid[t, j] = dot_nt(slp[t, rows, : 3 * n], w_heads_of(pw, width)).astype(bf16)
        for b in range(2):
            c_ig(t, b).start()

    def c_ig(t, b):
        return rcopy(hid.at[t, 2 * b + 1 - c], cg.at[b, t], is_.at[b, t], ir.at[b, t], p.core)

    def ig_y(t):
        return rcopy(cg.at[1 - y, t], yg.at[t], is_.at[2, t], ir.at[2, t], p.ynb)

    def ig_chip(t):
        for b in range(2):
            c_ig(t, b).wait()
            add_to(cg.at[b, t], hid.at[t, 2 * b + c])
        ig_y(t).start()

    def ig_end(t):
        ig_y(t).wait()
        o_ig[t] = (cg[y, t].astype(f32) + yg[t].astype(f32)).astype(o_ig.dtype)

    def done_piece(k, xx, yy):
        if k == 0:
            return o_inn.at[:, lanes(chunk_of(c, yy) * width + xx * w8, w8)]
        return o_out.at[rows_at((2 * yy + xx) * rz, rz), lanes(c * h2, h2)]

    def own_done(k):
        return pltpu.make_async_copy((yi if k == 0 else xo).at[z], done_piece(k, x, y), loc.at[2 + k])

    def done_y(k):
        return rcopy((yi if k == 0 else xo).at[z], done_piece(k, x, y), ps.at[k, 0], pr.at[k, 0], p.ynb)

    def done_x(k):
        return rcopy((yi if k == 0 else xo).at[z], done_piece(k, x, y), ps.at[k, 1], pr.at[k, 1], p.xnb)

    def done_on(k):
        return rcopy(done_piece(k, x, 1 - y), done_piece(k, x, 1 - y), ps.at[k, 2], pr.at[k, 2], p.xnb)

    def done_core(k, part):
        piece = done_piece(k, x if part % 2 == 0 else 1 - x, y if part < 2 else 1 - y)
        src = (yi if k == 0 else xo).at[z] if part == 0 else piece
        return rcopy(src, piece, ps.at[k, 3 + part], pr.at[k, 3 + part], p.core)

    def big_own():
        for k in (0, 1):
            own_done(k).start()
            done_y(k).start()
            done_x(k).start()
            done_core(k, 0).start()

    def big_on():
        for k in (0, 1):
            done_y(k).wait()
            done_on(k).start()
            done_core(k, 2).start()

    def big_end():
        for k in (0, 1):
            done_x(k).wait()
            done_core(k, 1).start()
        for k in (0, 1):
            done_on(k).wait()
            done_core(k, 3).start()

    def mix_end():
        x_m.wait()
        add_to(xm, cm.at[rows_at(z * rz, rz)])
        y_m.start()

    def quarters(g):
        group(g, out_quarter)
        group(g, inn_quarter)

    def head_step(h, s):
        step_of(qkv_chains[h], s)

    def q_start(h):
        q_x(h).start()

    slots = {
        0: [(inn_half, 0, 0), (inn_half, 1, 0)],
        3: [(of_chunk, order[1], out_half)],
        4: [(inn_half, 0, 1), (inn_other, 0), (out_last,)],
        5: [(step_of, mix_chain, 1)],
        7: [(of_chunk, order[2], out_half)],
        8: [(inn_half, 1, 1), (inn_other, 1)],
        9: [(group, 0, out_quarter)],
        10: [(group, 0, inn_quarter), (first_big,)],
        12: [(ig_of, 0)],
        13: [(of_chunk, order[-1], out_half)],
        14: [(ig_chip, 0), (step_of, mix_chain, 2)],
        16: [(quarters, 1), (big_step, 1)],
        17: [(reloaded,), (head_weights, 0)],
        20: [(head_weights, 1)],
        21: [(head_step, 0, 1), (big_step, 2)],
        22: [(step_of, mix_chain, 3), (lambda: x_m.start(),)],
        23: [(head_step, 0, 2), (head_step, 1, 1)],
    }
    if not placed:
        slots = {}
    put_one.wait()
    for t in range(trees):
        for h in range(heads):
            key = qkv[t, :, part(h, 1)]
            keys = keys_of(t, h)
            values = qkv[t, :, part(h, 2)]
            dk[...] = jnp.zeros_like(dk)
            dv[...] = jnp.zeros_like(dv)

            def block(i, carry):
                rows = pl.ds(pl.multiple_of(i * QB, QB), QB)
                s = dot_nt(queries_of(t, rows, h), keys)
                probs = jnp.exp(s - lse[t, rows, h : h + 1])
                grad = gat[rows, t * n + h * HD : t * n + (h + 1) * HD]
                dp = dot_nt(grad, values)
                inner = jnp.sum(probs * dp, axis=1, keepdims=True)
                ds = (probs * (dp - inner)).astype(bf16)
                dv[...] += dot_tn(probs.astype(bf16), grad)
                dk[...] += dot_tn(ds, qkv[t, rows, part(h, 0)])
                slp[t, rows, part(h, 0)] = (dot_nn(ds, key) * 0.125).astype(bf16)
                run_at(slots, (t * heads + h) * per_head, i)
                return carry

            lax.fori_loop(0, full // QB, block, 0)
            slp[t, :, part(h, 1)] = (dk[...] * 0.125).astype(bf16)
            slp[t, :, part(h, 2)] = dv[...].astype(bf16)
    if not placed:

        def slow_mix(s):
            step_of(mix_chain, s)

        def slow_big(s):
            big_step(s)
            for h in range(heads):
                step_of(qkv_chains[h], s)

        of_chunk(order[1], out_half)
        of_chunk(order[2], out_half)
        out_last()
        all_steps(slow_mix)
        x_m.start()
        for g in (0, 1):
            inn_half(g, 0)
            inn_half(g, 1)
            inn_other(g)
        reloaded()
        of_chunk(order[-1], out_half)
        for g in (0, 1):
            quarters(g)
        mix_end()
        ig_of(0)
        ig_chip(0)
        first_big()
        for h in range(heads):
            head_weights(h)
        all_steps(slow_big)
        q_x(0).start()
        big_own()
        big_on()

    dbias = jnp.zeros((1, 3 * n), f32)
    for t in range(trees):
        dbias = dbias + jnp.sum(slp[t, :, : 3 * n].astype(f32), axis=0, keepdims=True)
    gap = jnp.zeros((1, width - n), f32)
    mine = [
        jnp.concatenate([dbias[:, part(h, i)] for h in range(heads)] + [gap], axis=1) for i in (0, 2)
    ]
    mine = pltpu.roll(jnp.concatenate(mine + [jnp.zeros((6, width), f32)], axis=0), q * n, 1)
    v_acc[0:8] = v_acc[0:8] + mine
    v_c = rcopy(v_acc, v_in.at[0], ks.at[2], kr.at[2], p.core)
    v_x = rcopy(v_acc, v_in.at[1], vs.at[0], vr.at[0], p.xnb)
    v_y = rcopy(v_acc, v_in.at[2], vs.at[1], vr.at[1], p.ynb)
    def vcopy(way, s, b):
        dev = p.right if way == 0 else p.left
        return rcopy(v_z.at[b], v_z.at[b], bs.at[6, way, s], br.at[6, way, s], dev)

    def v_send(s):
        for way in (0, 1):
            ok, b = spread_send(way, s, z, nz)

            @pl.when(both(ok, s <= nz - 1))
            def _():
                vcopy(way, s, b).start()

    def v_get(s):
        for way in (0, 1):
            ok, b = spread_get(way, s, z, nz)

            @pl.when(ok)
            def _():
                vcopy(way, s, b).wait_recv()

        v_send(s + 1)

    v_c.start()
    if placed:
        head_weights(2)
    v_c.wait()
    v_acc[...] = v_acc[...] + v_in[0]
    v_x.start()
    if placed:
        mix_end()
    ig_of(1)
    v_x.wait()
    v_acc[...] = v_acc[...] + v_in[1]
    v_y.start()
    if placed:
        big_step(3)
        big_own()
        for h in range(heads):
            head_step(h, 3 - h)
        q_start(0)
    ig_chip(1)
    v_y.wait()
    v_acc[...] = v_acc[...] + v_in[2]
    v_z[z] = v_acc[...]
    v_send(1)
    if placed:
        head_step(1, 3)
        head_step(2, 2)
    q_start(1)
    if placed:
        big_on()
    y_m.wait()
    o_mix[:, lanes(c * h2, h2)] = (xm[...].astype(f32) + ym[...].astype(f32)).astype(bf16)
    m_core = rcopy(
        o_mix.at[:, lanes(c * h2, h2)], o_mix.at[:, lanes(c * h2, h2)], es.at[7], er.at[7], p.core
    )
    m_core.start()
    if placed:
        head_step(2, 3)
    q_start(2)
    ig_end(0)
    q_sum(0)
    q_sum(1)
    if placed:
        v_get(1)
        v_get(2)
    q_sum(2)
    if placed:
        v_get(3)
    else:
        all_steps(v_get)
    big_end()
    ig_end(1)

    def v_sum(i, carry):
        return carry + v_z[i]

    o_vec[...] = lax.fori_loop(0, nz, v_sum, jnp.zeros(o_vec.shape, f32))
    for h in range(heads):
        q_y(h).wait()
        q_on(h).start()
    for cp in [m_core, put_y] + [q_core(h) for h in range(heads)] + [q_on(h) for h in range(heads)]:
        cp.wait()
    for k in (0, 1):
        own_done(k).wait()
        for part_ in range(4):
            done_core(k, part_).wait()
    for ch in qkv_chains + [mix_chain, inn_chain, out_chain]:
        ch[2]()

    def vdrain(s, carry):
        for way in (0, 1):
            ok, b = spread_send(way, s, z, nz)

            @pl.when(ok)
            def _():
                vcopy(way, s, b).wait_send()

        return carry

    lax.fori_loop(1, nz, vdrain, 0)


def w_heads_of(pw, width):
    return pw[...].reshape(width, pw.shape[3])


def whole(nz, tokens, teacher, seg, valid, par, wq, wk, wv, vectors, mix, inn, out):
    trees, length, width = tokens.shape
    rz, wide = mix.shape[0], inn.shape[1]
    full, count, n = 4 * length, trees * length, width // 4
    heads = n // HD
    h2, w2, w4, w8 = width // 2, wide // 2, wide // 4, wide // 8
    vmem = pl.BlockSpec(memory_space=pltpu.VMEM)
    anyspace = pl.BlockSpec(memory_space=pl.ANY)
    shape = jax.ShapeDtypeStruct
    vec = (16, width)
    most = max(nz, 4)
    parts = 2 if rz % 32 == 0 else 1
    return pl.pallas_call(
        functools.partial(whole_body, nz),
        out_shape=(
            shape((count, width), bf16),
            shape((count, width), f32),
            shape((trees * full, width), bf16),
            shape((rz, wide), bf16),
            shape((4 * rz, width), bf16),
            shape((rz, width), bf16),
            shape((heads, 4, rz, 3 * HD), bf16),
            shape((trees, length, width), bf16),
            shape(vec, f32),
        ),
        in_specs=[anyspace] * 2 + [vmem] * 2 + [pl.BlockSpec(memory_space=pltpu.SMEM)] + [anyspace] * 3 + [vmem] * 9 + [anyspace] * 3,
        out_specs=[anyspace] * 5 + [vmem] * 4,
        scratch_shapes=[
            pltpu.SMEM((trees, NSEG), jnp.int32),
            V((trees, 4, length, width), bf16),
            V((trees, full, width), bf16),
            V((width, width), bf16),
            V((nz, rz, wide), bf16),
            V((wide, width), bf16),
            V((nz, parts, rz // parts, 3 * n), bf16),
            V((trees, full, 3 * n), bf16),
            V((trees, full, 8), f32),
            V((trees, full, 4 * HD), bf16),
            V((trees, full, n), bf16),
            V((4, trees, length, n), bf16),
            V((count, width), bf16),
            V((count, width), f32),
            V((count, width), f32),
            V((count, width), f32),
            V((count, width), bf16),
            V((count, width), bf16),
            V((count, width), bf16),
            V((count, width), bf16),
            V((count, 128), f32),
            V((count, 128), f32),
            V((width, width), bf16),
            V((full, trees * n), bf16),
            V((full, trees * n), bf16),
            V((full, HD), f32),
            V((full, HD), f32),
            V((nz, rz, w2), bf16),
            V((nz, 4 * rz, h2), bf16),
            V((width, h2), bf16),
            V((2, trees, length, width), bf16),
            V((nz, rz, w4), bf16),
            V((nz, 2 * rz, h2), bf16),
            V((nz, rz, w8), bf16),
            V((nz, rz, h2), bf16),
            V((trees, length, width), bf16),
            V((2, nz, rz, w8), bf16),
            V((2, nz, rz, h2), bf16),
            V((2, nz, rz, h2), bf16),
            V((heads, 2, nz, rz, 3 * HD), bf16),
            V((heads, nz, rz, 3 * HD), bf16),
            V((rz, h2), bf16),
            V((rz, h2), bf16),
            V((heads, rz, 3 * HD), bf16),
            V((3,) + vec, f32),
            V((nz,) + vec, f32),
            V(vec, f32),
            V((nz, 16, width), bf16),
            V((4, 8, count), jnp.int32),
            V(vec, f32),
            DMA((8,)), DMA((trees, 4)), DMA((trees * 4,)),
            DMA((nz,)), DMA((nz,)),
            DMA((3 + 3 * trees,)), DMA((3 + 3 * trees,)),
            DMA((6, 2, nz)), DMA((6, 2, nz)),
            DMA((2, 3, nz)), DMA((2, 3, nz)),
            DMA((3, 4, nz)), DMA((3, 4, nz)),
            DMA((trees, 3)), DMA((trees, 3)),
            DMA((3,)), DMA((3,)),
            DMA((5,)), DMA((5,)),
            DMA((2, most)), DMA((2, most)),
            DMA((3, nz)), DMA((3, nz)),
            DMA((2, nz)), DMA((2, nz)),
            DMA((3, trees)), DMA((3, trees)),
            DMA((2, 7)), DMA((2, 7)),
            DMA((7, 2, nz)), DMA((7, 2, nz)),
            DMA((25,)), DMA((25,)),
            DMA((2,)), DMA((2,)),
        ],
        compiler_params=pltpu.CompilerParams(
            collective_id=1, has_side_effects=True, vmem_limit_bytes=VMEM_LIMIT
        ),
        name="whole",
    )(tokens, teacher, seg, valid, par, wq, wk, wv, *vectors, mix, inn, out)


def finish_body(
    slots, spot, h_inn, h_out, h_mix, h_qkv, h_ig, h_one, vec,
    o_inn, o_out, o_mix, o_q, o_k, o_v, o_ig, o_loss, o0, o1, o2, o3, o4, o5, o6, o7, o8,
    inn, out, mix, qkv, ig, one, b_inn, b_out, b_mix, b_q, b_k, b_v, b_ig, get, put,
):
    sources = ((h_inn, inn), (h_out, out), (h_one, one), (h_ig, ig), (h_qkv, qkv), (h_mix, mix))
    loads = [pltpu.make_async_copy(a, b, get.at[i]) for i, (a, b) in enumerate(sources)]
    for cp in loads:
        cp.start()
    scale = slots / vec[spot : spot + 1, 0:1]
    stores = []

    def send(buf, dst):
        cp = pltpu.make_async_copy(buf, dst, put.at[len(stores)])
        cp.start()
        stores.append(cp)

    def each(size, fn):
        step = 64 if size % 64 == 0 else size

        def part(i, carry):
            fn(pl.ds(pl.multiple_of(i * step, step), step))
            return carry

        lax.fori_loop(0, size // step, part, 0)

    def scaled(dst, src):
        def part(rows):
            dst[rows] = src[rows].astype(f32) * scale

        each(src.shape[0], part)

    shard = lax.axis_index("shard")
    count = vec[spot : spot + 1, 0:1]
    o_loss[...] = jnp.sum(vec[spot - 1 : spot], axis=1, keepdims=True) / count
    width, size = vec.shape[1], o0.shape[0]
    turned = pltpu.roll(vec[0:8], lax.rem(width - shard * size, width), 1) * scale
    for i, o in enumerate((o0, o1, o2, o3, o4, o5, o6, o7)):
        o[...] = turned[i : i + 1, :size].reshape(size)
    wide, part = (spot - 9) * width, o8.shape[0]
    row = jnp.concatenate([vec[8 + i : 9 + i] for i in range(spot - 9)], axis=1)
    row = jnp.concatenate([row, jnp.zeros((7, wide), f32)], axis=0)
    row = pltpu.roll(row, lax.rem(wide - shard * part, wide), 1) * scale
    o8[...] = row[0:1, :part].reshape(part)

    loads[0].wait()
    scaled(b_inn, inn)
    send(b_inn, o_inn)
    loads[1].wait()
    scaled(b_out, out)
    send(b_out, o_out)
    loads[2].wait()
    loads[3].wait()
    for t in range(ig.shape[0]):

        def part(rows):
            b_ig[t, rows] = (one[t, rows] + ig[t, rows].astype(f32)) * scale

        each(ig.shape[1], part)
    send(b_ig, o_ig)
    loads[4].wait()
    for i, (buf, dst) in enumerate(((b_q, o_q), (b_k, o_k), (b_v, o_v))):
        for j in range(4):
            for h in range(qkv.shape[0]):
                at = (j * qkv.shape[0] + h) * HD
                buf[:, at : at + HD] = qkv[h, j, :, i * HD : (i + 1) * HD].astype(f32) * scale
        send(buf, dst)
    loads[5].wait()
    scaled(b_mix, mix)
    send(b_mix, o_mix)
    for cp in stores:
        cp.wait()


def finish(slots, spot, inn, out, mix, qkv, ig, one, vec, sizes):
    vmem = pl.BlockSpec(memory_space=pltpu.VMEM)
    anyspace = pl.BlockSpec(memory_space=pl.ANY)
    shapes = [inn.shape, out.shape, mix.shape, mix.shape, mix.shape, mix.shape, ig.shape]
    return pl.pallas_call(
        functools.partial(finish_body, slots, spot),
        out_shape=tuple(jax.ShapeDtypeStruct(sh, f32) for sh in shapes + [(1, 1)] + [(n,) for n in sizes]),
        in_specs=[anyspace] * 6 + [vmem],
        out_specs=[anyspace] * 7 + [vmem] * 10,
        scratch_shapes=[V(a.shape, a.dtype) for a in (inn, out, mix, qkv, ig, one)]
        + [V(sh, f32) for sh in shapes]
        + [DMA((6,)), DMA((7,))],
        compiler_params=pltpu.CompilerParams(vmem_limit_bytes=VMEM_LIMIT),
        name="finish",
    )(inn, out, mix, qkv, ig, one, vec)


def per_device(
    nz,
    tokens, teacher, seg_ids, parent_seg, valid,
    query_weight, query_bias, key_weight, value_weight, value_bias,
    mix_weight, mix_bias, first_gain, first_shift,
    inner_weight, inner_bias, outer_weight, outer_bias, second_gain, second_shift,
):
    trees, local_len, width = tokens.shape
    n_seq = lax.axis_size("seq")
    row_count = trees * local_len
    total_slots = row_count * lax.axis_size("replica") * nz * n_seq
    rz = mix_weight.shape[0]
    wide = inner_weight.shape[1]

    vectors = (
        query_bias, value_bias, mix_bias, first_gain, first_shift, outer_bias, second_gain, second_shift, inner_bias
    )

    layer_out, grad_one, _, r_inn, r_out, r_mix, r_qkv, r_ig, r_vec = whole(
        nz, tokens, teacher.reshape(row_count, width), seg_ids, valid, parent_seg,
        query_weight, key_weight, value_weight, vectors, mix_weight, inner_weight, outer_weight,
    )
    layer_out = layer_out.reshape(trees, local_len, width)
    spot = 8 + wide // width
    sizes = [rz] * 8 + [inner_bias.shape[0]]
    dinner, douter, dmix, dquery, dkey, dvalue, input_grad, loss, *rows = finish(
        total_slots, spot + 1, r_inn, r_out, r_mix, r_qkv, r_ig,
        grad_one.reshape(trees, local_len, width), r_vec, sizes,
    )
    return (
        layer_out, loss[0, 0], input_grad,
        dquery, rows[0], dkey, dvalue, rows[1],
        dmix, rows[2], rows[3], rows[4],
        dinner, rows[8], douter, rows[5], rows[6], rows[7],
    )


def solution(mesh):
    rows = P(("replica", "shard"), "seq", None)
    line = P(("replica", "shard"), "seq")
    mat = P("shard", None)
    row = P("shard")
    placed = (
        rows, rows, line, P(("replica", "shard"), None), line,
        mat, row, mat, mat, row, mat, row, row, row, mat, row, mat, row, row, row,
    )
    return jax.shard_map(
        functools.partial(per_device, mesh.shape["shard"]),
        mesh=mesh,
        in_specs=placed,
        out_specs=(
            rows, P(), rows,
            mat, row, mat, mat, row, mat, row, row, row, mat, row, mat, row, row, row,
        ),
        check_vma=False,
    )
```

```python
import functools

import jax
import jax.numpy as jnp
from jax import lax
from jax.experimental import pallas as pl
from jax.experimental.pallas import tpu as pltpu
from jax.sharding import PartitionSpec as P

HEADS = 12
HD = 64
NSEG = 8
MESH = pl.DeviceIdType.MESH
BIG = 1e30
norm_eps = 1e-12
f32 = jnp.float32
bf16 = jnp.bfloat16
VMEM_LIMIT = 63 * 1024 * 1024


class Place:
    def __init__(self, nz):
        self.nz = nz
        self.x = lax.axis_index("replica")
        self.z = lax.axis_index("shard")
        self.q = lax.axis_index("seq")
        self.y = self.q // 2
        self.c = self.q % 2
        x, z, y, c = self.x, self.z, self.y, self.c
        self.core = (x, z, 2 * y + 1 - c)
        self.ynb = (x, z, 2 * (1 - y) + c)
        self.xnb = (1 - x, z, self.q)
        self.right = (x, z + 1, self.q)
        self.left = (x, z - 1, self.q)

    def greet(self, more):
        bar = pltpu.get_barrier_semaphore()
        for peer in [self.core, self.ynb, self.xnb] + more:
            pl.semaphore_signal(bar, inc=1, device_id=peer, device_id_type=MESH)

        @pl.when(self.z > 0)
        def _():
            pl.semaphore_signal(bar, inc=1, device_id=self.left, device_id_type=MESH)

        @pl.when(self.z < self.nz - 1)
        def _():
            pl.semaphore_signal(bar, inc=1, device_id=self.right, device_id_type=MESH)

        peers = 3 + len(more) + (self.z > 0).astype(jnp.int32) + (self.z < self.nz - 1).astype(jnp.int32)
        pl.semaphore_wait(bar, peers)


def rcopy(src, dst, ssem, rsem, dev):
    return pltpu.make_async_remote_copy(
        src_ref=src, dst_ref=dst, send_sem=ssem, recv_sem=rsem, device_id=dev, device_id_type=MESH
    )


def both(a, b):
    return jnp.logical_and(a, b)


def dot_nt(a, b):
    return lax.dot_general(a, b, (((1,), (1,)), ((), ())), preferred_element_type=f32)


def dot_tn(a, b):
    return lax.dot_general(a, b, (((0,), (0,)), ((), ())), preferred_element_type=f32)


def dot_nn(a, b):
    return jnp.dot(a, b, preferred_element_type=f32)


def add_to(dst, src):
    dst[...] = (dst[...].astype(f32) + src[...].astype(f32)).astype(dst.dtype)


def lanes(start, size):
    return pl.ds(pl.multiple_of(start, 128), size)


def rows_at(start, size):
    return pl.ds(pl.multiple_of(start, 8), size)


def row_mean(v):
    return jnp.sum(v, axis=1, keepdims=True) * (1.0 / v.shape[1])


def norm_back(grad_hat, hat, inv):
    return inv * (grad_hat - row_mean(grad_hat) - hat * row_mean(grad_hat * hat))


def fold(v):
    return jnp.sum(v.reshape(v.shape[0] // 8, 8, v.shape[1]), axis=0)


def total_row(v):
    return jnp.sum(v, axis=0, keepdims=True)


QB = 256
RB = 32
DMA = pltpu.SemaphoreType.DMA
V = pltpu.VMEM


def spread_send(way, s, z, nz):
    if way == 0:
        return both(z >= s - 1, z < nz - 1), z - s + 1
    return both(z <= nz - s, z > 0), z + s - 1


def spread_get(way, s, z, nz):
    if way == 0:
        return z >= s, z - s
    return z <= nz - 1 - s, z + s


def whole_body(
    nz, x_hbm, tea_hbm, seg_ref, valid_ref, par_ref, wq_hbm, wk_hbm, wv_hbm, *more,
):
    vectors, (mix_hbm, inn_hbm, out_hbm) = more[:9], more[9:12]
    (
        y_hbm, one_hbm, xa_hbm, o_inn, o_out, o_mix, o_qkv, o_ig, o_vec, bits, hid, slp, mixa, inna, outa, pw, qkv,
        lse, feat, att, blocks, tok, A1, A2, A3, fl, gb, gp, tea, vm, inv1, mixg, gsend, gat, dk, dv, ci, co, cm, cg, xi, yo,
        yi, xo, yg, zi, zo, zm, zq, aq, xm, ym, xq, v_in, v_z, v_acc, sma, tga, vecs, loc, sav, rel, px, pr2, xs,
        xr, zs, zr, fs, fr, cs, cr, hs, hr, gs_, gr_, ks, kr, ds_, dr_, s1, r1, s2, r2, is_, ir, ps, pr, bs, br, es, er, vs, vr,
    ) = more[12:]
    p = Place(nz)
    z, c, y, x, q = p.z, p.c, p.y, p.x, p.q
    rz, width = mix_hbm.shape
    wide = inn_hbm.shape[1]
    trees, length = x_hbm.shape[0], x_hbm.shape[1]
    full = qkv.shape[1]
    count = trees * length
    n = width // 4
    heads = n // HD
    chunks = wide // width
    h2, w2, w4, w8 = width // 2, wide // 2, wide // 4, wide // 8
    cross = (x, z, 2 * (1 - y) + 1 - c)
    qy = 2 * (1 - y) + c
    o4 = 4 * rz

    load = [
        pltpu.make_async_copy(x_hbm, hid.at[:, q], loc.at[0]),
        pltpu.make_async_copy(wq_hbm, slp.at[0, pl.ds(0, rz)], loc.at[1]),
        pltpu.make_async_copy(wk_hbm, slp.at[0, pl.ds(256, rz)], loc.at[2]),
        pltpu.make_async_copy(wv_hbm, slp.at[0, pl.ds(512, rz)], loc.at[3]),
        pltpu.make_async_copy(mix_hbm, mixa.at[rows_at(z * rz, rz)], loc.at[4]),
        pltpu.make_async_copy(inn_hbm, inna.at[z], loc.at[5]),
        pltpu.make_async_copy(out_hbm, outa.at[rows_at(z * o4, o4)], loc.at[6]),
        pltpu.make_async_copy(tea_hbm, tea, loc.at[7]),
    ]
    for cp in load:
        cp.start()
    for t in range(trees):
        seg = seg_ref[t : t + 1, :]
        tga[q, 0:1, t * length : (t + 1) * length] = jnp.where(
            valid_ref[t : t + 1, :] == 1, seg, seg + NSEG
        )
    p.greet([cross])

    def x_core(t):
        return rcopy(hid.at[t, q], hid.at[t, q], xs.at[2 + t], xr.at[2 + t], p.core)

    def x_y(t):
        return rcopy(hid.at[t, q], hid.at[t, q], xs.at[2 + trees + t], xr.at[2 + trees + t], p.ynb)

    def x_on(t):
        return rcopy(hid.at[t, qy], hid.at[t, qy], xs.at[2 + 2 * trees + t], xr.at[2 + 2 * trees + t], p.core)

    t_core = rcopy(tga.at[q], tga.at[q], xs.at[0], xr.at[0], p.core)
    t_y = rcopy(tga.at[q], tga.at[q], xs.at[1], xr.at[1], p.ynb)
    t_on = rcopy(tga.at[qy], tga.at[qy], xs.at[2 + 3 * trees], xr.at[2 + 3 * trees], p.core)
    t_y.start()
    t_core.start()
    load[0].wait()
    for t in range(trees):
        x_y(t).start()
    for t in range(trees):
        x_core(t).start()

    parts, rows_in = pw.shape[1], pw.shape[2]
    back = lax.rem(width - q * n, width)
    for i in range(3):
        load[1 + i].wait()
        turned = pltpu.roll(slp[0, i * 256 : i * 256 + rz].astype(f32), back, 1)
        for h in range(heads):
            for half in range(parts):
                own = turned[half * rows_in : (half + 1) * rows_in, h * HD : (h + 1) * HD]
                pw[z, half, :, (3 * h + i) * HD : (3 * h + i + 1) * HD] = own.astype(bf16)
    def row_of(ref, size):
        own = ref[...].astype(f32).reshape(1, ref.shape[0])
        if ref.shape[0] == size:
            return own
        return jnp.concatenate([own, jnp.zeros((1, size - ref.shape[0]), f32)], axis=1)

    small = jnp.concatenate([row_of(v, width) for v in vectors[:8]], axis=0)
    wide_row = jnp.concatenate([row_of(vectors[8], wide), jnp.zeros((7, wide), f32)], axis=0)
    wide_row = pltpu.roll(wide_row, z * (wide // nz), 1)
    sma[z] = jnp.concatenate(
        [pltpu.roll(small, z * rz, 1)]
        + [wide_row[0:1, j * width : (j + 1) * width] for j in range(chunks)]
        + [jnp.zeros((8 - chunks, width), f32)],
        axis=0,
    ).astype(bf16)

    def at_row(ref, b, size):
        return ref.at[rows_at(b * size, size)]

    def piece_of(k, b, xx, yy):
        if k == 0:
            return inna.at[b, :, lanes(c * w2 + (2 * xx + yy) * w8, w8)]
        return outa.at[rows_at(b * o4 + 2 * xx * rz, 2 * rz), lanes(c * h2, h2)]

    there = {
        0: lambda b: pw.at[b, x if parts == 2 else 0],
        1: lambda b: sma.at[b],
        3: lambda b: mixa.at[rows_at(b * rz, rz), lanes(c * h2, h2)],
        4: lambda b: piece_of(0, b, x, y),
        5: lambda b: piece_of(1, b, x, y),
    }

    def zcopy(k, way, s, b):
        dev = p.right if way == 0 else p.left
        return rcopy(there[k](b), there[k](b), zs.at[k, way, s], zr.at[k, way, s], dev)

    def start_step(k, s):
        for way in (0, 1):
            cond, b = spread_send(way, s, z, nz)

            @pl.when(both(cond, s <= nz - 1))
            def _():
                zcopy(k, way, s, b).start()

    def each(s, fn):
        for way in (0, 1):
            cond, b = spread_get(way, s, z, nz)

            @pl.when(cond)
            def _():
                fn(way, b)

    def take(k, s):
        each(s, lambda way, b: zcopy(k, way, s, b).wait_recv())

    def to_y(k, b):
        return rcopy(piece_of(k, b, x, y), piece_of(k, b, x, y), fs.at[k, 0, b], fr.at[k, 0, b], p.ynb)

    def to_x(k, b):
        return rcopy(piece_of(k, b, x, y), piece_of(k, b, x, y), fs.at[k, 1, b], fr.at[k, 1, b], p.xnb)

    def onward(k, b):
        return rcopy(piece_of(k, b, x, 1 - y), piece_of(k, b, x, 1 - y), fs.at[k, 2, b], fr.at[k, 2, b], p.xnb)

    def core_copy(k, b, part):
        if k == 2:
            piece = there[3](b)
        else:
            piece = piece_of(k, b, x if part % 2 == 0 else 1 - x, y if part < 2 else 1 - y)
        return rcopy(piece, piece, cs.at[k, part, b], cr.at[k, part, b], p.core)

    def pw_x(b):
        return rcopy(pw.at[b, x], pw.at[b, x], px.at[b], pr2.at[b], p.xnb)

    for k in (0, 1):
        start_step(k, 1)

    def small_step(s, carry):
        for k in (0, 1):
            take(k, s)
        for k in (0, 1):
            start_step(k, s + 1)
        if parts == 2:
            each(s, lambda way, b: pw_x(b).start())
        return carry

    lax.fori_loop(1, nz - 1, small_step, 0)
    for i in (4, 5, 6, 7):
        load[i].wait()
    for k in (4, 3, 5):
        start_step(k, 1)
    for k in (0, 1):
        take(k, nz - 1)
    if parts == 2:
        each(nz - 1, lambda way, b: pw_x(b).start())

    def mix_step(s):
        def got(way, b):
            zcopy(3, way, s, b).wait_recv()
            core_copy(2, b, 0).start()

        each(s, got)
        start_step(3, s + 1)

    def z_step(k, s):
        def got(way, b):
            zcopy(4 + k, way, s, b).wait_recv()
            if k == 0:
                to_y(k, b).start()
            to_x(k, b).start()

        each(s, got)
        start_step(4 + k, s + 1)
        each(s, lambda way, b: core_copy(k, b, 0).start())

    def pass_on(k, s):
        def got(way, b):
            to_y(k, b).wait_recv()
            onward(k, b).start()
            core_copy(k, b, 2).start()

        each(s, got)

    def rest_of(k, s):
        def got(way, b):
            to_x(k, b).wait_recv()
            core_copy(k, b, 1).start()
            if k == 0:
                onward(k, b).wait_recv()
                core_copy(k, b, 3).start()

        each(s, got)

    def from_core(k, s):
        def got(way, b):
            for part in range((4, 2, 1)[k]):
                core_copy(k, b, part).wait_recv()

        each(s, got)

    def all_steps(*fns):
        def one(s, carry):
            for fn in fns:
                fn(s)
            return carry

        lax.fori_loop(1, nz, one, 0)

    placed = nz == 4

    small = lax.fori_loop(0, nz, lambda i, v: v + sma[i].astype(f32), jnp.zeros(vecs.shape, f32))
    vecs[...] = small
    turned = pltpu.roll(small, back, 1)
    bias = []
    for h in range(heads):
        cols = slice(h * HD, (h + 1) * HD)
        bias += [turned[0:1, cols], jnp.zeros((1, HD), f32), turned[1:2, cols]]
    bias = jnp.concatenate(bias, axis=1)

    t_y.wait_recv()
    t_on.start()
    t_core.wait()
    t_on.wait()

    row = lax.broadcasted_iota(jnp.int32, (16, 4 * HD), 0)
    lane = lax.broadcasted_iota(jnp.int32, (16, 4 * HD), 1)
    trow = lax.broadcasted_iota(jnp.int32, (16, full), 0)
    vrow = lax.broadcasted_iota(jnp.int32, (16, length), 0)
    ones = jnp.ones((16, 128), bf16)
    for t in range(trees):
        bits[t, 0] = jnp.int32(1)
        for s in range(1, NSEG):
            bits[t, s] = bits[t, par_ref[t, s]] + (1 << s)
        seen = jnp.zeros((16, 4 * HD), jnp.int32)
        for a in range(NSEG):
            seen = jnp.where(row == a, bits[t, a], seen)
        at = jnp.clip(lane - HD, 0, NSEG)
        unseen = ((seen >> at) & 1) == 0
        q_side = both(both(row < NSEG, both(lane >= HD, lane <= HD + NSEG)), unseen)
        k_side = both(row <= NSEG, lane == row + 3 * HD)
        table = jnp.where(q_side, -BIG, jnp.where(k_side, 1.0, 0.0)).astype(bf16)
        tag = jnp.concatenate(
            [tga[j, 0:1, t * length : (t + 1) * length] for j in range(full // length)], axis=1
        )
        gone = tag >= NSEG
        seg = jnp.where(gone, tag - NSEG, tag)
        seg = jnp.broadcast_to(seg, (16, full))
        gone = jnp.broadcast_to(jnp.where(gone, 1, 0), (16, full))
        hot = jnp.where(trow == NSEG, gone, jnp.where(trow == seg, 1, 0)).astype(f32).astype(bf16)
        feat[t] = dot_tn(hot, table).astype(bf16)
        here = jnp.broadcast_to(valid_ref[t : t + 1, :], (16, length))
        here = jnp.where(vrow == 0, here, 0).astype(f32).astype(bf16)
        vm[t * length : (t + 1) * length] = dot_tn(here, ones)

    t_y.wait_send()
    if parts == 2:
        all_steps(lambda s: each(s, lambda way, b: pw_x(b).wait()))
    w_heads = w_heads_of(pw, width)
    saves = []

    def project(t):
        x_core(t).wait()
        x_on(t).wait()
        for j in range(4):
            cp = pltpu.make_async_copy(
                hid.at[t, j], xa_hbm.at[pl.ds((t * 4 + j) * length, length)], sav.at[t, j]
            )
            cp.start()
            saves.append(cp)
        qkv[t] = (dot_nn(hid[t].reshape(full, width), w_heads) + bias).astype(bf16)

    for t in range(trees):
        x_y(t).wait()
        x_on(t).start()
        if t == 0:
            project(0)


    def part(h, i):
        return slice((3 * h + i) * HD, (3 * h + i + 1) * HD)

    def queries_of(t, rows, h):
        return jnp.concatenate([qkv[t, rows, part(h, 0)] * 0.125, feat[t, rows, HD : 2 * HD]], axis=1)

    def keys_of(t, h):
        return jnp.concatenate([qkv[t, :, part(h, 1)], feat[t, :, 3 * HD : 4 * HD]], axis=1)

    def token_rows(j):
        return pl.ds(pl.multiple_of(j * length, length), length)

    def send_heads(t, d):
        to = lax.rem(q + d, 4)
        return rcopy(
            att.at[t, token_rows(to)], blocks.at[q, t], hs.at[t, d - 1], hr.at[t, d - 1], (x, z, to)
        )

    def run_at(slots, first, i):
        for k in range(full // QB):
            fns = slots.get(first + k, [])
            if fns:

                @pl.when(i == k)
                def _():
                    for fn, *args in fns:
                        fn(*args)

    slots = {
        1: [(z_step, 0, 1)],
        5: [(mix_step, 1)],
        9: [(pass_on, 0, 1)],
        12: [(z_step, 0, 2)],
        13: [(z_step, 1, 1)],
        14: [(mix_step, 2)],
        18: [(pass_on, 0, 2)],
        21: [(z_step, 0, 3)],
        23: [(z_step, 1, 2)],
    }
    if not placed:
        slots = {}
    per_head = full // QB
    for t in range(trees):
        if t > 0:
            project(t)
        for h in range(heads):
            keys = keys_of(t, h)
            values = qkv[t, :, part(h, 2)]

            def block(i, carry):
                rows = pl.ds(pl.multiple_of(i * QB, QB), QB)
                s = dot_nt(queries_of(t, rows, h), keys)
                peak = jnp.max(s, axis=1, keepdims=True)
                e = jnp.exp(s - peak)
                total = jnp.sum(e, axis=1, keepdims=True)
                o = dot_nn(e.astype(bf16), values) / total
                att[t, rows, h * HD : (h + 1) * HD] = o.astype(bf16)
                lse[t, rows, h : h + 1] = peak + jnp.log(total)
                run_at(slots, (t * heads + h) * per_head, i)
                return carry

            lax.fori_loop(0, full // QB, block, 0)
        for d in (1, 2, 3):
            send_heads(t, d).start()
    for t in range(trees):
        blocks[q, t] = att[t, token_rows(q)]
    if placed:
        mix_step(3)
        pass_on(0, 3)
    else:
        all_steps(mix_step)
    for t in range(trees):
        for d in (1, 2, 3):
            send_heads(t, d).wait()

    for j in range(4):
        tok[:, j * n : (j + 1) * n] = blocks[j].reshape(count, n)
    all_steps(functools.partial(from_core, 2))
    A3[...] = dot_nn(tok[...], mixa[...])
    if placed:
        rest_of(0, 1)
        rest_of(0, 2)
        z_step(1, 3)

    def rows_of(i):
        return pl.ds(pl.multiple_of(i * RB, RB), RB)

    per = length // RB

    def first_norm(i, carry):
        rows = rows_of(i)
        own = hid[i // per, q, rows_of(i % per)].astype(f32)
        r1 = own + A3[rows] + vecs[2:3]
        center = r1 - row_mean(r1)
        inv = lax.rsqrt(row_mean(center * center) + norm_eps)
        hat = center * inv
        A1[rows] = hat
        inv1[rows] = jnp.broadcast_to(inv, (RB, 128))
        fl[rows] = (hat * vecs[3:4] + vecs[4:5]).astype(bf16)
        return carry

    lax.fori_loop(0, count // RB, first_norm, 0, unroll=2)
    for cp in saves:
        cp.wait()
    if placed:
        rest_of(0, 3)
    else:
        for k in (0, 1):
            all_steps(*[functools.partial(fn, k) for fn in ((z_step, pass_on, rest_of), (z_step, rest_of))[k]])
    all_steps(functools.partial(from_core, 0))

    def inner_chunk(j):
        return inna[:, :, j * width : (j + 1) * width].reshape(width, width)

    def hid_chunk(j):
        return hid[j // 2, 2 * (j % 2) : 2 * (j % 2) + 2].reshape(count, width)

    for j in range(chunks):
        A3[...] = dot_nn(fl[...], inner_chunk(j))

        def gelu(i, carry):
            rows = rows_of(i)
            pre = A3[rows] + vecs[8 + j : 9 + j]
            cdf = 0.5 + 0.5 * lax.erf(pre * (0.5**0.5))
            hid[j // 2, 2 * (j % 2) + i // per, rows_of(i % per)] = (pre * cdf).astype(bf16)
            slope = cdf + pre * jnp.exp(-0.5 * pre * pre) * 0.3989422804014327
            slp[j // 2, pl.ds(pl.multiple_of((j % 2) * count + i * RB, RB), RB)] = slope.astype(bf16)
            return carry

        lax.fori_loop(0, count // RB, gelu, 0, unroll=2)
        if placed and j == 1:
            rest_of(1, 1)
        if placed and j == 2:
            rest_of(1, 2)
            rest_of(1, 3)
    all_steps(functools.partial(from_core, 1))
    for j in range(chunks):
        more = dot_nn(hid_chunk(j), outa[j * width : (j + 1) * width])
        if j == 0:
            A2[...] = more
        else:
            A2[...] += more

    def drain(s, carry):
        for k in (0, 1, 3, 4, 5):
            for way in (0, 1):
                cond, b = spread_send(way, s, z, nz)

                @pl.when(cond)
                def _():
                    zcopy(k, way, s, b).wait_send()

        def end(way, b):
            core_copy(2, b, 0).wait_send()
            to_y(0, b).wait_send()
            onward(0, b).wait_send()
            for k in (0, 1):
                to_x(k, b).wait_send()
                for part in range((4, 2)[k]):
                    core_copy(k, b, part).wait_send()

        each(s, end)
        return carry

    lax.fori_loop(1, nz, drain, 0)

    zero = jnp.zeros((8, width), f32)

    def second_norm(i, carry):
        loss, dgain, dshift, dbias = carry
        rows = rows_of(i)
        first = A1[rows] * vecs[3:4] + vecs[4:5]
        r2 = first + A2[rows] + vecs[5:6]
        center = r2 - row_mean(r2)
        inv = lax.rsqrt(row_mean(center * center) + norm_eps)
        hat = center * inv
        out = hat * vecs[6:7] + vecs[7:8]
        err = out - tea[rows].astype(f32)
        tea[rows] = out.astype(bf16)
        weighted = vm[rows, 0:1] * err
        grad = 2.0 * weighted
        g2 = norm_back(grad * vecs[6:7], hat, inv)
        A2[rows] = g2
        low = g2.astype(bf16)
        gb[rows] = low
        return (
            loss + fold(weighted * err),
            dgain + fold(grad * hat),
            dshift + fold(grad),
            dbias + fold(low.astype(f32)),
        )

    loss, dgain, dshift, dbias = lax.fori_loop(0, count // RB, second_norm, (zero, zero, zero, zero), unroll=2)
    put_y = pltpu.make_async_copy(tea, y_hbm, loc.at[0])
    put_y.start()
    v_acc[...] = jnp.zeros_like(v_acc)
    spot = 8 + chunks
    v_acc[5:6] = total_row(dbias)
    v_acc[6:7] = total_row(dgain)
    v_acc[7:8] = total_row(dshift)
    v_acc[spot : spot + 1] = total_row(loss)
    v_acc[spot + 1 : spot + 2, 0:128] = total_row(vm[...])

    def c_out(d):
        return rcopy(outa.at[rows_at(d * o4, o4), lanes((1 - c) * h2, h2)], co.at[d], ds_.at[0, d], dr_.at[0, d], p.core)

    def chunk_of(core, k):
        return (chunks - 1) * core + (1 - 2 * core) * k

    def c_inn(k):
        src = inna.at[:, :, lanes(chunk_of(1 - c, k) * width, width)]
        return rcopy(src, ci.at[:, :, pl.ds(k * width, width)], ds_.at[1, k], dr_.at[1, k], p.core)

    def out_y(d):
        src = co.at[d, rows_at((1 - y) * 2 * rz, 2 * rz)]
        return rcopy(src, yo.at[d], s1.at[0, d], r1.at[0, d], p.ynb)

    def inn_x(d, k):
        src = ci.at[d, :, lanes(k * width + (1 - x) * w8, w8)]
        return rcopy(src, xi.at[d, :, pl.ds(k * w8, w8)], s1.at[1 + k, d], r1.at[1 + k, d], p.xnb)

    def out_x(d):
        src = yo.at[d, rows_at((1 - x) * rz, rz)]
        return rcopy(src, xo.at[d], s2.at[0, d], r2.at[0, d], p.xnb)

    def inn_y(d):
        return rcopy(xi.at[d, :, lanes((1 - y) * w8, w8)], yi.at[d], s2.at[1, d], r2.at[1, d], p.ynb)

    def span(lo, hi, fn):
        if hi - lo == 1:
            fn(lo)
            return

        def one(i, carry):
            fn(i)
            return carry

        lax.fori_loop(lo, hi, one, 0)

    def of_chunk(j, fn):
        span(j * nz // chunks, (j + 1) * nz // chunks, fn)

    def group(g, fn):
        def pair(i):
            fn(nz - 1 - i)
            fn(i)

        span(g * nz // 4, (g + 1) * nz // 4, pair)

    def out_chip(d):
        c_out(d).wait()
        for j in range(4):
            add_to(co.at[d, j * rz : (j + 1) * rz], outa.at[rows_at(d * o4 + j * rz, rz), lanes(c * h2, h2)])
        out_y(d).start()

    def inn_chip(g, k):
        if g == 0:
            c_inn(k).wait()

        def one(d):
            for j in range(2):
                at = slice(k * width + j * h2, k * width + (j + 1) * h2)
                add_to(ci.at[d, :, at], inna.at[d, :, lanes(chunk_of(c, k) * width + j * h2, h2)])
            inn_x(d, k).start()

        group(g, one)

    def out_half(d):
        out_y(d).wait()
        add_to(yo.at[d, :rz], co.at[d, rows_at(y * 2 * rz, rz)])
        add_to(yo.at[d, rz:], co.at[d, rows_at(y * 2 * rz + rz, rz)])
        out_x(d).start()

    def inn_half(g, k):
        def one(d):
            inn_x(d, k).wait()
            add_to(xi.at[d, :, k * w8 : (k + 1) * w8], ci.at[d, :, lanes(k * width + x * w8, w8)])

        group(g, one)

    def inn_other(g):
        group(g, lambda d: inn_y(d).start())

    def out_quarter(d):
        out_x(d).wait()
        add_to(xo.at[d], yo.at[d, rows_at(x * rz, rz)])

    def inn_quarter(d):
        inn_y(d).wait()
        add_to(yi.at[d], xi.at[d, :, lanes(y * w8, w8)])

    order = [3, 0, 2, 1]
    for step, j in enumerate(order):
        A3[...] = dot_nt(gb[...], outa[j * width : (j + 1) * width])

        def slopes(i, carry):
            rows = rows_of(i)
            slope = slp[j // 2, pl.ds(pl.multiple_of((j % 2) * count + i * RB, RB), RB)]
            low = (A3[rows] * slope.astype(f32)).astype(bf16)
            gp[rows] = low
            return carry + fold(low.astype(f32))

        v_acc[8 + j : 9 + j] = total_row(lax.fori_loop(0, count // RB, slopes, zero, unroll=2))
        outa[j * width : (j + 1) * width] = dot_tn(hid_chunk(j), gb[...]).astype(bf16)
        of_chunk(j, lambda d: c_out(d).start())
        A2[...] += dot_nt(gp[...], inner_chunk(j))
        inna[:, :, j * width : (j + 1) * width] = dot_tn(fl[...], gp[...]).astype(bf16).reshape(nz, rz, width)

        @pl.when(c == 1 - j // 2)
        def _():
            c_inn(step // 2).start()

        if step == 1:
            of_chunk(order[0], out_chip)
        if step == 2:
            inn_chip(0, 0)
            inn_chip(1, 0)

    def first_back(i, carry):
        dgain, dshift, dbias = carry
        rows = rows_of(i)
        grad = A2[rows]
        hat = A1[rows]
        g1 = norm_back(grad * vecs[3:4], hat, inv1[rows, 0:1])
        A2[rows] = g1
        low = g1.astype(bf16)
        gb[rows] = low
        return dgain + fold(grad * hat), dshift + fold(grad), dbias + fold(low.astype(f32))

    dgain, dshift, dbias = lax.fori_loop(0, count // RB, first_back, (zero, zero, zero), unroll=2)
    v_acc[2:3] = total_row(dbias)
    v_acc[3:4] = total_row(dgain)
    v_acc[4:5] = total_row(dshift)
    put_one = pltpu.make_async_copy(A2, one_hbm, loc.at[1])
    put_one.start()

    for j in range(4):
        part_j = dot_nt(gb[...], mixa[j * n : (j + 1) * n]).astype(bf16)
        for t in range(trees):
            gsend[j * length : (j + 1) * length, t * n : (t + 1) * n] = part_j[t * length : (t + 1) * length]

    def send_grads(d):
        to = lax.rem(q + d, 4)
        return rcopy(gsend.at[token_rows(to)], gat.at[token_rows(q)], gs_.at[d - 1], gr_.at[d - 1], (x, z, to))

    for d in (1, 2, 3):
        send_grads(d).start()
    gat[token_rows(q)] = gsend[token_rows(q)]

    of_chunk(order[0], out_half)
    inn_chip(0, 1)
    of_chunk(order[1], out_chip)
    inn_chip(1, 1)
    of_chunk(order[2], out_chip)
    reload = [
        pltpu.make_async_copy(
            xa_hbm.at[pl.ds(i * length, length)], outa.at[pl.ds(i * length, length)], rel.at[i]
        )
        for i in range(trees * 4)
    ]

    def out_last():
        of_chunk(order[-1], out_chip)
        for cp in reload:
            cp.start()

    def reloaded():
        for cp in reload:
            cp.wait()

    mixg[...] = dot_tn(tok[...], gb[...]).astype(bf16)
    c_mix = rcopy(mixg.at[:, lanes((1 - c) * h2, h2)], cm, ks.at[3], kr.at[3], p.core)
    c_mix.start()

    def chain(k, acc, buf):
        def copy(way, s, d):
            dev = p.right if way == 0 else p.left
            return rcopy(acc(d), buf(way, d), bs.at[k, way, s], br.at[k, way, s], dev)

        def sending(way, s):
            if way == 0:
                d = z + nz - s
                return both(d <= nz - 1, z < nz - 1), d
            d = z - nz + s
            return both(d >= 0, z > 0), d

        def getting(way, s):
            if way == 0:
                d = z - 1 + nz - s
                return both(d <= nz - 1, z > 0), d
            d = z + 1 - nz + s
            return both(d >= 0, z < nz - 1), d

        def send(s):
            for way in (0, 1):
                ok, d = sending(way, s)

                @pl.when(both(ok, s <= nz - 1))
                def _():
                    copy(way, s, d).start()

        def get(s):
            for way in (0, 1):
                ok, d = getting(way, s)

                @pl.when(ok)
                def _():
                    copy(way, s, d).wait_recv()
                    add_to(acc(d), buf(way, d))

        def drain(s, carry):
            for way in (0, 1):
                ok, d = sending(way, s)

                @pl.when(ok)
                def _():
                    copy(way, s, d).wait_send()

            return carry

        return send, get, lambda: lax.fori_loop(1, nz, drain, 0)

    def step_of(ch, s):
        ch[1](s)
        ch[0](s + 1)

    mix_chain = chain(3, lambda d: cm.at[rows_at(d * rz, rz)], lambda way, d: zm.at[way, d])
    inn_chain = chain(4, lambda d: yi.at[d], lambda way, d: zi.at[way, d])
    out_chain = chain(5, lambda d: xo.at[d], lambda way, d: zo.at[way, d])

    def head_chain(h):
        return chain(h, lambda d: aq.at[h, d], lambda way, d: zq.at[h, way, d])

    qkv_chains = [head_chain(h) for h in range(heads)]

    c_mix.wait()

    def mix_sum(i, carry):
        block = rows_at(i * rz, rz)
        add_to(cm.at[block], mixg.at[block, lanes(c * h2, h2)])
        return carry

    lax.fori_loop(0, nz, mix_sum, 0)
    mix_chain[0](1)
    for d in (1, 2, 3):
        send_grads(d).wait()

    def head_weights(h):
        cols = slice(3 * h * HD, 3 * (h + 1) * HD)
        grad = dot_tn(outa[0:full], slp[0, :, cols])
        for t in range(1, trees):
            grad = grad + dot_tn(outa[t * full : (t + 1) * full], slp[t, :, cols])
        aq[h] = grad.astype(bf16).reshape(nz, rz, 3 * HD)
        qkv_chains[h][0](1)

    def q_x(h):
        return rcopy(aq.at[h, z], xq.at[h], es.at[13 + h], er.at[13 + h], p.xnb)

    def q_y(h):
        return rcopy(o_qkv.at[h, q], o_qkv.at[h, q], es.at[16 + h], er.at[16 + h], p.ynb)

    def q_core(h):
        return rcopy(o_qkv.at[h, q], o_qkv.at[h, q], es.at[19 + h], er.at[19 + h], p.core)

    def q_on(h):
        return rcopy(o_qkv.at[h, qy], o_qkv.at[h, qy], es.at[22 + h], er.at[22 + h], p.core)

    def q_sum(h):
        q_x(h).wait()
        o_qkv[h, q] = (aq[h, z].astype(f32) + xq[h].astype(f32)).astype(bf16)
        q_y(h).start()
        q_core(h).start()

    x_m = rcopy(cm.at[rows_at(z * rz, rz)], xm, es.at[1], er.at[1], p.xnb)
    y_m = rcopy(xm, ym, es.at[4], er.at[4], p.ynb)

    def big_step(s):
        step_of(inn_chain, s)
        step_of(out_chain, s)

    def first_big():
        inn_chain[0](1)
        out_chain[0](1)

    def ig_of(t):
        for j in range(4):
            rows = slice(j * length, (j + 1) * length)
            hid[t, j] = dot_nt(slp[t, rows, : 3 * n], w_heads_of(pw, width)).astype(bf16)
        for b in range(2):
            c_ig(t, b).start()

    def c_ig(t, b):
        return rcopy(hid.at[t, 2 * b + 1 - c], cg.at[b, t], is_.at[b, t], ir.at[b, t], p.core)

    def ig_y(t):
        return rcopy(cg.at[1 - y, t], yg.at[t], is_.at[2, t], ir.at[2, t], p.ynb)

    def ig_chip(t):
        for b in range(2):
            c_ig(t, b).wait()
            add_to(cg.at[b, t], hid.at[t, 2 * b + c])
        ig_y(t).start()

    def ig_end(t):
        ig_y(t).wait()
        o_ig[t] = (cg[y, t].astype(f32) + yg[t].astype(f32)).astype(o_ig.dtype)

    def done_piece(k, xx, yy):
        if k == 0:
            return o_inn.at[:, lanes(chunk_of(c, yy) * width + xx * w8, w8)]
        return o_out.at[rows_at((2 * yy + xx) * rz, rz), lanes(c * h2, h2)]

    def own_done(k):
        return pltpu.make_async_copy((yi if k == 0 else xo).at[z], done_piece(k, x, y), loc.at[2 + k])

    def done_y(k):
        return rcopy((yi if k == 0 else xo).at[z], done_piece(k, x, y), ps.at[k, 0], pr.at[k, 0], p.ynb)

    def done_x(k):
        return rcopy((yi if k == 0 else xo).at[z], done_piece(k, x, y), ps.at[k, 1], pr.at[k, 1], p.xnb)

    def done_on(k):
        return rcopy(done_piece(k, x, 1 - y), done_piece(k, x, 1 - y), ps.at[k, 2], pr.at[k, 2], p.xnb)

    def done_core(k, part):
        piece = done_piece(k, x if part % 2 == 0 else 1 - x, y if part < 2 else 1 - y)
        src = (yi if k == 0 else xo).at[z] if part == 0 else piece
        return rcopy(src, piece, ps.at[k, 3 + part], pr.at[k, 3 + part], p.core)

    def big_own():
        for k in (0, 1):
            own_done(k).start()
            done_y(k).start()
            done_x(k).start()
            done_core(k, 0).start()

    def big_on():
        for k in (0, 1):
            done_y(k).wait()
            done_on(k).start()
            done_core(k, 2).start()

    def big_end():
        for k in (0, 1):
            done_x(k).wait()
            done_core(k, 1).start()
        for k in (0, 1):
            done_on(k).wait()
            done_core(k, 3).start()

    def mix_end():
        x_m.wait()
        add_to(xm, cm.at[rows_at(z * rz, rz)])
        y_m.start()

    def quarters(g):
        group(g, out_quarter)
        group(g, inn_quarter)

    def head_step(h, s):
        step_of(qkv_chains[h], s)

    def q_start(h):
        q_x(h).start()

    slots = {
        0: [(inn_half, 0, 0), (inn_half, 1, 0)],
        3: [(of_chunk, order[1], out_half)],
        4: [(inn_half, 0, 1), (inn_other, 0), (out_last,)],
        5: [(step_of, mix_chain, 1)],
        7: [(of_chunk, order[2], out_half)],
        8: [(inn_half, 1, 1), (inn_other, 1)],
        9: [(group, 0, out_quarter)],
        10: [(group, 0, inn_quarter), (first_big,)],
        12: [(ig_of, 0)],
        13: [(of_chunk, order[-1], out_half)],
        14: [(ig_chip, 0), (step_of, mix_chain, 2)],
        16: [(quarters, 1), (big_step, 1)],
        17: [(reloaded,), (head_weights, 0)],
        20: [(head_weights, 1)],
        21: [(head_step, 0, 1), (big_step, 2)],
        22: [(step_of, mix_chain, 3), (lambda: x_m.start(),)],
        23: [(head_step, 0, 2), (head_step, 1, 1)],
    }
    if not placed:
        slots = {}
    put_one.wait()
    for t in range(trees):
        for h in range(heads):
            key = qkv[t, :, part(h, 1)]
            keys = keys_of(t, h)
            values = qkv[t, :, part(h, 2)]
            dk[...] = jnp.zeros_like(dk)
            dv[...] = jnp.zeros_like(dv)

            def block(i, carry):
                rows = pl.ds(pl.multiple_of(i * QB, QB), QB)
                s = dot_nt(queries_of(t, rows, h), keys)
                probs = jnp.exp(s - lse[t, rows, h : h + 1])
                grad = gat[rows, t * n + h * HD : t * n + (h + 1) * HD]
                dp = dot_nt(grad, values)
                inner = jnp.sum(probs * dp, axis=1, keepdims=True)
                ds = (probs * (dp - inner)).astype(bf16)
                dv[...] += dot_tn(probs.astype(bf16), grad)
                dk[...] += dot_tn(ds, qkv[t, rows, part(h, 0)])
                slp[t, rows, part(h, 0)] = (dot_nn(ds, key) * 0.125).astype(bf16)
                run_at(slots, (t * heads + h) * per_head, i)
                return carry

            lax.fori_loop(0, full // QB, block, 0)
            slp[t, :, part(h, 1)] = (dk[...] * 0.125).astype(bf16)
            slp[t, :, part(h, 2)] = dv[...].astype(bf16)
    if not placed:

        def slow_mix(s):
            step_of(mix_chain, s)

        def slow_big(s):
            big_step(s)
            for h in range(heads):
                step_of(qkv_chains[h], s)

        of_chunk(order[1], out_half)
        of_chunk(order[2], out_half)
        out_last()
        all_steps(slow_mix)
        x_m.start()
        for g in (0, 1):
            inn_half(g, 0)
            inn_half(g, 1)
            inn_other(g)
        reloaded()
        of_chunk(order[-1], out_half)
        for g in (0, 1):
            quarters(g)
        mix_end()
        ig_of(0)
        ig_chip(0)
        first_big()
        for h in range(heads):
            head_weights(h)
        all_steps(slow_big)
        q_x(0).start()
        big_own()
        big_on()

    dbias = jnp.zeros((1, 3 * n), f32)
    for t in range(trees):
        dbias = dbias + jnp.sum(slp[t, :, : 3 * n].astype(f32), axis=0, keepdims=True)
    gap = jnp.zeros((1, width - n), f32)
    mine = [
        jnp.concatenate([dbias[:, part(h, i)] for h in range(heads)] + [gap], axis=1) for i in (0, 2)
    ]
    mine = pltpu.roll(jnp.concatenate(mine + [jnp.zeros((6, width), f32)], axis=0), q * n, 1)
    v_acc[0:8] = v_acc[0:8] + mine
    v_c = rcopy(v_acc, v_in.at[0], ks.at[2], kr.at[2], p.core)
    v_x = rcopy(v_acc, v_in.at[1], vs.at[0], vr.at[0], p.xnb)
    v_y = rcopy(v_acc, v_in.at[2], vs.at[1], vr.at[1], p.ynb)
    def vcopy(way, s, b):
        dev = p.right if way == 0 else p.left
        return rcopy(v_z.at[b], v_z.at[b], bs.at[6, way, s], br.at[6, way, s], dev)

    def v_send(s):
        for way in (0, 1):
            ok, b = spread_send(way, s, z, nz)

            @pl.when(both(ok, s <= nz - 1))
            def _():
                vcopy(way, s, b).start()

    def v_get(s):
        for way in (0, 1):
            ok, b = spread_get(way, s, z, nz)

            @pl.when(ok)
            def _():
                vcopy(way, s, b).wait_recv()

        v_send(s + 1)

    v_c.start()
    if placed:
        head_weights(2)
    v_c.wait()
    v_acc[...] = v_acc[...] + v_in[0]
    v_x.start()
    if placed:
        mix_end()
    ig_of(1)
    v_x.wait()
    v_acc[...] = v_acc[...] + v_in[1]
    v_y.start()
    if placed:
        big_step(3)
        big_own()
        for h in range(heads):
            head_step(h, 3 - h)
        q_start(0)
    ig_chip(1)
    v_y.wait()
    v_acc[...] = v_acc[...] + v_in[2]
    v_z[z] = v_acc[...]
    v_send(1)
    if placed:
        head_step(1, 3)
        head_step(2, 2)
    q_start(1)
    if placed:
        big_on()
    y_m.wait()
    o_mix[:, lanes(c * h2, h2)] = (xm[...].astype(f32) + ym[...].astype(f32)).astype(bf16)
    m_core = rcopy(
        o_mix.at[:, lanes(c * h2, h2)], o_mix.at[:, lanes(c * h2, h2)], es.at[7], er.at[7], p.core
    )
    m_core.start()
    if placed:
        head_step(2, 3)
    q_start(2)
    ig_end(0)
    q_sum(0)
    q_sum(1)
    if placed:
        v_get(1)
        v_get(2)
    q_sum(2)
    if placed:
        v_get(3)
    else:
        all_steps(v_get)
    big_end()
    ig_end(1)

    def v_sum(i, carry):
        return carry + v_z[i]

    o_vec[...] = lax.fori_loop(0, nz, v_sum, jnp.zeros(o_vec.shape, f32))
    for h in range(heads):
        q_y(h).wait()
        q_on(h).start()
    for cp in [m_core, put_y] + [q_core(h) for h in range(heads)] + [q_on(h) for h in range(heads)]:
        cp.wait()
    for k in (0, 1):
        own_done(k).wait()
        for part_ in range(4):
            done_core(k, part_).wait()
    for ch in qkv_chains + [mix_chain, inn_chain, out_chain]:
        ch[2]()

    def vdrain(s, carry):
        for way in (0, 1):
            ok, b = spread_send(way, s, z, nz)

            @pl.when(ok)
            def _():
                vcopy(way, s, b).wait_send()

        return carry

    lax.fori_loop(1, nz, vdrain, 0)


def w_heads_of(pw, width):
    return pw[...].reshape(width, pw.shape[3])


def whole(nz, tokens, teacher, seg, valid, par, wq, wk, wv, vectors, mix, inn, out):
    trees, length, width = tokens.shape
    rz, wide = mix.shape[0], inn.shape[1]
    full, count, n = 4 * length, trees * length, width // 4
    heads = n // HD
    h2, w2, w4, w8 = width // 2, wide // 2, wide // 4, wide // 8
    vmem = pl.BlockSpec(memory_space=pltpu.VMEM)
    anyspace = pl.BlockSpec(memory_space=pl.ANY)
    shape = jax.ShapeDtypeStruct
    vec = (16, width)
    most = max(nz, 4)
    parts = 2 if rz % 32 == 0 else 1
    return pl.pallas_call(
        functools.partial(whole_body, nz),
        out_shape=(
            shape((count, width), bf16),
            shape((count, width), f32),
            shape((trees * full, width), bf16),
            shape((rz, wide), bf16),
            shape((4 * rz, width), bf16),
            shape((rz, width), bf16),
            shape((heads, 4, rz, 3 * HD), bf16),
            shape((trees, length, width), bf16),
            shape(vec, f32),
        ),
        in_specs=[anyspace] * 2 + [vmem] * 2 + [pl.BlockSpec(memory_space=pltpu.SMEM)] + [anyspace] * 3 + [vmem] * 9 + [anyspace] * 3,
        out_specs=[anyspace] * 5 + [vmem] * 4,
        scratch_shapes=[
            pltpu.SMEM((trees, NSEG), jnp.int32),
            V((trees, 4, length, width), bf16),
            V((trees, full, width), bf16),
            V((width, width), bf16),
            V((nz, rz, wide), bf16),
            V((wide, width), bf16),
            V((nz, parts, rz // parts, 3 * n), bf16),
            V((trees, full, 3 * n), bf16),
            V((trees, full, 8), f32),
            V((trees, full, 4 * HD), bf16),
            V((trees, full, n), bf16),
            V((4, trees, length, n), bf16),
            V((count, width), bf16),
            V((count, width), f32),
            V((count, width), f32),
            V((count, width), f32),
            V((count, width), bf16),
            V((count, width), bf16),
            V((count, width), bf16),
            V((count, width), bf16),
            V((count, 128), f32),
            V((count, 128), f32),
            V((width, width), bf16),
            V((full, trees * n), bf16),
            V((full, trees * n), bf16),
            V((full, HD), f32),
            V((full, HD), f32),
            V((nz, rz, w2), bf16),
            V((nz, 4 * rz, h2), bf16),
            V((width, h2), bf16),
            V((2, trees, length, width), bf16),
            V((nz, rz, w4), bf16),
            V((nz, 2 * rz, h2), bf16),
            V((nz, rz, w8), bf16),
            V((nz, rz, h2), bf16),
            V((trees, length, width), bf16),
            V((2, nz, rz, w8), bf16),
            V((2, nz, rz, h2), bf16),
            V((2, nz, rz, h2), bf16),
            V((heads, 2, nz, rz, 3 * HD), bf16),
            V((heads, nz, rz, 3 * HD), bf16),
            V((rz, h2), bf16),
            V((rz, h2), bf16),
            V((heads, rz, 3 * HD), bf16),
            V((3,) + vec, f32),
            V((nz,) + vec, f32),
            V(vec, f32),
            V((nz, 16, width), bf16),
            V((4, 8, count), jnp.int32),
            V(vec, f32),
            DMA((8,)), DMA((trees, 4)), DMA((trees * 4,)),
            DMA((nz,)), DMA((nz,)),
            DMA((3 + 3 * trees,)), DMA((3 + 3 * trees,)),
            DMA((6, 2, nz)), DMA((6, 2, nz)),
            DMA((2, 3, nz)), DMA((2, 3, nz)),
            DMA((3, 4, nz)), DMA((3, 4, nz)),
            DMA((trees, 3)), DMA((trees, 3)),
            DMA((3,)), DMA((3,)),
            DMA((5,)), DMA((5,)),
            DMA((2, most)), DMA((2, most)),
            DMA((3, nz)), DMA((3, nz)),
            DMA((2, nz)), DMA((2, nz)),
            DMA((3, trees)), DMA((3, trees)),
            DMA((2, 7)), DMA((2, 7)),
            DMA((7, 2, nz)), DMA((7, 2, nz)),
            DMA((25,)), DMA((25,)),
            DMA((2,)), DMA((2,)),
        ],
        compiler_params=pltpu.CompilerParams(
            collective_id=1, has_side_effects=True, vmem_limit_bytes=VMEM_LIMIT
        ),
        name="whole",
    )(tokens, teacher, seg, valid, par, wq, wk, wv, *vectors, mix, inn, out)


def finish_body(
    slots, spot, h_inn, h_out, h_mix, h_qkv, h_ig, h_one, vec,
    o_inn, o_out, o_mix, o_q, o_k, o_v, o_ig, o_loss, o0, o1, o2, o3, o4, o5, o6, o7, o8,
    inn, out, mix, qkv, ig, one, b_inn, b_out, b_mix, b_q, b_k, b_v, b_ig, get, put,
):
    sources = ((h_inn, inn), (h_out, out), (h_one, one), (h_ig, ig), (h_qkv, qkv), (h_mix, mix))
    loads = [pltpu.make_async_copy(a, b, get.at[i]) for i, (a, b) in enumerate(sources)]
    for cp in loads:
        cp.start()
    scale = slots / vec[spot : spot + 1, 0:1]
    stores = []

    def send(buf, dst):
        cp = pltpu.make_async_copy(buf, dst, put.at[len(stores)])
        cp.start()
        stores.append(cp)

    def each(size, fn):
        step = 64 if size % 64 == 0 else size

        def part(i, carry):
            fn(pl.ds(pl.multiple_of(i * step, step), step))
            return carry

        lax.fori_loop(0, size // step, part, 0)

    def scaled(dst, src):
        def part(rows):
            dst[rows] = src[rows].astype(f32) * scale

        each(src.shape[0], part)

    shard = lax.axis_index("shard")
    count = vec[spot : spot + 1, 0:1]
    o_loss[...] = jnp.sum(vec[spot - 1 : spot], axis=1, keepdims=True) / count
    width, size = vec.shape[1], o0.shape[0]
    turned = pltpu.roll(vec[0:8], lax.rem(width - shard * size, width), 1) * scale
    for i, o in enumerate((o0, o1, o2, o3, o4, o5, o6, o7)):
        o[...] = turned[i : i + 1, :size].reshape(size)
    wide, part = (spot - 9) * width, o8.shape[0]
    row = jnp.concatenate([vec[8 + i : 9 + i] for i in range(spot - 9)], axis=1)
    row = jnp.concatenate([row, jnp.zeros((7, wide), f32)], axis=0)
    row = pltpu.roll(row, lax.rem(wide - shard * part, wide), 1) * scale
    o8[...] = row[0:1, :part].reshape(part)

    loads[0].wait()
    scaled(b_inn, inn)
    send(b_inn, o_inn)
    loads[1].wait()
    scaled(b_out, out)
    send(b_out, o_out)
    loads[2].wait()
    loads[3].wait()
    for t in range(ig.shape[0]):

        def part(rows):
            b_ig[t, rows] = (one[t, rows] + ig[t, rows].astype(f32)) * scale

        each(ig.shape[1], part)
    send(b_ig, o_ig)
    loads[4].wait()
    for i, (buf, dst) in enumerate(((b_q, o_q), (b_k, o_k), (b_v, o_v))):
        for j in range(4):
            for h in range(qkv.shape[0]):
                at = (j * qkv.shape[0] + h) * HD
                buf[:, at : at + HD] = qkv[h, j, :, i * HD : (i + 1) * HD].astype(f32) * scale
        send(buf, dst)
    loads[5].wait()
    scaled(b_mix, mix)
    send(b_mix, o_mix)
    for cp in stores:
        cp.wait()


def finish(slots, spot, inn, out, mix, qkv, ig, one, vec, sizes):
    vmem = pl.BlockSpec(memory_space=pltpu.VMEM)
    anyspace = pl.BlockSpec(memory_space=pl.ANY)
    shapes = [inn.shape, out.shape, mix.shape, mix.shape, mix.shape, mix.shape, ig.shape]
    return pl.pallas_call(
        functools.partial(finish_body, slots, spot),
        out_shape=tuple(jax.ShapeDtypeStruct(sh, f32) for sh in shapes + [(1, 1)] + [(n,) for n in sizes]),
        in_specs=[anyspace] * 6 + [vmem],
        out_specs=[anyspace] * 7 + [vmem] * 10,
        scratch_shapes=[V(a.shape, a.dtype) for a in (inn, out, mix, qkv, ig, one)]
        + [V(sh, f32) for sh in shapes]
        + [DMA((6,)), DMA((7,))],
        compiler_params=pltpu.CompilerParams(vmem_limit_bytes=VMEM_LIMIT),
        name="finish",
    )(inn, out, mix, qkv, ig, one, vec)


def per_device(
    nz,
    tokens, teacher, seg_ids, parent_seg, valid,
    query_weight, query_bias, key_weight, value_weight, value_bias,
    mix_weight, mix_bias, first_gain, first_shift,
    inner_weight, inner_bias, outer_weight, outer_bias, second_gain, second_shift,
):
    trees, local_len, width = tokens.shape
    n_seq = lax.axis_size("seq")
    row_count = trees * local_len
    total_slots = row_count * lax.axis_size("replica") * nz * n_seq
    rz = mix_weight.shape[0]
    wide = inner_weight.shape[1]

    vectors = (
        query_bias, value_bias, mix_bias, first_gain, first_shift, outer_bias, second_gain, second_shift, inner_bias
    )

    layer_out, grad_one, _, r_inn, r_out, r_mix, r_qkv, r_ig, r_vec = whole(
        nz, tokens, teacher.reshape(row_count, width), seg_ids, valid, parent_seg,
        query_weight, key_weight, value_weight, vectors, mix_weight, inner_weight, outer_weight,
    )
    layer_out = layer_out.reshape(trees, local_len, width)
    spot = 8 + wide // width
    sizes = [rz] * 8 + [inner_bias.shape[0]]
    dinner, douter, dmix, dquery, dkey, dvalue, input_grad, loss, *rows = finish(
        total_slots, spot + 1, r_inn, r_out, r_mix, r_qkv, r_ig,
        grad_one.reshape(trees, local_len, width), r_vec, sizes,
    )
    return (
        layer_out, loss[0, 0], input_grad,
        dquery, rows[0], dkey, dvalue, rows[1],
        dmix, rows[2], rows[3], rows[4],
        dinner, rows[8], douter, rows[5], rows[6], rows[7],
    )


def solution(mesh):
    rows = P(("replica", "shard"), "seq", None)
    line = P(("replica", "shard"), "seq")
    mat = P("shard", None)
    row = P("shard")
    placed = (
        rows, rows, line, P(("replica", "shard"), None), line,
        mat, row, mat, mat, row, mat, row, row, row, mat, row, mat, row, row, row,
    )
    return jax.shard_map(
        functools.partial(per_device, mesh.shape["shard"]),
        mesh=mesh,
        in_specs=placed,
        out_specs=(
            rows, P(), rows,
            mat, row, mat, mat, row, mat, row, row, row, mat, row, mat, row, row, row,
        ),
        check_vma=False,
    )
```
